128 devices in a mesh: fsdp: 8 (over x, core), tensor: 2 (over y_lo), context: 8 (over z, y_hi).
Axes of the slice: x: 4, y: 4 (y_hi: 2, y_lo: 2; y = y_hi * 2 + y_lo), z: 4, core: 2. Of those that a mesh axis runs over, the one named last changes fastest.
Arguments:
- block_input: bfloat16 [16384, 768], P(('fsdp', 'context')), may hold values from -6 to 6
- seq_lengths: int32 [8, 3], P('fsdp'), may hold values from 1 to 1536, 2048 in all within a row
- attn_gain: bfloat16 [768], P('fsdp'), may hold values from 0.5 to 1.5
- qkv_weight: bfloat16 [768, 3, 768], P('fsdp', None, 'tensor'), may hold values from -0.3969283 to 0.3969283
- proj_weight: bfloat16 [768, 768], P('tensor', 'fsdp'), may hold values from -4 to 4
- mlp_gain: bfloat16 [768], P('fsdp'), may hold values from 0.5 to 1.5
- gelu_weight: bfloat16 [768, 2, 1152], P('fsdp', None, 'tensor'), may hold values from -0.21875 to 0.21875
- down_weight: bfloat16 [1152, 768], P('tensor', 'fsdp'), may hold values from -0.1875 to 0.1875
- out_cotangent: bfloat16 [16384, 768], P(('fsdp', 'context')), may hold values from -6 to 6
Outputs:
- block_output: bfloat16 [16384, 768], P(('fsdp', 'context'))
- input_grad: float32 [16384, 768], P(('fsdp', 'context'))
- attngain_grad: float32 [768], P('fsdp')
- qkv_grad: float32 [768, 3, 768], P('fsdp', None, 'tensor')
- proj_grad: float32 [768, 768], P('tensor', 'fsdp')
- mlpgain_grad: float32 [768], P('fsdp')
- gelu_grad: float32 [768, 2, 1152], P('fsdp', None, 'tensor')
- down_grad: float32 [1152, 768], P('tensor', 'fsdp')
The draws below stay inside these ranges and needn't reach their ends.
All inputs are finite; a program needn't handle non-finite values.
Results may differ from the reference program's by a relative error of at most 0.02.
Values may be sent and summed in bfloat16 or wider, within the bound.
A program may use at most 128 MiB of HBM per device.

```python
import math
import jax
import jax.numpy as jnp
import numpy as np
from jax import lax

D = 768
HEADS = 12
HD = 64
FF = 1152
NSEQ = 3
GROUP_TOK = 2048
TOKENS = 16384
N_FSDP = 8


def draw_qkv_weight(key, part):
    column_count = HEADS * HD
    entries = jnp.clip(jax.random.normal(key, (D, 3, column_count), jnp.float32), -5.0, 5.0) / math.sqrt(D)
    return entries.astype(jnp.bfloat16)


def shard_levels(own_key, shape, split, least, high):
    def one(axis_at, parts):
        heights = jax.random.uniform(jax.random.fold_in(jax.random.fold_in(own_key, 6), axis_at), (parts,), jnp.float32, least / len(split), high / len(split))
        return jnp.repeat(jnp.exp(heights), shape[axis_at] // parts).reshape((-1,) + (1,) * (len(shape) - axis_at - 1))

    loudness = one(*split[0])
    for cut in split[1:]:
        loudness = loudness * one(*cut)
    return loudness


def split_up(amount, total, limit, slope):
    loads = [(1 << 20) // math.isqrt(standing ** slope) + 1 for standing in range(2, amount + 1)]
    rest, given = total - limit - (amount - 1), [1] * (amount - 1)
    while rest > 0:
        candidates = [i for i in range(amount - 1) if given[i] < limit]
        pool, budget = sum([loads[i] for i in candidates]), rest
        for i in candidates:
            more = min(limit - given[i], max(1, budget * loads[i] // pool), rest)
            given[i] = given[i] + more
            rest = rest - more
    return np.array([limit] + given)


def ragged(own_key, amount, total, reach, skew):
    if amount == 2:
        one = jax.random.randint(own_key, (), max(1, total - reach), min(reach, total - 1) + 1)
        return jnp.stack([one, total - one])
    sizes = jnp.asarray(split_up(amount, total, reach, skew), jnp.int32)
    twos = (amount - 1) // 2
    source_of, receiver = sizes[1:1 + 2 * twos:2], sizes[2:2 + 2 * twos:2]
    margin = jnp.minimum(source_of - 1, reach - receiver)
    shifted = jax.random.randint(jax.random.fold_in(own_key, 1), (twos,), 0, 1 << 20) % (margin + 1)
    sizes = sizes.at[1:1 + 2 * twos:2].set(source_of - shifted).at[2:2 + 2 * twos:2].set(receiver + shifted)
    return sizes[jax.random.permutation(jax.random.fold_in(own_key, 2), amount)]


def bell_draw(own_key, dims, deviation, limit, cuts=(), held_as=jnp.bfloat16):
    array = deviation * jax.random.normal(own_key, dims, jnp.float32)
    if cuts:
        array = array * shard_levels(own_key, dims, cuts, -0.22, 0.18)
    return jnp.clip(array, -limit, limit).astype(held_as)


def setup_inputs(seed: int = 0) -> dict:
    streams_of = jax.random.split(jax.random.key(seed), 10)
    block_input = bell_draw(streams_of[0], (TOKENS, D), 1.0, 6.0, ((0, 64),))
    seq_lengths = jax.vmap(lambda own: ragged(own, NSEQ, GROUP_TOK, GROUP_TOK * 3 // 4, 2))(jax.random.split(streams_of[1], N_FSDP)).reshape((N_FSDP, NSEQ)).astype(jnp.int32)
    attn_gain = jnp.clip(1.0 + 0.1 * jax.random.normal(streams_of[2], (D,), jnp.float32), 0.5, 1.5).astype(jnp.bfloat16)
    qkv_weight = draw_qkv_weight(jax.random.fold_in(streams_of[9], 71), 0)
    proj_weight = bell_draw(streams_of[4], (HEADS * HD, D), 2 ** -0.5, 4.0, ((0, 2), (1, 8)))
    mlp_gain = jnp.clip(1.0 + 0.1 * jax.random.normal(streams_of[5], (D,), jnp.float32), 0.5, 1.5).astype(jnp.bfloat16)
    gelu_weight = bell_draw(streams_of[6], (D, 2, FF), D ** -0.5, 0.21875, ((0, 8), (2, 2)))
    down_weight = bell_draw(streams_of[7], (FF, D), FF ** -0.5, 0.1875, ((0, 2), (1, 8)))
    out_cotangent = bell_draw(streams_of[8], (TOKENS, D), 1.0, 6.0, ((0, 64),))
    return {"block_input": block_input, "seq_lengths": seq_lengths, "attn_gain": attn_gain, "qkv_weight": qkv_weight, "proj_weight": proj_weight, "mlp_gain": mlp_gain, "gelu_weight": gelu_weight, "down_weight": down_weight, "out_cotangent": out_cotangent}


EPSILON = 1e-05
THETA = 160000.0
MASKED_LOW = -1e+30

def stored(values):
    return lax.optimization_barrier(values.astype(jnp.bfloat16))

def layer_norm(values):
    centre = values - lax.optimization_barrier(jnp.mean(values, axis=-1, keepdims=True))
    spread = lax.rsqrt(lax.optimization_barrier(jnp.mean(centre * centre, axis=-1, keepdims=True)) + EPSILON)
    return (centre * spread, spread)

def norm_back(grad_out, normed, spread, gain):
    scaled = grad_out * gain
    inner = lax.optimization_barrier(jnp.mean(scaled, axis=-1, keepdims=True)) + normed * lax.optimization_barrier(jnp.mean(scaled * normed, axis=-1, keepdims=True))
    return spread * (scaled - inner)

def segments_of(row_ids, lengths):
    ends = jnp.cumsum(lengths).astype(jnp.int32)
    segment = lax.optimization_barrier(jnp.sum((row_ids[:, None] >= ends[None, :]).astype(jnp.int32), axis=1)).astype(jnp.int32)
    starts = ends - lengths
    picked = segment[:, None] == jnp.arange(lengths.shape[0], dtype=jnp.int32)[None, :]
    begin = lax.optimization_barrier(jnp.sum(jnp.where(picked, starts[None, :], 0), axis=1)).astype(jnp.int32)
    return (segment, row_ids - begin)

def rope_tables(positions, head_dim):
    half_dim = head_dim // 2
    exponent = jnp.arange(half_dim, dtype=jnp.float32) * (-2.0 / head_dim)
    frequency = jnp.power(jnp.float32(THETA), exponent)
    angles = positions.astype(jnp.float32)[:, None] * frequency[None, :]
    return (jnp.cos(angles)[:, None, :], jnp.sin(angles)[:, None, :])

def rotate(values, cosine, sine_tab):
    half_dim = values.shape[-1] // 2
    lower_half, upper_half = (values[..., :half_dim], values[..., half_dim:])
    return jnp.concatenate([lower_half * cosine - upper_half * sine_tab, upper_half * cosine + lower_half * sine_tab], axis=-1)

def rotate_back(grads, cosine, sine_tab):
    half_dim = grads.shape[-1] // 2
    lower_half, upper_half = (grads[..., :half_dim], grads[..., half_dim:])
    return jnp.concatenate([lower_half * cosine + upper_half * sine_tab, upper_half * cosine - lower_half * sine_tab], axis=-1)

def gelu_parts(gate_pre):
    normal_cdf = 0.5 * (1.0 + jax.scipy.special.erf(gate_pre * 0.7071067811865476))
    density = jnp.exp(-0.5 * gate_pre * gate_pre) * 0.3989422804014327
    return (gate_pre * normal_cdf, normal_cdf + gate_pre * density)

def attend_block(items, key_bf, value_bf, key_segment):
    query_blk, query_segment = items
    scores = jnp.einsum('qhd,khd->hqk', query_blk.astype(jnp.float32), key_bf.astype(jnp.float32)) * 0.125
    same_doc = (query_segment[:, None] == key_segment[None, :])[None]
    row_max = lax.optimization_barrier(jnp.max(jnp.where(same_doc, scores, MASKED_LOW), axis=2))
    denom_sum = lax.optimization_barrier(jnp.sum(jnp.where(same_doc, jnp.exp(scores - row_max[:, :, None]), 0.0), axis=2))
    log_total = row_max + jnp.log(denom_sum)
    weights = stored(jnp.where(same_doc, jnp.exp(scores - log_total[:, :, None]), 0.0))
    mixed = jnp.einsum('hqk,khd->qhd', weights.astype(jnp.float32), value_bf.astype(jnp.float32))
    return (stored(mixed), log_total)

def group_pass(rows_in, lengths, cotangent, gains, matrices):
    attn_gain, mlp_gain = gains
    qkv_weight, proj_weight, gelu_weight, down_weight = matrices
    qkv_width = HEADS * HD
    row_ids = jnp.arange(GROUP_TOK, dtype=jnp.int32)
    segment, positions = segments_of(row_ids, lengths)
    cosine, sine_tab = rope_tables(positions, HD)
    attn_scale = attn_gain.astype(jnp.float32)
    mlp_scale = mlp_gain.astype(jnp.float32)
    inputs = rows_in.astype(jnp.float32)
    normed_attn, spread_attn = layer_norm(inputs)
    hidden_attn = stored(normed_attn * attn_scale)
    qkv_flat = qkv_weight.reshape(D, 3 * qkv_width)
    projected = jnp.dot(hidden_attn, qkv_flat, preferred_element_type=jnp.float32).reshape(GROUP_TOK, 3, HEADS, HD)
    query_bf = stored(rotate(projected[:, 0], cosine, sine_tab))
    key_bf = stored(rotate(projected[:, 1], cosine, sine_tab))
    value_bf = stored(projected[:, 2])
    query_block = 512 if GROUP_TOK % 512 == 0 else GROUP_TOK
    block_count = GROUP_TOK // query_block
    query_blocks = query_bf.reshape(block_count, query_block, HEADS, HD)
    segment_blocks = segment.reshape(block_count, query_block)
    mixed, log_total = lax.map(lambda items: attend_block(items, key_bf, value_bf, segment), (query_blocks, segment_blocks))
    mixed_heads = mixed.reshape(GROUP_TOK, HEADS, HD)
    attn_out = mixed.reshape(GROUP_TOK, qkv_width)
    residual = inputs + jnp.dot(attn_out, proj_weight, preferred_element_type=jnp.float32)
    normed_mlp, spread_mlp = layer_norm(residual)
    hidden_mlp = stored(normed_mlp * mlp_scale)
    gelu_flat = gelu_weight.reshape(D, 2 * FF)
    gate_up = jnp.dot(hidden_mlp, gelu_flat, preferred_element_type=jnp.float32).reshape(GROUP_TOK, 2, FF)
    gate_pre, up_pre = (gate_up[:, 0], gate_up[:, 1])
    gelu_val, gelu_slope = gelu_parts(gate_pre)
    activ = stored(gelu_val * up_pre)
    output = (residual + jnp.dot(activ, down_weight, preferred_element_type=jnp.float32)).astype(jnp.bfloat16)
    act_grad = jnp.dot(cotangent, down_weight.T, preferred_element_type=jnp.float32)
    down_grad = jnp.dot(activ.T, cotangent, preferred_element_type=jnp.float32)
    gate_up_grad = stored(jnp.stack([act_grad * up_pre * gelu_slope, act_grad * gelu_val], axis=1)).reshape(GROUP_TOK, 2 * FF)
    gelu_grad = jnp.dot(hidden_mlp.T, gate_up_grad, preferred_element_type=jnp.float32).reshape(D, 2, FF)
    mlp_in_grad = jnp.dot(gate_up_grad, gelu_flat.T, preferred_element_type=jnp.float32)
    mlpgain_grad = lax.optimization_barrier(jnp.sum(mlp_in_grad * normed_mlp, axis=0))
    resid_grad = cotangent.astype(jnp.float32) + norm_back(mlp_in_grad, normed_mlp, spread_mlp, mlp_scale)
    resid_bf = stored(resid_grad)
    out_grad = stored(jnp.dot(resid_bf, proj_weight.T, preferred_element_type=jnp.float32))
    proj_grad = jnp.dot(attn_out.T, resid_bf, preferred_element_type=jnp.float32)
    out_heads = out_grad.reshape(GROUP_TOK, HEADS, HD)
    delta = lax.optimization_barrier(jnp.sum(out_heads.astype(jnp.float32) * mixed_heads.astype(jnp.float32), axis=2))
    delta_blocks = jnp.transpose(delta.reshape(block_count, query_block, HEADS), (0, 2, 1))

    def back_block(running, items):
        key_acc, value_acc = running
        query_blk, query_segment, total_blk, grad_blk, delta_blk = items
        scores = jnp.einsum('qhd,khd->hqk', query_blk.astype(jnp.float32), key_bf.astype(jnp.float32)) * 0.125
        same_doc = (query_segment[:, None] == segment[None, :])[None]
        weights = jnp.where(same_doc, jnp.exp(scores - total_blk[:, :, None]), 0.0)
        prob_grad = jnp.einsum('qhd,khd->hqk', grad_blk.astype(jnp.float32), value_bf.astype(jnp.float32))
        score_grad = stored(weights * (prob_grad - delta_blk[:, :, None])).astype(jnp.float32)
        weight_bf = stored(weights).astype(jnp.float32)
        query_grad = jnp.einsum('hqk,khd->qhd', score_grad, key_bf.astype(jnp.float32)) * 0.125
        key_acc = key_acc + jnp.einsum('hqk,qhd->khd', score_grad, query_blk.astype(jnp.float32)) * 0.125
        value_acc = value_acc + jnp.einsum('hqk,qhd->khd', weight_bf, grad_blk.astype(jnp.float32))
        return ((key_acc, value_acc), query_grad)
    zeros_kv = jnp.zeros((GROUP_TOK, HEADS, HD), jnp.float32)
    grad_blocks = out_heads.reshape(block_count, query_block, HEADS, HD)
    (key_grad, value_grad), query_grads = lax.scan(back_block, (zeros_kv, zeros_kv), (query_blocks, segment_blocks, log_total, grad_blocks, delta_blocks))
    query_grad = query_grads.reshape(GROUP_TOK, HEADS, HD)
    qkv_rows = stored(jnp.stack([rotate_back(query_grad, cosine, sine_tab), rotate_back(key_grad, cosine, sine_tab), value_grad], axis=1)).reshape(GROUP_TOK, 3 * qkv_width)
    qkv_grad = jnp.dot(hidden_attn.T, qkv_rows, preferred_element_type=jnp.float32).reshape(D, 3, qkv_width)
    attn_in_grad = jnp.dot(qkv_rows, qkv_flat.T, preferred_element_type=jnp.float32)
    attngain_grad = lax.optimization_barrier(jnp.sum(attn_in_grad * normed_attn, axis=0))
    input_grad = resid_grad + norm_back(attn_in_grad, normed_attn, spread_attn, attn_scale)
    return (output, input_grad, (attngain_grad, qkv_grad, proj_grad, mlpgain_grad, gelu_grad, down_grad))

def reference(block_input, seq_lengths, attn_gain, qkv_weight, proj_weight, mlp_gain, gelu_weight, down_weight, out_cotangent):
    inputs = block_input.reshape(N_FSDP, GROUP_TOK, D)
    cotangents = out_cotangent.reshape(N_FSDP, GROUP_TOK, D)
    start_sums = (jnp.zeros((D,), jnp.float32), jnp.zeros((D, 3, HEADS * HD), jnp.float32), jnp.zeros((HEADS * HD, D), jnp.float32), jnp.zeros((D,), jnp.float32), jnp.zeros((D, 2, FF), jnp.float32), jnp.zeros((FF, D), jnp.float32))

    def one_group(running, items):
        rows_in, lengths, cotangent = items
        output, input_grad, grads = group_pass(rows_in, lengths, cotangent, (attn_gain, mlp_gain), (qkv_weight, proj_weight, gelu_weight, down_weight))
        return (jax.tree.map(lambda left_sum, right_sum: left_sum + right_sum, running, grads), (output, input_grad))
    totals, (outputs, input_grads) = lax.scan(one_group, start_sums, (inputs, seq_lengths, cotangents))
    return (outputs.reshape(TOKENS, D), input_grads.reshape(TOKENS, D), totals[0], totals[1], totals[2], totals[3], totals[4], totals[5])
```

```python
import jax
import jax.numpy as jnp
from jax import lax
from jax.sharding import PartitionSpec as P

HD = 64


EPSILON = 1e-05
THETA = 160000.0
MASKED_LOW = -1e30


def layer_norm(values):
    centre = values - jnp.mean(values, axis=-1, keepdims=True)
    spread = lax.rsqrt(jnp.mean(centre * centre, axis=-1, keepdims=True) + EPSILON)
    return (centre * spread, spread)


def norm_back(grad_out, normed, spread, gain):
    scaled = grad_out * gain
    inner = jnp.mean(scaled, axis=-1, keepdims=True) + normed * jnp.mean(
        scaled * normed, axis=-1, keepdims=True
    )
    return spread * (scaled - inner)


def segments_of(row_ids, lengths):
    ends = jnp.cumsum(lengths)
    segment = jnp.sum((row_ids[:, None] >= ends[None, :]).astype(jnp.int32), axis=1)
    starts = ends - lengths
    picked = segment[:, None] == jnp.arange(lengths.shape[0], dtype=jnp.int32)[None, :]
    begin = jnp.sum(jnp.where(picked, starts[None, :], 0), axis=1)
    return (segment, row_ids - begin)


def rope_tables(positions, head_dim):
    half_dim = head_dim // 2
    exponent = jnp.arange(half_dim, dtype=jnp.float32) * (-2.0 / head_dim)
    frequency = jnp.power(jnp.float32(THETA), exponent)
    angles = positions.astype(jnp.float32)[:, None] * frequency[None, :]
    return (jnp.cos(angles)[:, None, :], jnp.sin(angles)[:, None, :])


def rotate(values, cosine, sine_tab):
    half_dim = values.shape[-1] // 2
    lower_half, upper_half = (values[..., :half_dim], values[..., half_dim:])
    return jnp.concatenate(
        [lower_half * cosine - upper_half * sine_tab, upper_half * cosine + lower_half * sine_tab],
        axis=-1,
    )


def rotate_back(grads, cosine, sine_tab):
    half_dim = grads.shape[-1] // 2
    lower_half, upper_half = (grads[..., :half_dim], grads[..., half_dim:])
    return jnp.concatenate(
        [lower_half * cosine + upper_half * sine_tab, upper_half * cosine - lower_half * sine_tab],
        axis=-1,
    )


def gelu_parts(gate_pre):
    normal_cdf = 0.5 * (1.0 + jax.scipy.special.erf(gate_pre * 0.7071067811865476))
    density = jnp.exp(-0.5 * gate_pre * gate_pre) * 0.3989422804014327
    return (gate_pre * normal_cdf, normal_cdf + gate_pre * density)


def split_count(row_count):
    pieces = 1
    while row_count // pieces > 1024 and row_count % (2 * pieces) == 0:
        pieces = pieces * 2
    return pieces


def over_blocks(step, running, members):
    row_count = members[0].shape[0]
    pieces = split_count(row_count)
    stride = row_count // pieces

    def one_block(counter, current):
        offset = counter * stride
        sliced = tuple((lax.dynamic_slice_in_dim(member, offset, stride, 0) for member in members))
        return step(current, sliced, offset)

    return lax.fori_loop(0, pieces, one_block, running)


def guarded(step):

    def wrapped(running, members, first_row):
        return step(running, members, first_row)

    def folded(running, members, first_row):
        return over_blocks(wrapped, running, members)

    return folded


def on_device(
    block_input,
    seq_lengths,
    attn_gain,
    qkv_weight,
    proj_weight,
    mlp_gain,
    gelu_weight,
    down_weight,
    out_cotangent,
):
    row_count = block_input.shape[0]
    feature_count = block_input.shape[1]
    lengths = seq_lengths[0]
    group_rows = row_count * lax.axis_size("context")
    own_first = lax.axis_index("context") * row_count
    own_rows = own_first + jnp.arange(row_count, dtype=jnp.int32)
    own_segment, positions = segments_of(own_rows, lengths)
    cosine, sine_tab = rope_tables(positions, HD)
    gathered = (
        lax.all_gather(qkv_weight, "fsdp", axis=0, tiled=True),
        lax.all_gather(proj_weight, "fsdp", axis=1, tiled=True),
        lax.all_gather(gelu_weight, "fsdp", axis=0, tiled=True),
        lax.all_gather(down_weight, "fsdp", axis=1, tiled=True),
        lax.all_gather(attn_gain, "fsdp", axis=0, tiled=True),
        lax.all_gather(mlp_gain, "fsdp", axis=0, tiled=True),
    )
    qkv_full, proj_full, gelu_full, down_full, attn_full, mlp_full = gathered
    local_width = qkv_full.shape[2]
    head_count = local_width // HD
    hidden = gelu_full.shape[2]
    attn_scale = attn_full.astype(jnp.float32)
    mlp_scale = mlp_full.astype(jnp.float32)
    inputs = block_input.astype(jnp.float32)
    normed_attn, spread_attn = layer_norm(inputs)
    hidden_attn = (normed_attn * attn_scale).astype(jnp.bfloat16)
    qkv_flat = qkv_full.reshape(feature_count, 3 * local_width)
    projected = jnp.dot(hidden_attn, qkv_flat, preferred_element_type=jnp.float32).reshape(
        row_count, 3, head_count, HD
    )
    query_bf = rotate(projected[:, 0], cosine, sine_tab).astype(jnp.bfloat16)
    key_bf = rotate(projected[:, 1], cosine, sine_tab).astype(jnp.bfloat16)
    value_bf = projected[:, 2].astype(jnp.bfloat16)
    key_flat = key_bf.reshape(row_count, local_width)
    value_flat = value_bf.reshape(row_count, local_width)
    keys_group, values_group = (
        lax.all_gather(key_flat, "context", axis=0, tiled=True),
        lax.all_gather(value_flat, "context", axis=0, tiled=True),
    )
    keys_heads = keys_group.reshape(group_rows, head_count, HD)
    values_heads = values_group.reshape(group_rows, head_count, HD)
    group_segment, unused_pos = segments_of(jnp.arange(group_rows, dtype=jnp.int32), lengths)
    same_group = (own_segment[:, None] == group_segment[None, :])[None]
    fwd_scores = (
        jnp.einsum("qhd,khd->hqk", query_bf, keys_heads, preferred_element_type=jnp.float32) * 0.125
    )
    row_max = jnp.max(jnp.where(same_group, fwd_scores, MASKED_LOW), axis=2)
    denom_sum = jnp.sum(
        jnp.where(same_group, jnp.exp(fwd_scores - row_max[:, :, None]), 0.0), axis=2
    )
    log_total = row_max + jnp.log(denom_sum)
    fwd_weights = jnp.where(same_group, jnp.exp(fwd_scores - log_total[:, :, None]), 0.0).astype(
        jnp.bfloat16
    )
    mixed = jnp.einsum(
        "hqk,khd->qhd", fwd_weights, values_heads, preferred_element_type=jnp.float32
    ).astype(jnp.bfloat16)
    mixed_flat = mixed.reshape(row_count, local_width)
    attn_part = jnp.dot(mixed_flat, proj_full, preferred_element_type=jnp.float32)
    residual = inputs + lax.psum(attn_part, "tensor")
    normed_mlp, spread_mlp = layer_norm(residual)
    hidden_mlp = (normed_mlp * mlp_scale).astype(jnp.bfloat16)
    gelu_flat = gelu_full.reshape(feature_count, 2 * hidden)
    gate_up = jnp.dot(hidden_mlp, gelu_flat, preferred_element_type=jnp.float32).reshape(
        row_count, 2, hidden
    )
    gate_pre, up_pre = (gate_up[:, 0], gate_up[:, 1])
    gelu_val, gelu_slope = gelu_parts(gate_pre)
    activ = (gelu_val * up_pre).astype(jnp.bfloat16)
    mlp_part = jnp.dot(activ, down_full, preferred_element_type=jnp.float32)
    block_output = (
        residual + lax.psum(mlp_part.astype(jnp.bfloat16), "tensor").astype(jnp.float32)
    ).astype(jnp.bfloat16)
    act_grad = jnp.dot(out_cotangent, down_full.T, preferred_element_type=jnp.float32)
    down_grad_t = jnp.dot(out_cotangent.T, activ, preferred_element_type=jnp.float32)
    gate_up_grad = (
        jnp.stack([act_grad * up_pre * gelu_slope, act_grad * gelu_val], axis=1)
        .astype(jnp.bfloat16)
        .reshape(row_count, 2 * hidden)
    )
    gelu_grad = jnp.dot(hidden_mlp.T, gate_up_grad, preferred_element_type=jnp.float32).reshape(
        feature_count, 2, hidden
    )
    mlp_in_grad = lax.psum(
        jnp.dot(gate_up_grad, gelu_flat.T, preferred_element_type=jnp.float32), "tensor"
    )
    mlpgain_grad = jnp.sum(mlp_in_grad * normed_mlp, axis=0)
    resid_grad = out_cotangent.astype(jnp.float32) + norm_back(
        mlp_in_grad, normed_mlp, spread_mlp, mlp_scale
    )
    resid_bf = resid_grad.astype(jnp.bfloat16)
    out_grad = jnp.dot(resid_bf, proj_full.T, preferred_element_type=jnp.float32).astype(
        jnp.bfloat16
    )
    proj_grad_t = jnp.dot(resid_bf.T, mixed_flat, preferred_element_type=jnp.float32)
    out_heads = out_grad.reshape(row_count, head_count, HD)
    delta = jnp.transpose(
        jnp.sum(out_heads.astype(jnp.float32) * mixed.astype(jnp.float32), axis=2)
    )

    def key_terms(members, first_row):
        key_count = members[0].shape[0]
        key_part = members[0].reshape(key_count, head_count, HD)
        value_part = members[1].reshape(key_count, head_count, HD)
        key_segment, unused = segments_of(
            first_row + jnp.arange(key_count, dtype=jnp.int32), lengths
        )
        same_doc = (own_segment[:, None] == key_segment[None, :])[None]
        scores = (
            jnp.einsum("qhd,khd->hqk", query_bf, key_part, preferred_element_type=jnp.float32)
            * 0.125
        )
        weights = jnp.where(same_doc, jnp.exp(scores - log_total[:, :, None]), 0.0)
        prob_grad = jnp.einsum(
            "qhd,khd->hqk", out_heads, value_part, preferred_element_type=jnp.float32
        )
        score_grad = (weights * (prob_grad - delta[:, :, None])).astype(jnp.bfloat16)
        return (key_part, weights, score_grad)

    def owner_step(running, members, first_row):
        query_grad, key_all, value_all = running
        key_part, weights, score_grad = key_terms(members, first_row)
        key_count = key_part.shape[0]
        query_grad = (
            query_grad
            + jnp.einsum("hqk,khd->qhd", score_grad, key_part, preferred_element_type=jnp.float32)
            * 0.125
        )
        key_piece = (
            jnp.einsum(
                "hqk,qhd->khd", score_grad, query_bf, preferred_element_type=jnp.float32
            ).reshape(key_count, local_width)
            * 0.125
        )
        value_piece = jnp.einsum(
            "hqk,qhd->khd",
            weights.astype(jnp.bfloat16),
            out_heads,
            preferred_element_type=jnp.float32,
        ).reshape(key_count, local_width)
        key_all = lax.dynamic_update_slice_in_dim(
            key_all,
            lax.dynamic_slice_in_dim(key_all, first_row, key_count, 0) + key_piece,
            first_row,
            0,
        )
        value_all = lax.dynamic_update_slice_in_dim(
            value_all,
            lax.dynamic_slice_in_dim(value_all, first_row, key_count, 0) + value_piece,
            first_row,
            0,
        )
        return (query_grad, key_all, value_all)

    grad_start = jnp.zeros((row_count, head_count, HD), jnp.float32)
    back_state = (
        grad_start,
        jnp.zeros((group_rows, local_width), jnp.float32),
        jnp.zeros((group_rows, local_width), jnp.float32),
    )
    back_result = guarded(owner_step)(
        back_state,
        (
            lax.all_gather(key_flat, "context", axis=0, tiled=True),
            lax.all_gather(value_flat, "context", axis=0, tiled=True),
        ),
        jnp.int32(0),
    )
    query_grad = back_result[0]
    key_grad, value_grad = (
        lax.psum_scatter(
            back_result[1].astype(jnp.bfloat16), "context", scatter_dimension=0, tiled=True
        ).astype(jnp.float32),
        lax.psum_scatter(
            back_result[2].astype(jnp.bfloat16), "context", scatter_dimension=0, tiled=True
        ).astype(jnp.float32),
    )
    key_grad = key_grad.reshape(row_count, head_count, HD)
    value_grad = value_grad.reshape(row_count, head_count, HD)
    qkv_rows = (
        jnp.stack(
            [
                rotate_back(query_grad, cosine, sine_tab),
                rotate_back(key_grad, cosine, sine_tab),
                value_grad,
            ],
            axis=1,
        )
        .astype(jnp.bfloat16)
        .reshape(row_count, 3 * local_width)
    )
    qkv_grad = jnp.dot(hidden_attn.T, qkv_rows, preferred_element_type=jnp.float32).reshape(
        feature_count, 3, local_width
    )
    attn_in_grad = lax.psum(
        jnp.dot(qkv_rows, qkv_flat.T, preferred_element_type=jnp.float32).astype(jnp.bfloat16),
        "tensor",
    ).astype(jnp.float32)
    attngain_grad = jnp.sum(attn_in_grad * normed_attn, axis=0)
    input_grad = resid_grad + norm_back(attn_in_grad, normed_attn, spread_attn, attn_scale)
    grads = (
        attngain_grad[:, None],
        mlpgain_grad[:, None],
        qkv_grad.reshape(feature_count, 3 * local_width),
        gelu_grad.reshape(feature_count, 2 * hidden),
        proj_grad_t,
        down_grad_t,
    )
    widths = [g.shape[1] for g in grads]
    packed = jnp.concatenate(grads, axis=1)
    packed = lax.psum_scatter(packed, "fsdp", scatter_dimension=0, tiled=True)
    packed = lax.psum(packed, "context")
    pieces = []
    start = 0
    for width in widths:
        pieces.append(packed[:, start : start + width])
        start += width
    shard_rows = packed.shape[0]
    shares = (
        pieces[0][:, 0],
        pieces[2].reshape(shard_rows, 3, local_width),
        pieces[4].T,
        pieces[1][:, 0],
        pieces[3].reshape(shard_rows, 2, hidden),
        pieces[5].T,
    )
    return (
        block_output,
        input_grad,
        shares[0],
        shares[1],
        shares[2],
        shares[3],
        shares[4],
        shares[5],
    )


def solution(mesh):
    in_specs = (
        P(("fsdp", "context"), None),
        P("fsdp", None),
        P("fsdp"),
        P("fsdp", None, "tensor"),
        P("tensor", "fsdp"),
        P("fsdp"),
        P("fsdp", None, "tensor"),
        P("tensor", "fsdp"),
        P(("fsdp", "context"), None),
    )
    out_specs = (
        P(("fsdp", "context"), None),
        P(("fsdp", "context"), None),
        P("fsdp"),
        P("fsdp", None, "tensor"),
        P("tensor", "fsdp"),
        P("fsdp"),
        P("fsdp", None, "tensor"),
        P("tensor", "fsdp"),
    )
    return jax.shard_map(
        on_device, mesh=mesh, in_specs=in_specs, out_specs=out_specs, check_vma=False
    )
```

```python
import jax
import jax.numpy as jnp
from jax import lax
from jax.sharding import PartitionSpec as P

HD = 64


EPSILON = 1e-05
THETA = 160000.0
MASKED_LOW = -1e30


def layer_norm(values):
    centre = values - jnp.mean(values, axis=-1, keepdims=True)
    spread = lax.rsqrt(jnp.mean(centre * centre, axis=-1, keepdims=True) + EPSILON)
    return (centre * spread, spread)


def norm_back(grad_out, normed, spread, gain):
    scaled = grad_out * gain
    inner = jnp.mean(scaled, axis=-1, keepdims=True) + normed * jnp.mean(
        scaled * normed, axis=-1, keepdims=True
    )
    return spread * (scaled - inner)


def segments_of(row_ids, lengths):
    ends = jnp.cumsum(lengths)
    segment = jnp.sum((row_ids[:, None] >= ends[None, :]).astype(jnp.int32), axis=1)
    starts = ends - lengths
    picked = segment[:, None] == jnp.arange(lengths.shape[0], dtype=jnp.int32)[None, :]
    begin = jnp.sum(jnp.where(picked, starts[None, :], 0), axis=1)
    return (segment, row_ids - begin)


def rope_tables(positions, head_dim):
    half_dim = head_dim // 2
    exponent = jnp.arange(half_dim, dtype=jnp.float32) * (-2.0 / head_dim)
    frequency = jnp.power(jnp.float32(THETA), exponent)
    angles = positions.astype(jnp.float32)[:, None] * frequency[None, :]
    return (jnp.cos(angles)[:, None, :], jnp.sin(angles)[:, None, :])


def rotate(values, cosine, sine_tab):
    half_dim = values.shape[-1] // 2
    lower_half, upper_half = (values[..., :half_dim], values[..., half_dim:])
    return jnp.concatenate(
        [lower_half * cosine - upper_half * sine_tab, upper_half * cosine + lower_half * sine_tab],
        axis=-1,
    )


def rotate_back(grads, cosine, sine_tab):
    half_dim = grads.shape[-1] // 2
    lower_half, upper_half = (grads[..., :half_dim], grads[..., half_dim:])
    return jnp.concatenate(
        [lower_half * cosine + upper_half * sine_tab, upper_half * cosine - lower_half * sine_tab],
        axis=-1,
    )


def gelu_parts(gate_pre):
    normal_cdf = 0.5 * (1.0 + jax.scipy.special.erf(gate_pre * 0.7071067811865476))
    density = jnp.exp(-0.5 * gate_pre * gate_pre) * 0.3989422804014327
    return (gate_pre * normal_cdf, normal_cdf + gate_pre * density)


def pair_sum(values, axis_name):
    if lax.axis_size(axis_name) != 2:
        return lax.psum(values, axis_name)
    other = lax.ppermute(values, axis_name, perm=[(0, 1), (1, 0)])
    return values.astype(jnp.float32) + other.astype(jnp.float32)


def split_count(row_count):
    pieces = 1
    while row_count // pieces > 1024 and row_count % (2 * pieces) == 0:
        pieces = pieces * 2
    return pieces


def over_blocks(step, running, members):
    row_count = members[0].shape[0]
    pieces = split_count(row_count)
    stride = row_count // pieces

    def one_block(counter, current):
        offset = counter * stride
        sliced = tuple((lax.dynamic_slice_in_dim(member, offset, stride, 0) for member in members))
        return step(current, sliced, offset)

    return lax.fori_loop(0, pieces, one_block, running)


def guarded(step):

    def wrapped(running, members, first_row):
        return step(running, members, first_row)

    def folded(running, members, first_row):
        return over_blocks(wrapped, running, members)

    return folded


def on_device(
    block_input,
    seq_lengths,
    attn_gain,
    qkv_weight,
    proj_weight,
    mlp_gain,
    gelu_weight,
    down_weight,
    out_cotangent,
):
    row_count = block_input.shape[0]
    feature_count = block_input.shape[1]
    lengths = seq_lengths[0]
    group_rows = row_count * lax.axis_size("context")
    own_first = lax.axis_index("context") * row_count
    own_rows = own_first + jnp.arange(row_count, dtype=jnp.int32)
    own_segment, positions = segments_of(own_rows, lengths)
    cosine, sine_tab = rope_tables(positions, HD)
    gathered = (
        lax.all_gather(qkv_weight, "fsdp", axis=0, tiled=True),
        lax.all_gather(proj_weight, "fsdp", axis=1, tiled=True),
        lax.all_gather(gelu_weight, "fsdp", axis=0, tiled=True),
        lax.all_gather(down_weight, "fsdp", axis=1, tiled=True),
        lax.all_gather(attn_gain, "fsdp", axis=0, tiled=True),
        lax.all_gather(mlp_gain, "fsdp", axis=0, tiled=True),
    )
    qkv_full, proj_full, gelu_full, down_full, attn_full, mlp_full = gathered
    local_width = qkv_full.shape[2]
    head_count = local_width // HD
    hidden = gelu_full.shape[2]
    attn_scale = attn_full.astype(jnp.float32)
    mlp_scale = mlp_full.astype(jnp.float32)
    inputs = block_input.astype(jnp.float32)
    normed_attn, spread_attn = layer_norm(inputs)
    hidden_attn = (normed_attn * attn_scale).astype(jnp.bfloat16)
    qkv_flat = qkv_full.reshape(feature_count, 3 * local_width)
    projected = jnp.dot(hidden_attn, qkv_flat, preferred_element_type=jnp.float32).reshape(
        row_count, 3, head_count, HD
    )
    query_bf = rotate(projected[:, 0], cosine, sine_tab).astype(jnp.bfloat16)
    key_bf = rotate(projected[:, 1], cosine, sine_tab).astype(jnp.bfloat16)
    value_bf = projected[:, 2].astype(jnp.bfloat16)
    key_flat = key_bf.reshape(row_count, local_width)
    value_flat = value_bf.reshape(row_count, local_width)
    kv_group = lax.all_gather(
        jnp.concatenate([key_flat, value_flat], axis=1), "context", axis=0, tiled=True
    )
    keys_group, values_group = (kv_group[:, :local_width], kv_group[:, local_width:])
    keys_heads = keys_group.reshape(group_rows, head_count, HD)
    values_heads = values_group.reshape(group_rows, head_count, HD)
    group_segment, unused_pos = segments_of(jnp.arange(group_rows, dtype=jnp.int32), lengths)
    same_group = (own_segment[:, None] == group_segment[None, :])[None]
    fwd_scores = (
        jnp.einsum("qhd,khd->hqk", query_bf, keys_heads, preferred_element_type=jnp.float32) * 0.125
    )
    row_max = jnp.max(jnp.where(same_group, fwd_scores, MASKED_LOW), axis=2)
    denom_sum = jnp.sum(
        jnp.where(same_group, jnp.exp(fwd_scores - row_max[:, :, None]), 0.0), axis=2
    )
    log_total = row_max + jnp.log(denom_sum)
    fwd_weights = jnp.where(same_group, jnp.exp(fwd_scores - log_total[:, :, None]), 0.0).astype(
        jnp.bfloat16
    )
    mixed = jnp.einsum(
        "hqk,khd->qhd", fwd_weights, values_heads, preferred_element_type=jnp.float32
    ).astype(jnp.bfloat16)
    mixed_flat = mixed.reshape(row_count, local_width)
    attn_part = jnp.dot(mixed_flat, proj_full, preferred_element_type=jnp.float32)
    residual = inputs + pair_sum(attn_part, "tensor")
    normed_mlp, spread_mlp = layer_norm(residual)
    hidden_mlp = (normed_mlp * mlp_scale).astype(jnp.bfloat16)
    gelu_flat = gelu_full.reshape(feature_count, 2 * hidden)
    gate_up = jnp.dot(hidden_mlp, gelu_flat, preferred_element_type=jnp.float32).reshape(
        row_count, 2, hidden
    )
    gate_pre, up_pre = (gate_up[:, 0], gate_up[:, 1])
    gelu_val, gelu_slope = gelu_parts(gate_pre)
    activ = (gelu_val * up_pre).astype(jnp.bfloat16)
    mlp_part = jnp.dot(activ, down_full, preferred_element_type=jnp.float32)
    block_output = (
        residual + pair_sum(mlp_part.astype(jnp.bfloat16), "tensor")
    ).astype(jnp.bfloat16)
    act_grad = jnp.dot(out_cotangent, down_full.T, preferred_element_type=jnp.float32)
    down_grad_t = jnp.dot(out_cotangent.T, activ, preferred_element_type=jnp.float32)
    gate_up_grad = (
        jnp.stack([act_grad * up_pre * gelu_slope, act_grad * gelu_val], axis=1)
        .astype(jnp.bfloat16)
        .reshape(row_count, 2 * hidden)
    )
    gelu_grad = jnp.dot(hidden_mlp.T, gate_up_grad, preferred_element_type=jnp.float32).reshape(
        feature_count, 2, hidden
    )
    mlp_in_grad = pair_sum(
        jnp.dot(gate_up_grad, gelu_flat.T, preferred_element_type=jnp.float32), "tensor"
    )
    mlpgain_grad = jnp.sum(mlp_in_grad * normed_mlp, axis=0)
    resid_grad = out_cotangent.astype(jnp.float32) + norm_back(
        mlp_in_grad, normed_mlp, spread_mlp, mlp_scale
    )
    resid_bf = resid_grad.astype(jnp.bfloat16)
    out_grad = jnp.dot(resid_bf, proj_full.T, preferred_element_type=jnp.float32).astype(
        jnp.bfloat16
    )
    proj_grad_t = jnp.dot(resid_bf.T, mixed_flat, preferred_element_type=jnp.float32)
    out_heads = out_grad.reshape(row_count, head_count, HD)
    delta = jnp.transpose(
        jnp.sum(out_heads.astype(jnp.float32) * mixed.astype(jnp.float32), axis=2)
    )

    def key_terms(members, first_row):
        key_count = members[0].shape[0]
        key_part = members[0].reshape(key_count, head_count, HD)
        value_part = members[1].reshape(key_count, head_count, HD)
        key_segment, unused = segments_of(
            first_row + jnp.arange(key_count, dtype=jnp.int32), lengths
        )
        same_doc = (own_segment[:, None] == key_segment[None, :])[None]
        scores = (
            jnp.einsum("qhd,khd->hqk", query_bf, key_part, preferred_element_type=jnp.float32)
            * 0.125
        )
        weights = jnp.where(same_doc, jnp.exp(scores - log_total[:, :, None]), 0.0)
        prob_grad = jnp.einsum(
            "qhd,khd->hqk", out_heads, value_part, preferred_element_type=jnp.float32
        )
        score_grad = (weights * (prob_grad - delta[:, :, None])).astype(jnp.bfloat16)
        return (key_part, weights, score_grad)

    def owner_step(running, members, first_row):
        query_grad, key_all, value_all = running
        key_part, weights, score_grad = key_terms(members, first_row)
        key_count = key_part.shape[0]
        query_grad = (
            query_grad
            + jnp.einsum("hqk,khd->qhd", score_grad, key_part, preferred_element_type=jnp.float32)
            * 0.125
        )
        key_piece = (
            jnp.einsum(
                "hqk,qhd->khd", score_grad, query_bf, preferred_element_type=jnp.float32
            ).reshape(key_count, local_width)
            * 0.125
        )
        value_piece = jnp.einsum(
            "hqk,qhd->khd",
            weights.astype(jnp.bfloat16),
            out_heads,
            preferred_element_type=jnp.float32,
        ).reshape(key_count, local_width)
        key_all = lax.dynamic_update_slice_in_dim(
            key_all,
            lax.dynamic_slice_in_dim(key_all, first_row, key_count, 0) + key_piece,
            first_row,
            0,
        )
        value_all = lax.dynamic_update_slice_in_dim(
            value_all,
            lax.dynamic_slice_in_dim(value_all, first_row, key_count, 0) + value_piece,
            first_row,
            0,
        )
        return (query_grad, key_all, value_all)

    grad_start = jnp.zeros((row_count, head_count, HD), jnp.float32)
    back_state = (
        grad_start,
        jnp.zeros((group_rows, local_width), jnp.float32),
        jnp.zeros((group_rows, local_width), jnp.float32),
    )
    back_result = guarded(owner_step)(
        back_state,
        (keys_group, values_group),
        jnp.int32(0),
    )
    query_grad = back_result[0]
    kv_grad = lax.psum_scatter(
        jnp.concatenate([back_result[1], back_result[2]], axis=1).astype(jnp.bfloat16),
        "context",
        scatter_dimension=0,
        tiled=True,
    ).astype(jnp.float32)
    key_grad, value_grad = (kv_grad[:, :local_width], kv_grad[:, local_width:])
    key_grad = key_grad.reshape(row_count, head_count, HD)
    value_grad = value_grad.reshape(row_count, head_count, HD)
    qkv_rows = (
        jnp.stack(
            [
                rotate_back(query_grad, cosine, sine_tab),
                rotate_back(key_grad, cosine, sine_tab),
                value_grad,
            ],
            axis=1,
        )
        .astype(jnp.bfloat16)
        .reshape(row_count, 3 * local_width)
    )
    qkv_grad = jnp.dot(hidden_attn.T, qkv_rows, preferred_element_type=jnp.float32).reshape(
        feature_count, 3, local_width
    )
    attn_in_grad = pair_sum(
        jnp.dot(qkv_rows, qkv_flat.T, preferred_element_type=jnp.float32).astype(jnp.bfloat16),
        "tensor",
    )
    attngain_grad = jnp.sum(attn_in_grad * normed_attn, axis=0)
    input_grad = resid_grad + norm_back(attn_in_grad, normed_attn, spread_attn, attn_scale)
    grads = (
        attngain_grad[:, None],
        mlpgain_grad[:, None],
        qkv_grad.reshape(feature_count, 3 * local_width),
        gelu_grad.reshape(feature_count, 2 * hidden),
        proj_grad_t,
        down_grad_t,
    )
    widths = [g.shape[1] for g in grads]
    packed = jnp.concatenate(grads, axis=1)
    packed = lax.psum_scatter(packed, "fsdp", scatter_dimension=0, tiled=True)
    packed = lax.psum(packed, "context")
    pieces = []
    start = 0
    for width in widths:
        pieces.append(packed[:, start : start + width])
        start += width
    shard_rows = packed.shape[0]
    shares = (
        pieces[0][:, 0],
        pieces[2].reshape(shard_rows, 3, local_width),
        pieces[4].T,
        pieces[1][:, 0],
        pieces[3].reshape(shard_rows, 2, hidden),
        pieces[5].T,
    )
    return (
        block_output,
        input_grad,
        shares[0],
        shares[1],
        shares[2],
        shares[3],
        shares[4],
        shares[5],
    )


def solution(mesh):
    in_specs = (
        P(("fsdp", "context"), None),
        P("fsdp", None),
        P("fsdp"),
        P("fsdp", None, "tensor"),
        P("tensor", "fsdp"),
        P("fsdp"),
        P("fsdp", None, "tensor"),
        P("tensor", "fsdp"),
        P(("fsdp", "context"), None),
    )
    out_specs = (
        P(("fsdp", "context"), None),
        P(("fsdp", "context"), None),
        P("fsdp"),
        P("fsdp", None, "tensor"),
        P("tensor", "fsdp"),
        P("fsdp"),
        P("fsdp", None, "tensor"),
        P("tensor", "fsdp"),
    )
    return jax.shard_map(
        on_device, mesh=mesh, in_specs=in_specs, out_specs=out_specs, check_vma=False
    )
```

```python
import jax
import jax.numpy as jnp
from jax import lax
from jax.sharding import PartitionSpec as P

HD = 64


EPSILON = 1e-05
THETA = 160000.0
MASKED_LOW = -1e30


def layer_norm(values):
    centre = values - jnp.mean(values, axis=-1, keepdims=True)
    spread = lax.rsqrt(jnp.mean(centre * centre, axis=-1, keepdims=True) + EPSILON)
    return (centre * spread, spread)


def norm_back(grad_out, normed, spread, gain):
    scaled = grad_out * gain
    inner = jnp.mean(scaled, axis=-1, keepdims=True) + normed * jnp.mean(
        scaled * normed, axis=-1, keepdims=True
    )
    return spread * (scaled - inner)


def segments_of(row_ids, lengths):
    ends = jnp.cumsum(lengths)
    segment = jnp.sum((row_ids[:, None] >= ends[None, :]).astype(jnp.int32), axis=1)
    starts = ends - lengths
    picked = segment[:, None] == jnp.arange(lengths.shape[0], dtype=jnp.int32)[None, :]
    begin = jnp.sum(jnp.where(picked, starts[None, :], 0), axis=1)
    return (segment, row_ids - begin)


def rope_tables(positions, head_dim):
    half_dim = head_dim // 2
    exponent = jnp.arange(half_dim, dtype=jnp.float32) * (-2.0 / head_dim)
    frequency = jnp.power(jnp.float32(THETA), exponent)
    angles = positions.astype(jnp.float32)[:, None] * frequency[None, :]
    return (jnp.cos(angles)[:, None, :], jnp.sin(angles)[:, None, :])


def rotate(values, cosine, sine_tab):
    half_dim = values.shape[-1] // 2
    lower_half, upper_half = (values[..., :half_dim], values[..., half_dim:])
    return jnp.concatenate(
        [lower_half * cosine - upper_half * sine_tab, upper_half * cosine + lower_half * sine_tab],
        axis=-1,
    )


def rotate_back(grads, cosine, sine_tab):
    half_dim = grads.shape[-1] // 2
    lower_half, upper_half = (grads[..., :half_dim], grads[..., half_dim:])
    return jnp.concatenate(
        [lower_half * cosine + upper_half * sine_tab, upper_half * cosine - lower_half * sine_tab],
        axis=-1,
    )


def gelu_parts(gate_pre):
    normal_cdf = 0.5 * (1.0 + jax.scipy.special.erf(gate_pre * 0.7071067811865476))
    density = jnp.exp(-0.5 * gate_pre * gate_pre) * 0.3989422804014327
    return (gate_pre * normal_cdf, normal_cdf + gate_pre * density)


def pair_sum(values, axis_name):
    if lax.axis_size(axis_name) != 2:
        return lax.psum(values, axis_name)
    other = lax.ppermute(values, axis_name, perm=[(0, 1), (1, 0)])
    return values.astype(jnp.float32) + other.astype(jnp.float32)


def split_count(row_count):
    pieces = 1
    while row_count // pieces > 1024 and row_count % (2 * pieces) == 0:
        pieces = pieces * 2
    return pieces


def over_blocks(step, running, members):
    row_count = members[0].shape[0]
    pieces = split_count(row_count)
    stride = row_count // pieces

    def one_block(counter, current):
        offset = counter * stride
        sliced = tuple((lax.dynamic_slice_in_dim(member, offset, stride, 0) for member in members))
        return step(current, sliced, offset)

    return lax.fori_loop(0, pieces, one_block, running)


def guarded(step):

    def wrapped(running, members, first_row):
        return step(running, members, first_row)

    def folded(running, members, first_row):
        return over_blocks(wrapped, running, members)

    return folded


def on_device(
    block_input,
    seq_lengths,
    attn_gain,
    qkv_weight,
    proj_weight,
    mlp_gain,
    gelu_weight,
    down_weight,
    out_cotangent,
):
    row_count = block_input.shape[0]
    feature_count = block_input.shape[1]
    lengths = seq_lengths[0]
    group_rows = row_count * lax.axis_size("context")
    own_first = lax.axis_index("context") * row_count
    own_rows = own_first + jnp.arange(row_count, dtype=jnp.int32)
    own_segment, positions = segments_of(own_rows, lengths)
    cosine, sine_tab = rope_tables(positions, HD)
    gathered = (
        lax.all_gather(qkv_weight, "fsdp", axis=0, tiled=True),
        lax.all_gather(proj_weight, "fsdp", axis=1, tiled=True),
        lax.all_gather(gelu_weight, "fsdp", axis=0, tiled=True),
        lax.all_gather(down_weight, "fsdp", axis=1, tiled=True),
        lax.all_gather(attn_gain, "fsdp", axis=0, tiled=True),
        lax.all_gather(mlp_gain, "fsdp", axis=0, tiled=True),
    )
    qkv_full, proj_full, gelu_full, down_full, attn_full, mlp_full = gathered
    local_width = qkv_full.shape[2]
    head_count = local_width // HD
    hidden = gelu_full.shape[2]
    attn_scale = attn_full.astype(jnp.float32)
    mlp_scale = mlp_full.astype(jnp.float32)
    inputs = block_input.astype(jnp.float32)
    normed_attn, spread_attn = layer_norm(inputs)
    hidden_attn = (normed_attn * attn_scale).astype(jnp.bfloat16)
    qkv_flat = qkv_full.reshape(feature_count, 3 * local_width)
    projected = jnp.dot(hidden_attn, qkv_flat, preferred_element_type=jnp.float32).reshape(
        row_count, 3, head_count, HD
    )
    query_bf = rotate(projected[:, 0], cosine, sine_tab).astype(jnp.bfloat16)
    key_bf = rotate(projected[:, 1], cosine, sine_tab).astype(jnp.bfloat16)
    value_bf = projected[:, 2].astype(jnp.bfloat16)
    key_flat = key_bf.reshape(row_count, local_width)
    value_flat = value_bf.reshape(row_count, local_width)
    kv_group = lax.all_gather(
        jnp.concatenate([key_flat, value_flat], axis=1), "context", axis=0, tiled=True
    )
    keys_group, values_group = (kv_group[:, :local_width], kv_group[:, local_width:])
    keys_heads = keys_group.reshape(group_rows, head_count, HD)
    values_heads = values_group.reshape(group_rows, head_count, HD)
    group_segment, unused_pos = segments_of(jnp.arange(group_rows, dtype=jnp.int32), lengths)
    same_group = (own_segment[:, None] == group_segment[None, :])[None]
    fwd_scores = (
        jnp.einsum("qhd,khd->hqk", query_bf, keys_heads, preferred_element_type=jnp.float32) * 0.125
    )
    row_max = jnp.max(jnp.where(same_group, fwd_scores, MASKED_LOW), axis=2)
    denom_sum = jnp.sum(
        jnp.where(same_group, jnp.exp(fwd_scores - row_max[:, :, None]), 0.0), axis=2
    )
    log_total = row_max + jnp.log(denom_sum)
    fwd_weights = jnp.where(same_group, jnp.exp(fwd_scores - log_total[:, :, None]), 0.0).astype(
        jnp.bfloat16
    )
    mixed = jnp.einsum(
        "hqk,khd->qhd", fwd_weights, values_heads, preferred_element_type=jnp.float32
    ).astype(jnp.bfloat16)
    mixed_flat = mixed.reshape(row_count, local_width)
    attn_part = jnp.dot(mixed_flat, proj_full, preferred_element_type=jnp.float32)
    residual = inputs + pair_sum(attn_part, "tensor")
    normed_mlp, spread_mlp = layer_norm(residual)
    hidden_mlp = (normed_mlp * mlp_scale).astype(jnp.bfloat16)
    gelu_flat = gelu_full.reshape(feature_count, 2 * hidden)
    gate_up = jnp.dot(hidden_mlp, gelu_flat, preferred_element_type=jnp.float32).reshape(
        row_count, 2, hidden
    )
    gate_pre, up_pre = (gate_up[:, 0], gate_up[:, 1])
    gelu_val, gelu_slope = gelu_parts(gate_pre)
    activ = (gelu_val * up_pre).astype(jnp.bfloat16)
    mlp_part = jnp.dot(activ, down_full, preferred_element_type=jnp.float32)
    block_output = (
        residual + pair_sum(mlp_part.astype(jnp.bfloat16), "tensor")
    ).astype(jnp.bfloat16)
    act_grad = jnp.dot(out_cotangent, down_full.T, preferred_element_type=jnp.float32)
    down_grad_t = jnp.dot(out_cotangent.T, activ, preferred_element_type=jnp.float32)
    gate_up_grad = (
        jnp.stack([act_grad * up_pre * gelu_slope, act_grad * gelu_val], axis=1)
        .astype(jnp.bfloat16)
        .reshape(row_count, 2 * hidden)
    )
    gelu_grad = jnp.dot(hidden_mlp.T, gate_up_grad, preferred_element_type=jnp.float32).reshape(
        feature_count, 2, hidden
    )
    mlp_in_grad = pair_sum(
        jnp.dot(gate_up_grad, gelu_flat.T, preferred_element_type=jnp.float32), "tensor"
    )
    mlpgain_grad = jnp.sum(mlp_in_grad * normed_mlp, axis=0)
    resid_grad = out_cotangent.astype(jnp.float32) + norm_back(
        mlp_in_grad, normed_mlp, spread_mlp, mlp_scale
    )
    resid_bf = resid_grad.astype(jnp.bfloat16)
    out_grad = jnp.dot(resid_bf, proj_full.T, preferred_element_type=jnp.float32).astype(
        jnp.bfloat16
    )
    proj_grad_t = jnp.dot(resid_bf.T, mixed_flat, preferred_element_type=jnp.float32)
    out_heads = out_grad.reshape(row_count, head_count, HD)
    delta = jnp.transpose(
        jnp.sum(out_heads.astype(jnp.float32) * mixed.astype(jnp.float32), axis=2)
    )

    def key_terms(members, first_row):
        key_count = members[0].shape[0]
        key_part = members[0].reshape(key_count, head_count, HD)
        value_part = members[1].reshape(key_count, head_count, HD)
        key_segment, unused = segments_of(
            first_row + jnp.arange(key_count, dtype=jnp.int32), lengths
        )
        same_doc = (own_segment[:, None] == key_segment[None, :])[None]
        scores = (
            jnp.einsum("qhd,khd->hqk", query_bf, key_part, preferred_element_type=jnp.float32)
            * 0.125
        )
        weights = jnp.where(same_doc, jnp.exp(scores - log_total[:, :, None]), 0.0)
        prob_grad = jnp.einsum(
            "qhd,khd->hqk", out_heads, value_part, preferred_element_type=jnp.float32
        )
        score_grad = (weights * (prob_grad - delta[:, :, None])).astype(jnp.bfloat16)
        return (key_part, weights, score_grad)

    def owner_step(running, members, first_row):
        query_grad, key_all, value_all = running
        key_part, weights, score_grad = key_terms(members, first_row)
        key_count = key_part.shape[0]
        query_grad = (
            query_grad
            + jnp.einsum("hqk,khd->qhd", score_grad, key_part, preferred_element_type=jnp.float32)
            * 0.125
        )
        key_piece = (
            jnp.einsum(
                "hqk,qhd->khd", score_grad, query_bf, preferred_element_type=jnp.float32
            ).reshape(key_count, local_width)
            * 0.125
        )
        value_piece = jnp.einsum(
            "hqk,qhd->khd",
            weights.astype(jnp.bfloat16),
            out_heads,
            preferred_element_type=jnp.float32,
        ).reshape(key_count, local_width)
        key_all = lax.dynamic_update_slice_in_dim(
            key_all,
            lax.dynamic_slice_in_dim(key_all, first_row, key_count, 0) + key_piece,
            first_row,
            0,
        )
        value_all = lax.dynamic_update_slice_in_dim(
            value_all,
            lax.dynamic_slice_in_dim(value_all, first_row, key_count, 0) + value_piece,
            first_row,
            0,
        )
        return (query_grad, key_all, value_all)

    grad_start = jnp.zeros((row_count, head_count, HD), jnp.float32)
    back_state = (
        grad_start,
        jnp.zeros((group_rows, local_width), jnp.float32),
        jnp.zeros((group_rows, local_width), jnp.float32),
    )
    back_result = guarded(owner_step)(
        back_state,
        (keys_group, values_group),
        jnp.int32(0),
    )
    query_grad = back_result[0]
    kv_grad = lax.psum_scatter(
        jnp.concatenate([back_result[1], back_result[2]], axis=1).astype(jnp.bfloat16),
        "context",
        scatter_dimension=0,
        tiled=True,
    ).astype(jnp.float32)
    key_grad, value_grad = (kv_grad[:, :local_width], kv_grad[:, local_width:])
    key_grad = key_grad.reshape(row_count, head_count, HD)
    value_grad = value_grad.reshape(row_count, head_count, HD)
    qkv_rows = (
        jnp.stack(
            [
                rotate_back(query_grad, cosine, sine_tab),
                rotate_back(key_grad, cosine, sine_tab),
                value_grad,
            ],
            axis=1,
        )
        .astype(jnp.bfloat16)
        .reshape(row_count, 3 * local_width)
    )
    qkv_grad = jnp.dot(hidden_attn.T, qkv_rows, preferred_element_type=jnp.float32).reshape(
        feature_count, 3, local_width
    )
    attn_in_grad = pair_sum(
        jnp.dot(qkv_rows, qkv_flat.T, preferred_element_type=jnp.float32).astype(jnp.bfloat16),
        "tensor",
    )
    attngain_grad = jnp.sum(attn_in_grad * normed_attn, axis=0)
    input_grad = resid_grad + norm_back(attn_in_grad, normed_attn, spread_attn, attn_scale)
    grads = (
        attngain_grad[:, None],
        mlpgain_grad[:, None],
        qkv_grad.reshape(feature_count, 3 * local_width),
        gelu_grad.reshape(feature_count, 2 * hidden),
        proj_grad_t,
        down_grad_t,
    )
    widths = [g.shape[1] for g in grads]
    packed = jnp.concatenate(grads, axis=1).astype(jnp.bfloat16)
    packed = lax.psum_scatter(packed, "fsdp", scatter_dimension=0, tiled=True)
    packed = lax.psum(packed, "context").astype(jnp.float32)
    pieces = []
    start = 0
    for width in widths:
        pieces.append(packed[:, start : start + width])
        start += width
    shard_rows = packed.shape[0]
    shares = (
        pieces[0][:, 0],
        pieces[2].reshape(shard_rows, 3, local_width),
        pieces[4].T,
        pieces[1][:, 0],
        pieces[3].reshape(shard_rows, 2, hidden),
        pieces[5].T,
    )
    return (
        block_output,
        input_grad,
        shares[0],
        shares[1],
        shares[2],
        shares[3],
        shares[4],
        shares[5],
    )


def solution(mesh):
    in_specs = (
        P(("fsdp", "context"), None),
        P("fsdp", None),
        P("fsdp"),
        P("fsdp", None, "tensor"),
        P("tensor", "fsdp"),
        P("fsdp"),
        P("fsdp", None, "tensor"),
        P("tensor", "fsdp"),
        P(("fsdp", "context"), None),
    )
    out_specs = (
        P(("fsdp", "context"), None),
        P(("fsdp", "context"), None),
        P("fsdp"),
        P("fsdp", None, "tensor"),
        P("tensor", "fsdp"),
        P("fsdp"),
        P("fsdp", None, "tensor"),
        P("tensor", "fsdp"),
    )
    return jax.shard_map(
        on_device, mesh=mesh, in_specs=in_specs, out_specs=out_specs, check_vma=False
    )
```

```python
import jax
import jax.numpy as jnp
from jax import lax
from jax.sharding import PartitionSpec as P

HD = 64


EPSILON = 1e-05
THETA = 160000.0
MASKED_LOW = -1e30


def layer_norm(values):
    centre = values - jnp.mean(values, axis=-1, keepdims=True)
    spread = lax.rsqrt(jnp.mean(centre * centre, axis=-1, keepdims=True) + EPSILON)
    return (centre * spread, spread)


def norm_back(grad_out, normed, spread, gain):
    scaled = grad_out * gain
    inner = jnp.mean(scaled, axis=-1, keepdims=True) + normed * jnp.mean(
        scaled * normed, axis=-1, keepdims=True
    )
    return spread * (scaled - inner)


def segments_of(row_ids, lengths):
    ends = jnp.cumsum(lengths)
    segment = jnp.sum((row_ids[:, None] >= ends[None, :]).astype(jnp.int32), axis=1)
    starts = ends - lengths
    picked = segment[:, None] == jnp.arange(lengths.shape[0], dtype=jnp.int32)[None, :]
    begin = jnp.sum(jnp.where(picked, starts[None, :], 0), axis=1)
    return (segment, row_ids - begin)


def rope_tables(positions, head_dim):
    half_dim = head_dim // 2
    exponent = jnp.arange(half_dim, dtype=jnp.float32) * (-2.0 / head_dim)
    frequency = jnp.power(jnp.float32(THETA), exponent)
    angles = positions.astype(jnp.float32)[:, None] * frequency[None, :]
    return (jnp.cos(angles)[:, None, :], jnp.sin(angles)[:, None, :])


def rotate(values, cosine, sine_tab):
    half_dim = values.shape[-1] // 2
    lower_half, upper_half = (values[..., :half_dim], values[..., half_dim:])
    return jnp.concatenate(
        [lower_half * cosine - upper_half * sine_tab, upper_half * cosine + lower_half * sine_tab],
        axis=-1,
    )


def rotate_back(grads, cosine, sine_tab):
    half_dim = grads.shape[-1] // 2
    lower_half, upper_half = (grads[..., :half_dim], grads[..., half_dim:])
    return jnp.concatenate(
        [lower_half * cosine + upper_half * sine_tab, upper_half * cosine - lower_half * sine_tab],
        axis=-1,
    )


def gelu_parts(gate_pre):
    normal_cdf = 0.5 * (1.0 + jax.scipy.special.erf(gate_pre * 0.7071067811865476))
    density = jnp.exp(-0.5 * gate_pre * gate_pre) * 0.3989422804014327
    return (gate_pre * normal_cdf, normal_cdf + gate_pre * density)


def pair_sum(values, axis_name):
    if lax.axis_size(axis_name) != 2:
        return lax.psum(values, axis_name)
    other = lax.ppermute(values, axis_name, perm=[(0, 1), (1, 0)])
    return values.astype(jnp.float32) + other.astype(jnp.float32)


def context_gather(values, axis_name):
    count = lax.axis_size(axis_name)
    spread = jnp.broadcast_to(values[None], (count,) + values.shape)
    gathered = lax.all_to_all(spread, axis_name, 0, 0, tiled=True)
    return gathered.reshape((count * values.shape[0],) + values.shape[1:])


def context_scatter_sum(values, axis_name):
    count = lax.axis_size(axis_name)
    rows = values.shape[0] // count
    parts = lax.all_to_all(
        values.reshape((count, rows) + values.shape[1:]), axis_name, 0, 0, tiled=True
    )
    return jnp.sum(parts.astype(jnp.float32), axis=0)


def split_count(row_count):
    pieces = 1
    while row_count // pieces > 1024 and row_count % (2 * pieces) == 0:
        pieces = pieces * 2
    return pieces


def over_blocks(step, running, members):
    row_count = members[0].shape[0]
    pieces = split_count(row_count)
    stride = row_count // pieces

    def one_block(counter, current):
        offset = counter * stride
        sliced = tuple((lax.dynamic_slice_in_dim(member, offset, stride, 0) for member in members))
        return step(current, sliced, offset)

    return lax.fori_loop(0, pieces, one_block, running)


def guarded(step):

    def wrapped(running, members, first_row):
        return step(running, members, first_row)

    def folded(running, members, first_row):
        return over_blocks(wrapped, running, members)

    return folded


def on_device(
    block_input,
    seq_lengths,
    attn_gain,
    qkv_weight,
    proj_weight,
    mlp_gain,
    gelu_weight,
    down_weight,
    out_cotangent,
):
    row_count = block_input.shape[0]
    feature_count = block_input.shape[1]
    lengths = seq_lengths[0]
    group_rows = row_count * lax.axis_size("context")
    own_first = lax.axis_index("context") * row_count
    own_rows = own_first + jnp.arange(row_count, dtype=jnp.int32)
    own_segment, positions = segments_of(own_rows, lengths)
    cosine, sine_tab = rope_tables(positions, HD)
    gathered = (
        lax.all_gather(qkv_weight, "fsdp", axis=0, tiled=True),
        lax.all_gather(proj_weight, "fsdp", axis=1, tiled=True),
        lax.all_gather(gelu_weight, "fsdp", axis=0, tiled=True),
        lax.all_gather(down_weight, "fsdp", axis=1, tiled=True),
        lax.all_gather(attn_gain, "fsdp", axis=0, tiled=True),
        lax.all_gather(mlp_gain, "fsdp", axis=0, tiled=True),
    )
    qkv_full, proj_full, gelu_full, down_full, attn_full, mlp_full = gathered
    local_width = qkv_full.shape[2]
    head_count = local_width // HD
    hidden = gelu_full.shape[2]
    attn_scale = attn_full.astype(jnp.float32)
    mlp_scale = mlp_full.astype(jnp.float32)
    inputs = block_input.astype(jnp.float32)
    normed_attn, spread_attn = layer_norm(inputs)
    hidden_attn = (normed_attn * attn_scale).astype(jnp.bfloat16)
    qkv_flat = qkv_full.reshape(feature_count, 3 * local_width)
    projected = jnp.dot(hidden_attn, qkv_flat, preferred_element_type=jnp.float32).reshape(
        row_count, 3, head_count, HD
    )
    query_bf = rotate(projected[:, 0], cosine, sine_tab).astype(jnp.bfloat16)
    key_bf = rotate(projected[:, 1], cosine, sine_tab).astype(jnp.bfloat16)
    value_bf = projected[:, 2].astype(jnp.bfloat16)
    key_flat = key_bf.reshape(row_count, local_width)
    value_flat = value_bf.reshape(row_count, local_width)
    kv_group = context_gather(jnp.concatenate([key_flat, value_flat], axis=1), "context")
    keys_group, values_group = (kv_group[:, :local_width], kv_group[:, local_width:])
    keys_heads = keys_group.reshape(group_rows, head_count, HD)
    values_heads = values_group.reshape(group_rows, head_count, HD)
    group_segment, unused_pos = segments_of(jnp.arange(group_rows, dtype=jnp.int32), lengths)
    same_group = (own_segment[:, None] == group_segment[None, :])[None]
    fwd_scores = (
        jnp.einsum("qhd,khd->hqk", query_bf, keys_heads, preferred_element_type=jnp.float32) * 0.125
    )
    row_max = jnp.max(jnp.where(same_group, fwd_scores, MASKED_LOW), axis=2)
    denom_sum = jnp.sum(
        jnp.where(same_group, jnp.exp(fwd_scores - row_max[:, :, None]), 0.0), axis=2
    )
    log_total = row_max + jnp.log(denom_sum)
    fwd_weights = jnp.where(same_group, jnp.exp(fwd_scores - log_total[:, :, None]), 0.0).astype(
        jnp.bfloat16
    )
    mixed = jnp.einsum(
        "hqk,khd->qhd", fwd_weights, values_heads, preferred_element_type=jnp.float32
    ).astype(jnp.bfloat16)
    mixed_flat = mixed.reshape(row_count, local_width)
    attn_part = jnp.dot(mixed_flat, proj_full, preferred_element_type=jnp.float32)
    residual = inputs + pair_sum(attn_part, "tensor")
    normed_mlp, spread_mlp = layer_norm(residual)
    hidden_mlp = (normed_mlp * mlp_scale).astype(jnp.bfloat16)
    gelu_flat = gelu_full.reshape(feature_count, 2 * hidden)
    gate_up = jnp.dot(hidden_mlp, gelu_flat, preferred_element_type=jnp.float32).reshape(
        row_count, 2, hidden
    )
    gate_pre, up_pre = (gate_up[:, 0], gate_up[:, 1])
    gelu_val, gelu_slope = gelu_parts(gate_pre)
    activ = (gelu_val * up_pre).astype(jnp.bfloat16)
    mlp_part = jnp.dot(activ, down_full, preferred_element_type=jnp.float32)
    block_output = (
        residual + pair_sum(mlp_part.astype(jnp.bfloat16), "tensor")
    ).astype(jnp.bfloat16)
    act_grad = jnp.dot(out_cotangent, down_full.T, preferred_element_type=jnp.float32)
    down_grad_t = jnp.dot(out_cotangent.T, activ, preferred_element_type=jnp.float32)
    gate_up_grad = (
        jnp.stack([act_grad * up_pre * gelu_slope, act_grad * gelu_val], axis=1)
        .astype(jnp.bfloat16)
        .reshape(row_count, 2 * hidden)
    )
    gelu_grad = jnp.dot(hidden_mlp.T, gate_up_grad, preferred_element_type=jnp.float32).reshape(
        feature_count, 2, hidden
    )
    mlp_in_grad = pair_sum(
        jnp.dot(gate_up_grad, gelu_flat.T, preferred_element_type=jnp.float32), "tensor"
    )
    mlpgain_grad = jnp.sum(mlp_in_grad * normed_mlp, axis=0)
    resid_grad = out_cotangent.astype(jnp.float32) + norm_back(
        mlp_in_grad, normed_mlp, spread_mlp, mlp_scale
    )
    resid_bf = resid_grad.astype(jnp.bfloat16)
    out_grad = jnp.dot(resid_bf, proj_full.T, preferred_element_type=jnp.float32).astype(
        jnp.bfloat16
    )
    proj_grad_t = jnp.dot(resid_bf.T, mixed_flat, preferred_element_type=jnp.float32)
    out_heads = out_grad.reshape(row_count, head_count, HD)
    delta = jnp.transpose(
        jnp.sum(out_heads.astype(jnp.float32) * mixed.astype(jnp.float32), axis=2)
    )

    def key_terms(members, first_row):
        key_count = members[0].shape[0]
        key_part = members[0].reshape(key_count, head_count, HD)
        value_part = members[1].reshape(key_count, head_count, HD)
        key_segment, unused = segments_of(
            first_row + jnp.arange(key_count, dtype=jnp.int32), lengths
        )
        same_doc = (own_segment[:, None] == key_segment[None, :])[None]
        scores = (
            jnp.einsum("qhd,khd->hqk", query_bf, key_part, preferred_element_type=jnp.float32)
            * 0.125
        )
        weights = jnp.where(same_doc, jnp.exp(scores - log_total[:, :, None]), 0.0)
        prob_grad = jnp.einsum(
            "qhd,khd->hqk", out_heads, value_part, preferred_element_type=jnp.float32
        )
        score_grad = (weights * (prob_grad - delta[:, :, None])).astype(jnp.bfloat16)
        return (key_part, weights, score_grad)

    def owner_step(running, members, first_row):
        query_grad, key_all, value_all = running
        key_part, weights, score_grad = key_terms(members, first_row)
        key_count = key_part.shape[0]
        query_grad = (
            query_grad
            + jnp.einsum("hqk,khd->qhd", score_grad, key_part, preferred_element_type=jnp.float32)
            * 0.125
        )
        key_piece = (
            jnp.einsum(
                "hqk,qhd->khd", score_grad, query_bf, preferred_element_type=jnp.float32
            ).reshape(key_count, local_width)
            * 0.125
        )
        value_piece = jnp.einsum(
            "hqk,qhd->khd",
            weights.astype(jnp.bfloat16),
            out_heads,
            preferred_element_type=jnp.float32,
        ).reshape(key_count, local_width)
        key_all = lax.dynamic_update_slice_in_dim(
            key_all,
            lax.dynamic_slice_in_dim(key_all, first_row, key_count, 0) + key_piece,
            first_row,
            0,
        )
        value_all = lax.dynamic_update_slice_in_dim(
            value_all,
            lax.dynamic_slice_in_dim(value_all, first_row, key_count, 0) + value_piece,
            first_row,
            0,
        )
        return (query_grad, key_all, value_all)

    grad_start = jnp.zeros((row_count, head_count, HD), jnp.float32)
    back_state = (
        grad_start,
        jnp.zeros((group_rows, local_width), jnp.float32),
        jnp.zeros((group_rows, local_width), jnp.float32),
    )
    back_result = guarded(owner_step)(
        back_state,
        (keys_group, values_group),
        jnp.int32(0),
    )
    query_grad = back_result[0]
    kv_grad = context_scatter_sum(
        jnp.concatenate([back_result[1], back_result[2]], axis=1).astype(jnp.bfloat16), "context"
    )
    key_grad, value_grad = (kv_grad[:, :local_width], kv_grad[:, local_width:])
    key_grad = key_grad.reshape(row_count, head_count, HD)
    value_grad = value_grad.reshape(row_count, head_count, HD)
    qkv_rows = (
        jnp.stack(
            [
                rotate_back(query_grad, cosine, sine_tab),
                rotate_back(key_grad, cosine, sine_tab),
                value_grad,
            ],
            axis=1,
        )
        .astype(jnp.bfloat16)
        .reshape(row_count, 3 * local_width)
    )
    qkv_grad = jnp.dot(hidden_attn.T, qkv_rows, preferred_element_type=jnp.float32).reshape(
        feature_count, 3, local_width
    )
    attn_in_grad = pair_sum(
        jnp.dot(qkv_rows, qkv_flat.T, preferred_element_type=jnp.float32).astype(jnp.bfloat16),
        "tensor",
    )
    attngain_grad = jnp.sum(attn_in_grad * normed_attn, axis=0)
    input_grad = resid_grad + norm_back(attn_in_grad, normed_attn, spread_attn, attn_scale)
    grads = (
        attngain_grad[:, None],
        mlpgain_grad[:, None],
        qkv_grad.reshape(feature_count, 3 * local_width),
        gelu_grad.reshape(feature_count, 2 * hidden),
        proj_grad_t,
        down_grad_t,
    )
    widths = [g.shape[1] for g in grads]
    packed = jnp.concatenate(grads, axis=1).astype(jnp.bfloat16)
    packed = lax.psum_scatter(packed, "fsdp", scatter_dimension=0, tiled=True)
    packed = context_gather(
        context_scatter_sum(packed, "context").astype(jnp.bfloat16), "context"
    ).astype(jnp.float32)
    pieces = []
    start = 0
    for width in widths:
        pieces.append(packed[:, start : start + width])
        start += width
    shard_rows = packed.shape[0]
    shares = (
        pieces[0][:, 0],
        pieces[2].reshape(shard_rows, 3, local_width),
        pieces[4].T,
        pieces[1][:, 0],
        pieces[3].reshape(shard_rows, 2, hidden),
        pieces[5].T,
    )
    return (
        block_output,
        input_grad,
        shares[0],
        shares[1],
        shares[2],
        shares[3],
        shares[4],
        shares[5],
    )


def solution(mesh):
    in_specs = (
        P(("fsdp", "context"), None),
        P("fsdp", None),
        P("fsdp"),
        P("fsdp", None, "tensor"),
        P("tensor", "fsdp"),
        P("fsdp"),
        P("fsdp", None, "tensor"),
        P("tensor", "fsdp"),
        P(("fsdp", "context"), None),
    )
    out_specs = (
        P(("fsdp", "context"), None),
        P(("fsdp", "context"), None),
        P("fsdp"),
        P("fsdp", None, "tensor"),
        P("tensor", "fsdp"),
        P("fsdp"),
        P("fsdp", None, "tensor"),
        P("tensor", "fsdp"),
    )
    return jax.shard_map(
        on_device, mesh=mesh, in_specs=in_specs, out_specs=out_specs, check_vma=False
    )
```

```python
import jax
import jax.numpy as jnp
from jax import lax
from jax.sharding import PartitionSpec as P

HD = 64


EPSILON = 1e-05
THETA = 160000.0
MASKED_LOW = -1e30


def layer_norm(values):
    centre = values - jnp.mean(values, axis=-1, keepdims=True)
    spread = lax.rsqrt(jnp.mean(centre * centre, axis=-1, keepdims=True) + EPSILON)
    return (centre * spread, spread)


def norm_back(grad_out, normed, spread, gain):
    scaled = grad_out * gain
    inner = jnp.mean(scaled, axis=-1, keepdims=True) + normed * jnp.mean(
        scaled * normed, axis=-1, keepdims=True
    )
    return spread * (scaled - inner)


def segments_of(row_ids, lengths):
    ends = jnp.cumsum(lengths)
    segment = jnp.sum((row_ids[:, None] >= ends[None, :]).astype(jnp.int32), axis=1)
    starts = ends - lengths
    picked = segment[:, None] == jnp.arange(lengths.shape[0], dtype=jnp.int32)[None, :]
    begin = jnp.sum(jnp.where(picked, starts[None, :], 0), axis=1)
    return (segment, row_ids - begin)


def rope_tables(positions, head_dim):
    half_dim = head_dim // 2
    exponent = jnp.arange(half_dim, dtype=jnp.float32) * (-2.0 / head_dim)
    frequency = jnp.power(jnp.float32(THETA), exponent)
    angles = positions.astype(jnp.float32)[:, None] * frequency[None, :]
    return (jnp.cos(angles)[:, None, :], jnp.sin(angles)[:, None, :])


def rotate(values, cosine, sine_tab):
    half_dim = values.shape[-1] // 2
    lower_half, upper_half = (values[..., :half_dim], values[..., half_dim:])
    return jnp.concatenate(
        [lower_half * cosine - upper_half * sine_tab, upper_half * cosine + lower_half * sine_tab],
        axis=-1,
    )


def rotate_back(grads, cosine, sine_tab):
    half_dim = grads.shape[-1] // 2
    lower_half, upper_half = (grads[..., :half_dim], grads[..., half_dim:])
    return jnp.concatenate(
        [lower_half * cosine + upper_half * sine_tab, upper_half * cosine - lower_half * sine_tab],
        axis=-1,
    )


def gelu_parts(gate_pre):
    normal_cdf = 0.5 * (1.0 + jax.scipy.special.erf(gate_pre * 0.7071067811865476))
    density = jnp.exp(-0.5 * gate_pre * gate_pre) * 0.3989422804014327
    return (gate_pre * normal_cdf, normal_cdf + gate_pre * density)


def pair_sum(values, axis_name):
    if lax.axis_size(axis_name) != 2:
        return lax.psum(values, axis_name)
    other = lax.ppermute(values, axis_name, perm=[(0, 1), (1, 0)])
    return values.astype(jnp.float32) + other.astype(jnp.float32)


def context_gather(values, axis_name):
    count = lax.axis_size(axis_name)
    spread = jnp.broadcast_to(values[None], (count,) + values.shape)
    gathered = lax.all_to_all(spread, axis_name, 0, 0, tiled=True)
    return gathered.reshape((count * values.shape[0],) + values.shape[1:])


def context_scatter_sum(values, axis_name):
    count = lax.axis_size(axis_name)
    rows = values.shape[0] // count
    parts = lax.all_to_all(
        values.reshape((count, rows) + values.shape[1:]), axis_name, 0, 0, tiled=True
    )
    return jnp.sum(parts.astype(jnp.float32), axis=0)


def on_device(
    block_input,
    seq_lengths,
    attn_gain,
    qkv_weight,
    proj_weight,
    mlp_gain,
    gelu_weight,
    down_weight,
    out_cotangent,
):
    row_count = block_input.shape[0]
    feature_count = block_input.shape[1]
    lengths = seq_lengths[0]
    group_rows = row_count * lax.axis_size("context")
    own_first = lax.axis_index("context") * row_count
    own_rows = own_first + jnp.arange(row_count, dtype=jnp.int32)
    own_segment, positions = segments_of(own_rows, lengths)
    cosine, sine_tab = rope_tables(positions, HD)
    shard_rows = qkv_weight.shape[0]
    local_width = qkv_weight.shape[2]
    head_count = local_width // HD
    hidden = gelu_weight.shape[2]
    first_pack = lax.all_gather(
        jnp.concatenate(
            [
                qkv_weight.reshape(shard_rows, 3 * local_width),
                attn_gain[:, None],
                mlp_gain[:, None],
            ],
            axis=1,
        ),
        "fsdp",
        axis=0,
        tiled=True,
    )
    second_pack = lax.all_gather(
        jnp.concatenate(
            [proj_weight.T, gelu_weight.reshape(shard_rows, 2 * hidden), down_weight.T], axis=1
        ),
        "fsdp",
        axis=0,
        tiled=True,
    )
    qkv_flat = first_pack[:, : 3 * local_width]
    attn_full = first_pack[:, 3 * local_width]
    mlp_full = first_pack[:, 3 * local_width + 1]
    proj_t = second_pack[:, :local_width]
    gelu_flat = second_pack[:, local_width : local_width + 2 * hidden]
    down_t = second_pack[:, local_width + 2 * hidden :]
    attn_scale = attn_full.astype(jnp.float32)
    mlp_scale = mlp_full.astype(jnp.float32)
    inputs = block_input.astype(jnp.float32)
    normed_attn, spread_attn = layer_norm(inputs)
    hidden_attn = (normed_attn * attn_scale).astype(jnp.bfloat16)
    projected = jnp.dot(hidden_attn, qkv_flat, preferred_element_type=jnp.float32).reshape(
        row_count, 3, head_count, HD
    )
    query_bf = rotate(projected[:, 0], cosine, sine_tab).astype(jnp.bfloat16)
    key_bf = rotate(projected[:, 1], cosine, sine_tab).astype(jnp.bfloat16)
    value_bf = projected[:, 2].astype(jnp.bfloat16)
    key_flat = key_bf.reshape(row_count, local_width)
    value_flat = value_bf.reshape(row_count, local_width)
    kv_group = context_gather(jnp.concatenate([key_flat, value_flat], axis=1), "context")
    keys_group, values_group = (kv_group[:, :local_width], kv_group[:, local_width:])
    keys_heads = keys_group.reshape(group_rows, head_count, HD)
    values_heads = values_group.reshape(group_rows, head_count, HD)
    group_segment, unused_pos = segments_of(jnp.arange(group_rows, dtype=jnp.int32), lengths)
    same_group = (own_segment[:, None] == group_segment[None, :])[None]
    fwd_scores = (
        jnp.einsum("qhd,khd->hqk", query_bf, keys_heads, preferred_element_type=jnp.float32) * 0.125
    )
    row_max = jnp.max(jnp.where(same_group, fwd_scores, MASKED_LOW), axis=2)
    denom_sum = jnp.sum(
        jnp.where(same_group, jnp.exp(fwd_scores - row_max[:, :, None]), 0.0), axis=2
    )
    log_total = row_max + jnp.log(denom_sum)
    fwd_probs = jnp.where(same_group, jnp.exp(fwd_scores - log_total[:, :, None]), 0.0)
    fwd_weights = fwd_probs.astype(jnp.bfloat16)
    mixed = jnp.einsum(
        "hqk,khd->qhd", fwd_weights, values_heads, preferred_element_type=jnp.float32
    ).astype(jnp.bfloat16)
    mixed_flat = mixed.reshape(row_count, local_width)
    attn_part = jnp.dot(mixed_flat, proj_t.T, preferred_element_type=jnp.float32)
    residual = inputs + pair_sum(attn_part, "tensor")
    normed_mlp, spread_mlp = layer_norm(residual)
    hidden_mlp = (normed_mlp * mlp_scale).astype(jnp.bfloat16)
    gate_up = jnp.dot(hidden_mlp, gelu_flat, preferred_element_type=jnp.float32).reshape(
        row_count, 2, hidden
    )
    gate_pre, up_pre = (gate_up[:, 0], gate_up[:, 1])
    gelu_val, gelu_slope = gelu_parts(gate_pre)
    activ = (gelu_val * up_pre).astype(jnp.bfloat16)
    mlp_part = jnp.dot(activ, down_t.T, preferred_element_type=jnp.float32)
    block_output = (
        residual + pair_sum(mlp_part.astype(jnp.bfloat16), "tensor")
    ).astype(jnp.bfloat16)
    act_grad = jnp.dot(out_cotangent, down_t, preferred_element_type=jnp.float32)
    down_grad_t = jnp.dot(out_cotangent.T, activ, preferred_element_type=jnp.float32)
    gate_up_grad = (
        jnp.stack([act_grad * up_pre * gelu_slope, act_grad * gelu_val], axis=1)
        .astype(jnp.bfloat16)
        .reshape(row_count, 2 * hidden)
    )
    gelu_grad = jnp.dot(hidden_mlp.T, gate_up_grad, preferred_element_type=jnp.float32).reshape(
        feature_count, 2, hidden
    )
    mlp_in_grad = pair_sum(
        jnp.dot(gate_up_grad, gelu_flat.T, preferred_element_type=jnp.float32), "tensor"
    )
    mlpgain_grad = jnp.sum(mlp_in_grad * normed_mlp, axis=0)
    resid_grad = out_cotangent.astype(jnp.float32) + norm_back(
        mlp_in_grad, normed_mlp, spread_mlp, mlp_scale
    )
    resid_bf = resid_grad.astype(jnp.bfloat16)
    out_grad = jnp.dot(resid_bf, proj_t, preferred_element_type=jnp.float32).astype(
        jnp.bfloat16
    )
    proj_grad_t = jnp.dot(resid_bf.T, mixed_flat, preferred_element_type=jnp.float32)
    out_heads = out_grad.reshape(row_count, head_count, HD)
    delta = jnp.transpose(
        jnp.sum(out_heads.astype(jnp.float32) * mixed.astype(jnp.float32), axis=2)
    )

    prob_grad = jnp.einsum(
        "qhd,khd->hqk", out_heads, values_heads, preferred_element_type=jnp.float32
    )
    score_grad = (fwd_probs * (prob_grad - delta[:, :, None])).astype(jnp.bfloat16)
    query_grad = (
        jnp.einsum("hqk,khd->qhd", score_grad, keys_heads, preferred_element_type=jnp.float32)
        * 0.125
    )
    key_all = (
        jnp.einsum("hqk,qhd->khd", score_grad, query_bf, preferred_element_type=jnp.float32)
        * 0.125
    ).reshape(group_rows, local_width)
    value_all = jnp.einsum(
        "hqk,qhd->khd", fwd_weights, out_heads, preferred_element_type=jnp.float32
    ).reshape(group_rows, local_width)
    kv_grad = context_scatter_sum(
        jnp.concatenate([key_all, value_all], axis=1).astype(jnp.bfloat16), "context"
    )
    key_grad, value_grad = (kv_grad[:, :local_width], kv_grad[:, local_width:])
    key_grad = key_grad.reshape(row_count, head_count, HD)
    value_grad = value_grad.reshape(row_count, head_count, HD)
    qkv_rows = (
        jnp.stack(
            [
                rotate_back(query_grad, cosine, sine_tab),
                rotate_back(key_grad, cosine, sine_tab),
                value_grad,
            ],
            axis=1,
        )
        .astype(jnp.bfloat16)
        .reshape(row_count, 3 * local_width)
    )
    qkv_grad = jnp.dot(hidden_attn.T, qkv_rows, preferred_element_type=jnp.float32).reshape(
        feature_count, 3, local_width
    )
    attn_in_grad = pair_sum(
        jnp.dot(qkv_rows, qkv_flat.T, preferred_element_type=jnp.float32).astype(jnp.bfloat16),
        "tensor",
    )
    attngain_grad = jnp.sum(attn_in_grad * normed_attn, axis=0)
    input_grad = resid_grad + norm_back(attn_in_grad, normed_attn, spread_attn, attn_scale)
    grads = (
        attngain_grad[:, None],
        mlpgain_grad[:, None],
        qkv_grad.reshape(feature_count, 3 * local_width),
        gelu_grad.reshape(feature_count, 2 * hidden),
        proj_grad_t,
        down_grad_t,
    )
    widths = [g.shape[1] for g in grads]
    packed = jnp.concatenate(grads, axis=1).astype(jnp.bfloat16)
    packed = lax.psum_scatter(packed, "fsdp", scatter_dimension=0, tiled=True)
    packed = context_gather(
        context_scatter_sum(packed, "context").astype(jnp.bfloat16), "context"
    ).astype(jnp.float32)
    pieces = []
    start = 0
    for width in widths:
        pieces.append(packed[:, start : start + width])
        start += width
    shard_rows = packed.shape[0]
    shares = (
        pieces[0][:, 0],
        pieces[2].reshape(shard_rows, 3, local_width),
        pieces[4].T,
        pieces[1][:, 0],
        pieces[3].reshape(shard_rows, 2, hidden),
        pieces[5].T,
    )
    return (
        block_output,
        input_grad,
        shares[0],
        shares[1],
        shares[2],
        shares[3],
        shares[4],
        shares[5],
    )


def solution(mesh):
    in_specs = (
        P(("fsdp", "context"), None),
        P("fsdp", None),
        P("fsdp"),
        P("fsdp", None, "tensor"),
        P("tensor", "fsdp"),
        P("fsdp"),
        P("fsdp", None, "tensor"),
        P("tensor", "fsdp"),
        P(("fsdp", "context"), None),
    )
    out_specs = (
        P(("fsdp", "context"), None),
        P(("fsdp", "context"), None),
        P("fsdp"),
        P("fsdp", None, "tensor"),
        P("tensor", "fsdp"),
        P("fsdp"),
        P("fsdp", None, "tensor"),
        P("tensor", "fsdp"),
    )
    return jax.shard_map(
        on_device, mesh=mesh, in_specs=in_specs, out_specs=out_specs, check_vma=False
    )
```

```python
import jax
import jax.numpy as jnp
from jax import lax
from jax.sharding import PartitionSpec as P

HD = 64


EPSILON = 1e-05
THETA = 160000.0
MASKED_LOW = -1e30


def layer_norm(values):
    centre = values - jnp.mean(values, axis=-1, keepdims=True)
    spread = lax.rsqrt(jnp.mean(centre * centre, axis=-1, keepdims=True) + EPSILON)
    return (centre * spread, spread)


def norm_back(grad_out, normed, spread, gain):
    scaled = grad_out * gain
    inner = jnp.mean(scaled, axis=-1, keepdims=True) + normed * jnp.mean(
        scaled * normed, axis=-1, keepdims=True
    )
    return spread * (scaled - inner)


def segments_of(row_ids, lengths):
    ends = jnp.cumsum(lengths)
    segment = jnp.sum((row_ids[:, None] >= ends[None, :]).astype(jnp.int32), axis=1)
    starts = ends - lengths
    picked = segment[:, None] == jnp.arange(lengths.shape[0], dtype=jnp.int32)[None, :]
    begin = jnp.sum(jnp.where(picked, starts[None, :], 0), axis=1)
    return (segment, row_ids - begin)


def rope_tables(positions, head_dim):
    half_dim = head_dim // 2
    exponent = jnp.arange(half_dim, dtype=jnp.float32) * (-2.0 / head_dim)
    frequency = jnp.power(jnp.float32(THETA), exponent)
    angles = positions.astype(jnp.float32)[:, None] * frequency[None, :]
    return (jnp.cos(angles)[:, None, :], jnp.sin(angles)[:, None, :])


def rotate(values, cosine, sine_tab):
    half_dim = values.shape[-1] // 2
    lower_half, upper_half = (values[..., :half_dim], values[..., half_dim:])
    return jnp.concatenate(
        [lower_half * cosine - upper_half * sine_tab, upper_half * cosine + lower_half * sine_tab],
        axis=-1,
    )


def rotate_back(grads, cosine, sine_tab):
    half_dim = grads.shape[-1] // 2
    lower_half, upper_half = (grads[..., :half_dim], grads[..., half_dim:])
    return jnp.concatenate(
        [lower_half * cosine + upper_half * sine_tab, upper_half * cosine - lower_half * sine_tab],
        axis=-1,
    )


def gelu_parts(gate_pre):
    normal_cdf = 0.5 * (1.0 + jax.scipy.special.erf(gate_pre * 0.7071067811865476))
    density = jnp.exp(-0.5 * gate_pre * gate_pre) * 0.3989422804014327
    return (gate_pre * normal_cdf, normal_cdf + gate_pre * density)


def pair_sum(values, axis_name):
    if lax.axis_size(axis_name) != 2:
        return lax.psum(values, axis_name)
    other = lax.ppermute(values, axis_name, perm=[(0, 1), (1, 0)])
    return values.astype(jnp.float32) + other.astype(jnp.float32)


def context_gather(values, axis_name):
    count = lax.axis_size(axis_name)
    spread = jnp.broadcast_to(values[None], (count,) + values.shape)
    gathered = lax.all_to_all(spread, axis_name, 0, 0, tiled=True)
    return gathered.reshape((count * values.shape[0],) + values.shape[1:])


def context_scatter_sum(values, axis_name):
    count = lax.axis_size(axis_name)
    rows = values.shape[0] // count
    parts = lax.all_to_all(
        values.reshape((count, rows) + values.shape[1:]), axis_name, 0, 0, tiled=True
    )
    return jnp.sum(parts.astype(jnp.float32), axis=0)


def on_device(
    block_input,
    seq_lengths,
    attn_gain,
    qkv_weight,
    proj_weight,
    mlp_gain,
    gelu_weight,
    down_weight,
    out_cotangent,
):
    row_count = block_input.shape[0]
    feature_count = block_input.shape[1]
    lengths = seq_lengths[0]
    group_rows = row_count * lax.axis_size("context")
    own_first = lax.axis_index("context") * row_count
    own_rows = own_first + jnp.arange(row_count, dtype=jnp.int32)
    own_segment, positions = segments_of(own_rows, lengths)
    cosine, sine_tab = rope_tables(positions, HD)
    shard_rows = qkv_weight.shape[0]
    local_width = qkv_weight.shape[2]
    head_count = local_width // HD
    hidden = gelu_weight.shape[2]
    first_pack = lax.all_gather(
        jnp.concatenate(
            [
                qkv_weight.reshape(shard_rows, 3 * local_width),
                attn_gain[:, None],
                mlp_gain[:, None],
            ],
            axis=1,
        ),
        "fsdp",
        axis=0,
        tiled=True,
    )
    second_pack = lax.all_gather(
        jnp.concatenate(
            [proj_weight.T, gelu_weight.reshape(shard_rows, 2 * hidden), down_weight.T], axis=1
        ),
        "fsdp",
        axis=0,
        tiled=True,
    )
    qkv_flat = first_pack[:, : 3 * local_width]
    attn_full = first_pack[:, 3 * local_width]
    mlp_full = first_pack[:, 3 * local_width + 1]
    proj_t = second_pack[:, :local_width]
    gelu_flat = second_pack[:, local_width : local_width + 2 * hidden]
    down_t = second_pack[:, local_width + 2 * hidden :]
    attn_scale = attn_full.astype(jnp.float32)
    mlp_scale = mlp_full.astype(jnp.float32)
    inputs = block_input.astype(jnp.float32)
    normed_attn, spread_attn = layer_norm(inputs)
    hidden_attn = (normed_attn * attn_scale).astype(jnp.bfloat16)
    projected = jnp.dot(hidden_attn, qkv_flat, preferred_element_type=jnp.float32).reshape(
        row_count, 3, head_count, HD
    )
    query_bf = rotate(projected[:, 0], cosine, sine_tab).astype(jnp.bfloat16)
    key_bf = rotate(projected[:, 1], cosine, sine_tab).astype(jnp.bfloat16)
    value_bf = projected[:, 2].astype(jnp.bfloat16)
    key_flat = key_bf.reshape(row_count, local_width)
    value_flat = value_bf.reshape(row_count, local_width)
    kv_group = context_gather(jnp.concatenate([key_flat, value_flat], axis=1), "context")
    keys_group, values_group = (kv_group[:, :local_width], kv_group[:, local_width:])
    keys_heads = keys_group.reshape(group_rows, head_count, HD)
    values_heads = values_group.reshape(group_rows, head_count, HD)
    group_segment, unused_pos = segments_of(jnp.arange(group_rows, dtype=jnp.int32), lengths)
    same_group = (own_segment[:, None] == group_segment[None, :])[None]
    fwd_scores = (
        jnp.einsum("qhd,khd->hqk", query_bf, keys_heads, preferred_element_type=jnp.float32) * 0.125
    )
    row_max = jnp.max(jnp.where(same_group, fwd_scores, MASKED_LOW), axis=2)
    denom_sum = jnp.sum(
        jnp.where(same_group, jnp.exp(fwd_scores - row_max[:, :, None]), 0.0), axis=2
    )
    log_total = row_max + jnp.log(denom_sum)
    fwd_probs = jnp.where(same_group, jnp.exp(fwd_scores - log_total[:, :, None]), 0.0)
    fwd_weights = fwd_probs.astype(jnp.bfloat16)
    mixed = jnp.einsum(
        "hqk,khd->qhd", fwd_weights, values_heads, preferred_element_type=jnp.float32
    ).astype(jnp.bfloat16)
    mixed_flat = mixed.reshape(row_count, local_width)
    attn_part = jnp.dot(mixed_flat, proj_t.T, preferred_element_type=jnp.float32)
    residual = inputs + pair_sum(attn_part, "tensor")
    normed_mlp, spread_mlp = layer_norm(residual)
    hidden_mlp = (normed_mlp * mlp_scale).astype(jnp.bfloat16)
    gate_up = jnp.dot(hidden_mlp, gelu_flat, preferred_element_type=jnp.float32).reshape(
        row_count, 2, hidden
    )
    gate_pre, up_pre = (gate_up[:, 0], gate_up[:, 1])
    gelu_val, gelu_slope = gelu_parts(gate_pre)
    activ = (gelu_val * up_pre).astype(jnp.bfloat16)
    mlp_part = jnp.dot(activ, down_t.T, preferred_element_type=jnp.float32)
    block_output = (
        residual + pair_sum(mlp_part.astype(jnp.bfloat16), "tensor")
    ).astype(jnp.bfloat16)
    act_grad = jnp.dot(out_cotangent, down_t, preferred_element_type=jnp.float32)
    down_grad_t = jnp.dot(out_cotangent.T, activ, preferred_element_type=jnp.float32)
    gate_up_grad = (
        jnp.stack([act_grad * up_pre * gelu_slope, act_grad * gelu_val], axis=1)
        .astype(jnp.bfloat16)
        .reshape(row_count, 2 * hidden)
    )
    gelu_grad = jnp.dot(hidden_mlp.T, gate_up_grad, preferred_element_type=jnp.float32).reshape(
        feature_count, 2, hidden
    )
    mlp_in_grad = pair_sum(
        jnp.dot(gate_up_grad, gelu_flat.T, preferred_element_type=jnp.float32), "tensor"
    )
    mlpgain_grad = jnp.sum(mlp_in_grad * normed_mlp, axis=0)
    resid_grad = out_cotangent.astype(jnp.float32) + norm_back(
        mlp_in_grad, normed_mlp, spread_mlp, mlp_scale
    )
    resid_bf = resid_grad.astype(jnp.bfloat16)
    out_grad = jnp.dot(resid_bf, proj_t, preferred_element_type=jnp.float32).astype(
        jnp.bfloat16
    )
    proj_grad_t = jnp.dot(resid_bf.T, mixed_flat, preferred_element_type=jnp.float32)
    out_heads = out_grad.reshape(row_count, head_count, HD)
    delta = jnp.transpose(
        jnp.sum(out_heads.astype(jnp.float32) * mixed.astype(jnp.float32), axis=2)
    )

    prob_grad = jnp.einsum(
        "qhd,khd->hqk", out_heads, values_heads, preferred_element_type=jnp.float32
    )
    score_grad = (fwd_probs * (prob_grad - delta[:, :, None])).astype(jnp.bfloat16)
    query_grad = (
        jnp.einsum("hqk,khd->qhd", score_grad, keys_heads, preferred_element_type=jnp.float32)
        * 0.125
    )
    key_all = (
        jnp.einsum("hqk,qhd->khd", score_grad, query_bf, preferred_element_type=jnp.float32)
        * 0.125
    ).reshape(group_rows, local_width)
    value_all = jnp.einsum(
        "hqk,qhd->khd", fwd_weights, out_heads, preferred_element_type=jnp.float32
    ).reshape(group_rows, local_width)
    kv_grad = context_scatter_sum(
        jnp.concatenate([key_all, value_all], axis=1).astype(jnp.bfloat16), "context"
    )
    key_grad, value_grad = (kv_grad[:, :local_width], kv_grad[:, local_width:])
    key_grad = key_grad.reshape(row_count, head_count, HD)
    value_grad = value_grad.reshape(row_count, head_count, HD)
    qkv_rows = (
        jnp.stack(
            [
                rotate_back(query_grad, cosine, sine_tab),
                rotate_back(key_grad, cosine, sine_tab),
                value_grad,
            ],
            axis=1,
        )
        .astype(jnp.bfloat16)
        .reshape(row_count, 3 * local_width)
    )
    qkv_grad = jnp.dot(hidden_attn.T, qkv_rows, preferred_element_type=jnp.float32).reshape(
        feature_count, 3, local_width
    )
    attn_in_grad = pair_sum(
        jnp.dot(qkv_rows, qkv_flat.T, preferred_element_type=jnp.float32).astype(jnp.bfloat16),
        "tensor",
    )
    attngain_grad = jnp.sum(attn_in_grad * normed_attn, axis=0)
    input_grad = resid_grad + norm_back(attn_in_grad, normed_attn, spread_attn, attn_scale)
    def reduce_pack(members):
        packed = jnp.concatenate(members, axis=1).astype(jnp.bfloat16)
        packed = lax.psum_scatter(packed, "fsdp", scatter_dimension=0, tiled=True)
        packed = context_gather(
            context_scatter_sum(packed, "context").astype(jnp.bfloat16), "context"
        ).astype(jnp.float32)
        pieces = []
        start = 0
        for member in members:
            pieces.append(packed[:, start : start + member.shape[1]])
            start += member.shape[1]
        return pieces

    mlp_pieces = reduce_pack(
        [mlpgain_grad[:, None], gelu_grad.reshape(feature_count, 2 * hidden), down_grad_t]
    )
    attn_pieces = reduce_pack(
        [attngain_grad[:, None], qkv_grad.reshape(feature_count, 3 * local_width), proj_grad_t]
    )
    shares = (
        attn_pieces[0][:, 0],
        attn_pieces[1].reshape(shard_rows, 3, local_width),
        attn_pieces[2].T,
        mlp_pieces[0][:, 0],
        mlp_pieces[1].reshape(shard_rows, 2, hidden),
        mlp_pieces[2].T,
    )
    return (
        block_output,
        input_grad,
        shares[0],
        shares[1],
        shares[2],
        shares[3],
        shares[4],
        shares[5],
    )


def solution(mesh):
    in_specs = (
        P(("fsdp", "context"), None),
        P("fsdp", None),
        P("fsdp"),
        P("fsdp", None, "tensor"),
        P("tensor", "fsdp"),
        P("fsdp"),
        P("fsdp", None, "tensor"),
        P("tensor", "fsdp"),
        P(("fsdp", "context"), None),
    )
    out_specs = (
        P(("fsdp", "context"), None),
        P(("fsdp", "context"), None),
        P("fsdp"),
        P("fsdp", None, "tensor"),
        P("tensor", "fsdp"),
        P("fsdp"),
        P("fsdp", None, "tensor"),
        P("tensor", "fsdp"),
    )
    return jax.shard_map(
        on_device, mesh=mesh, in_specs=in_specs, out_specs=out_specs, check_vma=False
    )
```

```python
import functools

import jax
import jax.numpy as jnp
from jax import lax
from jax.experimental import pallas as pl
from jax.experimental.pallas import tpu as pltpu
from jax.sharding import PartitionSpec as P

HD = 64


EPSILON = 1e-05
THETA = 160000.0
MASKED_LOW = -1e30


def layer_norm(values):
    centre = values - jnp.mean(values, axis=-1, keepdims=True)
    spread = lax.rsqrt(jnp.mean(centre * centre, axis=-1, keepdims=True) + EPSILON)
    return (centre * spread, spread)


def norm_back(grad_out, normed, spread, gain):
    scaled = grad_out * gain
    inner = jnp.mean(scaled, axis=-1, keepdims=True) + normed * jnp.mean(
        scaled * normed, axis=-1, keepdims=True
    )
    return spread * (scaled - inner)


def segments_of(row_ids, lengths):
    ends = jnp.cumsum(lengths)
    segment = jnp.sum((row_ids[:, None] >= ends[None, :]).astype(jnp.int32), axis=1)
    starts = ends - lengths
    picked = segment[:, None] == jnp.arange(lengths.shape[0], dtype=jnp.int32)[None, :]
    begin = jnp.sum(jnp.where(picked, starts[None, :], 0), axis=1)
    return (segment, row_ids - begin)


def rope_tables(positions, head_dim):
    half_dim = head_dim // 2
    exponent = jnp.arange(half_dim, dtype=jnp.float32) * (-2.0 / head_dim)
    frequency = jnp.power(jnp.float32(THETA), exponent)
    angles = positions.astype(jnp.float32)[:, None] * frequency[None, :]
    return (jnp.cos(angles)[:, None, :], jnp.sin(angles)[:, None, :])


def rotate(values, cosine, sine_tab):
    half_dim = values.shape[-1] // 2
    lower_half, upper_half = (values[..., :half_dim], values[..., half_dim:])
    return jnp.concatenate(
        [lower_half * cosine - upper_half * sine_tab, upper_half * cosine + lower_half * sine_tab],
        axis=-1,
    )


def rotate_back(grads, cosine, sine_tab):
    half_dim = grads.shape[-1] // 2
    lower_half, upper_half = (grads[..., :half_dim], grads[..., half_dim:])
    return jnp.concatenate(
        [lower_half * cosine + upper_half * sine_tab, upper_half * cosine - lower_half * sine_tab],
        axis=-1,
    )


def gelu_parts(gate_pre):
    normal_cdf = 0.5 * (1.0 + jax.scipy.special.erf(gate_pre * 0.7071067811865476))
    density = jnp.exp(-0.5 * gate_pre * gate_pre) * 0.3989422804014327
    return (gate_pre * normal_cdf, normal_cdf + gate_pre * density)


def pair_sum(values, axis_name):
    if lax.axis_size(axis_name) != 2:
        return lax.psum(values, axis_name)
    other = lax.ppermute(values, axis_name, perm=[(0, 1), (1, 0)])
    return values.astype(jnp.float32) + other.astype(jnp.float32)


def exchange_kernel(same, axis_name, count, source, landed, send_sem, recv_sem):
    me = lax.axis_index(axis_name)
    barrier = pltpu.get_barrier_semaphore()
    for step in range(1, count):
        peer = lax.rem(me + step, count)
        pl.semaphore_signal(
            barrier, inc=1, device_id={axis_name: peer}, device_id_type=pl.DeviceIdType.MESH
        )
    pl.semaphore_wait(barrier, count - 1)
    copies = []
    for step in range(1, count):
        peer = lax.rem(me + step, count)
        copy = pltpu.make_async_remote_copy(
            src_ref=source if same else source.at[peer],
            dst_ref=landed.at[me],
            send_sem=send_sem.at[step],
            recv_sem=recv_sem.at[step],
            device_id={axis_name: peer},
            device_id_type=pl.DeviceIdType.MESH,
        )
        copy.start()
        copies.append(copy)
    landed[me] = source[...] if same else source[me]
    for copy in copies:
        copy.wait()


EXCHANGE_IDS = {}


def exchange(values, axis_name, same):
    count = lax.axis_size(axis_name)
    slot_shape = values.shape if same else values.shape[1:]
    key = (axis_name, same, values.shape, str(values.dtype))
    if key not in EXCHANGE_IDS:
        EXCHANGE_IDS[key] = len(EXCHANGE_IDS)
    slot_bytes = values.dtype.itemsize
    for size in slot_shape:
        slot_bytes *= size
    return pl.pallas_call(
        functools.partial(exchange_kernel, same, axis_name, count),
        out_shape=jax.ShapeDtypeStruct((count,) + slot_shape, values.dtype),
        in_specs=[pl.BlockSpec(memory_space=pltpu.VMEM)],
        out_specs=pl.BlockSpec(memory_space=pltpu.VMEM),
        scratch_shapes=[pltpu.SemaphoreType.DMA((count,)), pltpu.SemaphoreType.DMA((count,))],
        compiler_params=pltpu.CompilerParams(
            collective_id=EXCHANGE_IDS[key], has_side_effects=True
        ),
        cost_estimate=pl.CostEstimate(
            flops=0, bytes_accessed=2 * count * slot_bytes, transcendentals=0
        ),
    )(values)


def context_gather(values, axis_name):
    count = lax.axis_size(axis_name)
    gathered = exchange(values, axis_name, True)
    return gathered.reshape((count * values.shape[0],) + values.shape[1:])


def context_scatter_sum(values, axis_name):
    count = lax.axis_size(axis_name)
    rows = values.shape[0] // count
    parts = exchange(values.reshape((count, rows) + values.shape[1:]), axis_name, False)
    return jnp.sum(parts.astype(jnp.float32), axis=0)


def on_device(
    block_input,
    seq_lengths,
    attn_gain,
    qkv_weight,
    proj_weight,
    mlp_gain,
    gelu_weight,
    down_weight,
    out_cotangent,
):
    row_count = block_input.shape[0]
    feature_count = block_input.shape[1]
    lengths = seq_lengths[0]
    group_rows = row_count * lax.axis_size("context")
    own_first = lax.axis_index("context") * row_count
    own_rows = own_first + jnp.arange(row_count, dtype=jnp.int32)
    own_segment, positions = segments_of(own_rows, lengths)
    cosine, sine_tab = rope_tables(positions, HD)
    shard_rows = qkv_weight.shape[0]
    local_width = qkv_weight.shape[2]
    head_count = local_width // HD
    hidden = gelu_weight.shape[2]
    first_pack = lax.all_gather(
        jnp.concatenate(
            [
                qkv_weight.reshape(shard_rows, 3 * local_width),
                attn_gain[:, None],
                mlp_gain[:, None],
            ],
            axis=1,
        ),
        "fsdp",
        axis=0,
        tiled=True,
    )
    second_pack = lax.all_gather(
        jnp.concatenate(
            [proj_weight.T, gelu_weight.reshape(shard_rows, 2 * hidden), down_weight.T], axis=1
        ),
        "fsdp",
        axis=0,
        tiled=True,
    )
    qkv_flat = first_pack[:, : 3 * local_width]
    attn_full = first_pack[:, 3 * local_width]
    mlp_full = first_pack[:, 3 * local_width + 1]
    proj_t = second_pack[:, :local_width]
    gelu_flat = second_pack[:, local_width : local_width + 2 * hidden]
    down_t = second_pack[:, local_width + 2 * hidden :]
    attn_scale = attn_full.astype(jnp.float32)
    mlp_scale = mlp_full.astype(jnp.float32)
    inputs = block_input.astype(jnp.float32)
    normed_attn, spread_attn = layer_norm(inputs)
    hidden_attn = (normed_attn * attn_scale).astype(jnp.bfloat16)
    projected = jnp.dot(hidden_attn, qkv_flat, preferred_element_type=jnp.float32).reshape(
        row_count, 3, head_count, HD
    )
    query_bf = rotate(projected[:, 0], cosine, sine_tab).astype(jnp.bfloat16)
    key_bf = rotate(projected[:, 1], cosine, sine_tab).astype(jnp.bfloat16)
    value_bf = projected[:, 2].astype(jnp.bfloat16)
    key_flat = key_bf.reshape(row_count, local_width)
    value_flat = value_bf.reshape(row_count, local_width)
    kv_group = context_gather(jnp.concatenate([key_flat, value_flat], axis=1), "context")
    keys_group, values_group = (kv_group[:, :local_width], kv_group[:, local_width:])
    keys_heads = keys_group.reshape(group_rows, head_count, HD)
    values_heads = values_group.reshape(group_rows, head_count, HD)
    group_segment, unused_pos = segments_of(jnp.arange(group_rows, dtype=jnp.int32), lengths)
    same_group = (own_segment[:, None] == group_segment[None, :])[None]
    fwd_scores = (
        jnp.einsum("qhd,khd->hqk", query_bf, keys_heads, preferred_element_type=jnp.float32) * 0.125
    )
    row_max = jnp.max(jnp.where(same_group, fwd_scores, MASKED_LOW), axis=2)
    denom_sum = jnp.sum(
        jnp.where(same_group, jnp.exp(fwd_scores - row_max[:, :, None]), 0.0), axis=2
    )
    log_total = row_max + jnp.log(denom_sum)
    fwd_probs = jnp.where(same_group, jnp.exp(fwd_scores - log_total[:, :, None]), 0.0)
    fwd_weights = fwd_probs.astype(jnp.bfloat16)
    mixed = jnp.einsum(
        "hqk,khd->qhd", fwd_weights, values_heads, preferred_element_type=jnp.float32
    ).astype(jnp.bfloat16)
    mixed_flat = mixed.reshape(row_count, local_width)
    attn_part = jnp.dot(mixed_flat, proj_t.T, preferred_element_type=jnp.float32)
    residual = inputs + pair_sum(attn_part, "tensor")
    normed_mlp, spread_mlp = layer_norm(residual)
    hidden_mlp = (normed_mlp * mlp_scale).astype(jnp.bfloat16)
    gate_up = jnp.dot(hidden_mlp, gelu_flat, preferred_element_type=jnp.float32).reshape(
        row_count, 2, hidden
    )
    gate_pre, up_pre = (gate_up[:, 0], gate_up[:, 1])
    gelu_val, gelu_slope = gelu_parts(gate_pre)
    activ = (gelu_val * up_pre).astype(jnp.bfloat16)
    mlp_part = jnp.dot(activ, down_t.T, preferred_element_type=jnp.float32)
    block_output = (
        residual + pair_sum(mlp_part.astype(jnp.bfloat16), "tensor")
    ).astype(jnp.bfloat16)
    act_grad = jnp.dot(out_cotangent, down_t, preferred_element_type=jnp.float32)
    down_grad_t = jnp.dot(out_cotangent.T, activ, preferred_element_type=jnp.float32)
    gate_up_grad = (
        jnp.stack([act_grad * up_pre * gelu_slope, act_grad * gelu_val], axis=1)
        .astype(jnp.bfloat16)
        .reshape(row_count, 2 * hidden)
    )
    gelu_grad = jnp.dot(hidden_mlp.T, gate_up_grad, preferred_element_type=jnp.float32).reshape(
        feature_count, 2, hidden
    )
    mlp_in_grad = pair_sum(
        jnp.dot(gate_up_grad, gelu_flat.T, preferred_element_type=jnp.float32), "tensor"
    )
    mlpgain_grad = jnp.sum(mlp_in_grad * normed_mlp, axis=0)
    resid_grad = out_cotangent.astype(jnp.float32) + norm_back(
        mlp_in_grad, normed_mlp, spread_mlp, mlp_scale
    )
    resid_bf = resid_grad.astype(jnp.bfloat16)
    out_grad = jnp.dot(resid_bf, proj_t, preferred_element_type=jnp.float32).astype(
        jnp.bfloat16
    )
    proj_grad_t = jnp.dot(resid_bf.T, mixed_flat, preferred_element_type=jnp.float32)
    out_heads = out_grad.reshape(row_count, head_count, HD)
    delta = jnp.transpose(
        jnp.sum(out_heads.astype(jnp.float32) * mixed.astype(jnp.float32), axis=2)
    )

    prob_grad = jnp.einsum(
        "qhd,khd->hqk", out_heads, values_heads, preferred_element_type=jnp.float32
    )
    score_grad = (fwd_probs * (prob_grad - delta[:, :, None])).astype(jnp.bfloat16)
    query_grad = (
        jnp.einsum("hqk,khd->qhd", score_grad, keys_heads, preferred_element_type=jnp.float32)
        * 0.125
    )
    key_all = (
        jnp.einsum("hqk,qhd->khd", score_grad, query_bf, preferred_element_type=jnp.float32)
        * 0.125
    ).reshape(group_rows, local_width)
    value_all = jnp.einsum(
        "hqk,qhd->khd", fwd_weights, out_heads, preferred_element_type=jnp.float32
    ).reshape(group_rows, local_width)
    kv_grad = context_scatter_sum(
        jnp.concatenate([key_all, value_all], axis=1).astype(jnp.bfloat16), "context"
    )
    key_grad, value_grad = (kv_grad[:, :local_width], kv_grad[:, local_width:])
    key_grad = key_grad.reshape(row_count, head_count, HD)
    value_grad = value_grad.reshape(row_count, head_count, HD)
    qkv_rows = (
        jnp.stack(
            [
                rotate_back(query_grad, cosine, sine_tab),
                rotate_back(key_grad, cosine, sine_tab),
                value_grad,
            ],
            axis=1,
        )
        .astype(jnp.bfloat16)
        .reshape(row_count, 3 * local_width)
    )
    qkv_grad = jnp.dot(hidden_attn.T, qkv_rows, preferred_element_type=jnp.float32).reshape(
        feature_count, 3, local_width
    )
    attn_in_grad = pair_sum(
        jnp.dot(qkv_rows, qkv_flat.T, preferred_element_type=jnp.float32).astype(jnp.bfloat16),
        "tensor",
    )
    attngain_grad = jnp.sum(attn_in_grad * normed_attn, axis=0)
    input_grad = resid_grad + norm_back(attn_in_grad, normed_attn, spread_attn, attn_scale)
    def reduce_pack(members):
        packed = jnp.concatenate(members, axis=1).astype(jnp.bfloat16)
        packed = lax.psum_scatter(packed, "fsdp", scatter_dimension=0, tiled=True)
        packed = context_gather(
            context_scatter_sum(packed, "context").astype(jnp.bfloat16), "context"
        ).astype(jnp.float32)
        pieces = []
        start = 0
        for member in members:
            pieces.append(packed[:, start : start + member.shape[1]])
            start += member.shape[1]
        return pieces

    mlp_pieces = reduce_pack(
        [mlpgain_grad[:, None], gelu_grad.reshape(feature_count, 2 * hidden), down_grad_t]
    )
    attn_pieces = reduce_pack(
        [attngain_grad[:, None], qkv_grad.reshape(feature_count, 3 * local_width), proj_grad_t]
    )
    shares = (
        attn_pieces[0][:, 0],
        attn_pieces[1].reshape(shard_rows, 3, local_width),
        attn_pieces[2].T,
        mlp_pieces[0][:, 0],
        mlp_pieces[1].reshape(shard_rows, 2, hidden),
        mlp_pieces[2].T,
    )
    return (
        block_output,
        input_grad,
        shares[0],
        shares[1],
        shares[2],
        shares[3],
        shares[4],
        shares[5],
    )


def solution(mesh):
    in_specs = (
        P(("fsdp", "context"), None),
        P("fsdp", None),
        P("fsdp"),
        P("fsdp", None, "tensor"),
        P("tensor", "fsdp"),
        P("fsdp"),
        P("fsdp", None, "tensor"),
        P("tensor", "fsdp"),
        P(("fsdp", "context"), None),
    )
    out_specs = (
        P(("fsdp", "context"), None),
        P(("fsdp", "context"), None),
        P("fsdp"),
        P("fsdp", None, "tensor"),
        P("tensor", "fsdp"),
        P("fsdp"),
        P("fsdp", None, "tensor"),
        P("tensor", "fsdp"),
    )
    return jax.shard_map(
        on_device, mesh=mesh, in_specs=in_specs, out_specs=out_specs, check_vma=False
    )
```

```python
import functools

import jax
import jax.numpy as jnp
from jax import lax
from jax.experimental import pallas as pl
from jax.experimental.pallas import tpu as pltpu
from jax.sharding import PartitionSpec as P

HD = 64


EPSILON = 1e-05
THETA = 160000.0
MASKED_LOW = -1e30


def layer_norm(values):
    centre = values - jnp.mean(values, axis=-1, keepdims=True)
    spread = lax.rsqrt(jnp.mean(centre * centre, axis=-1, keepdims=True) + EPSILON)
    return (centre * spread, spread)


def norm_back(grad_out, normed, spread, gain):
    scaled = grad_out * gain
    inner = jnp.mean(scaled, axis=-1, keepdims=True) + normed * jnp.mean(
        scaled * normed, axis=-1, keepdims=True
    )
    return spread * (scaled - inner)


def segments_of(row_ids, lengths):
    ends = jnp.cumsum(lengths)
    segment = jnp.sum((row_ids[:, None] >= ends[None, :]).astype(jnp.int32), axis=1)
    starts = ends - lengths
    picked = segment[:, None] == jnp.arange(lengths.shape[0], dtype=jnp.int32)[None, :]
    begin = jnp.sum(jnp.where(picked, starts[None, :], 0), axis=1)
    return (segment, row_ids - begin)


def rope_tables(positions, head_dim):
    half_dim = head_dim // 2
    exponent = jnp.arange(half_dim, dtype=jnp.float32) * (-2.0 / head_dim)
    frequency = jnp.power(jnp.float32(THETA), exponent)
    angles = positions.astype(jnp.float32)[:, None] * frequency[None, :]
    return (jnp.cos(angles)[:, None, :], jnp.sin(angles)[:, None, :])


def rotate(values, cosine, sine_tab):
    half_dim = values.shape[-1] // 2
    lower_half, upper_half = (values[..., :half_dim], values[..., half_dim:])
    return jnp.concatenate(
        [lower_half * cosine - upper_half * sine_tab, upper_half * cosine + lower_half * sine_tab],
        axis=-1,
    )


def rotate_back(grads, cosine, sine_tab):
    half_dim = grads.shape[-1] // 2
    lower_half, upper_half = (grads[..., :half_dim], grads[..., half_dim:])
    return jnp.concatenate(
        [lower_half * cosine + upper_half * sine_tab, upper_half * cosine - lower_half * sine_tab],
        axis=-1,
    )


def gelu_parts(gate_pre):
    normal_cdf = 0.5 * (1.0 + jax.scipy.special.erf(gate_pre * 0.7071067811865476))
    density = jnp.exp(-0.5 * gate_pre * gate_pre) * 0.3989422804014327
    return (gate_pre * normal_cdf, normal_cdf + gate_pre * density)


def pair_kernel(axis_name, source, total, landed, send_sem, recv_sem):
    partner = 1 - lax.axis_index(axis_name)
    barrier = pltpu.get_barrier_semaphore()
    pl.semaphore_signal(
        barrier, inc=1, device_id={axis_name: partner}, device_id_type=pl.DeviceIdType.MESH
    )
    pl.semaphore_wait(barrier, 1)
    copy = pltpu.make_async_remote_copy(
        src_ref=source,
        dst_ref=landed,
        send_sem=send_sem,
        recv_sem=recv_sem,
        device_id={axis_name: partner},
        device_id_type=pl.DeviceIdType.MESH,
    )
    copy.start()
    copy.wait()
    total[...] = source[...].astype(jnp.float32) + landed[...].astype(jnp.float32)


def pair_sum(values, axis_name, call_id):
    if lax.axis_size(axis_name) != 2:
        return lax.psum(values.astype(jnp.float32), axis_name)
    value_bytes = values.dtype.itemsize * values.size
    return pl.pallas_call(
        functools.partial(pair_kernel, axis_name),
        out_shape=jax.ShapeDtypeStruct(values.shape, jnp.float32),
        in_specs=[pl.BlockSpec(memory_space=pltpu.VMEM)],
        out_specs=pl.BlockSpec(memory_space=pltpu.VMEM),
        scratch_shapes=[
            pltpu.VMEM(values.shape, values.dtype),
            pltpu.SemaphoreType.DMA(()),
            pltpu.SemaphoreType.DMA(()),
        ],
        compiler_params=pltpu.CompilerParams(
            collective_id=call_id, has_side_effects=True
        ),
        cost_estimate=pl.CostEstimate(
            flops=values.size, bytes_accessed=3 * value_bytes + 4 * values.size, transcendentals=0
        ),
    )(values)


def context_gather(values, axis_name):
    count = lax.axis_size(axis_name)
    spread = jnp.broadcast_to(values[None], (count,) + values.shape)
    gathered = lax.all_to_all(spread, axis_name, 0, 0, tiled=True)
    return gathered.reshape((count * values.shape[0],) + values.shape[1:])


def context_scatter_sum(values, axis_name):
    count = lax.axis_size(axis_name)
    rows = values.shape[0] // count
    parts = lax.all_to_all(
        values.reshape((count, rows) + values.shape[1:]), axis_name, 0, 0, tiled=True
    )
    return jnp.sum(parts.astype(jnp.float32), axis=0)


def on_device(
    block_input,
    seq_lengths,
    attn_gain,
    qkv_weight,
    proj_weight,
    mlp_gain,
    gelu_weight,
    down_weight,
    out_cotangent,
):
    row_count = block_input.shape[0]
    feature_count = block_input.shape[1]
    lengths = seq_lengths[0]
    group_rows = row_count * lax.axis_size("context")
    own_first = lax.axis_index("context") * row_count
    own_rows = own_first + jnp.arange(row_count, dtype=jnp.int32)
    own_segment, positions = segments_of(own_rows, lengths)
    cosine, sine_tab = rope_tables(positions, HD)
    shard_rows = qkv_weight.shape[0]
    local_width = qkv_weight.shape[2]
    head_count = local_width // HD
    hidden = gelu_weight.shape[2]
    first_pack = lax.all_gather(
        jnp.concatenate(
            [
                qkv_weight.reshape(shard_rows, 3 * local_width),
                attn_gain[:, None],
                mlp_gain[:, None],
            ],
            axis=1,
        ),
        "fsdp",
        axis=0,
        tiled=True,
    )
    second_pack = lax.all_gather(
        jnp.concatenate(
            [proj_weight.T, gelu_weight.reshape(shard_rows, 2 * hidden), down_weight.T], axis=1
        ),
        "fsdp",
        axis=0,
        tiled=True,
    )
    qkv_flat = first_pack[:, : 3 * local_width]
    attn_full = first_pack[:, 3 * local_width]
    mlp_full = first_pack[:, 3 * local_width + 1]
    proj_t = second_pack[:, :local_width]
    gelu_flat = second_pack[:, local_width : local_width + 2 * hidden]
    down_t = second_pack[:, local_width + 2 * hidden :]
    attn_scale = attn_full.astype(jnp.float32)
    mlp_scale = mlp_full.astype(jnp.float32)
    inputs = block_input.astype(jnp.float32)
    normed_attn, spread_attn = layer_norm(inputs)
    hidden_attn = (normed_attn * attn_scale).astype(jnp.bfloat16)
    projected = jnp.dot(hidden_attn, qkv_flat, preferred_element_type=jnp.float32).reshape(
        row_count, 3, head_count, HD
    )
    query_bf = rotate(projected[:, 0], cosine, sine_tab).astype(jnp.bfloat16)
    key_bf = rotate(projected[:, 1], cosine, sine_tab).astype(jnp.bfloat16)
    value_bf = projected[:, 2].astype(jnp.bfloat16)
    key_flat = key_bf.reshape(row_count, local_width)
    value_flat = value_bf.reshape(row_count, local_width)
    kv_group = context_gather(jnp.concatenate([key_flat, value_flat], axis=1), "context")
    keys_group, values_group = (kv_group[:, :local_width], kv_group[:, local_width:])
    keys_heads = keys_group.reshape(group_rows, head_count, HD)
    values_heads = values_group.reshape(group_rows, head_count, HD)
    group_segment, unused_pos = segments_of(jnp.arange(group_rows, dtype=jnp.int32), lengths)
    same_group = (own_segment[:, None] == group_segment[None, :])[None]
    fwd_scores = (
        jnp.einsum("qhd,khd->hqk", query_bf, keys_heads, preferred_element_type=jnp.float32) * 0.125
    )
    row_max = jnp.max(jnp.where(same_group, fwd_scores, MASKED_LOW), axis=2)
    denom_sum = jnp.sum(
        jnp.where(same_group, jnp.exp(fwd_scores - row_max[:, :, None]), 0.0), axis=2
    )
    log_total = row_max + jnp.log(denom_sum)
    fwd_probs = jnp.where(same_group, jnp.exp(fwd_scores - log_total[:, :, None]), 0.0)
    fwd_weights = fwd_probs.astype(jnp.bfloat16)
    mixed = jnp.einsum(
        "hqk,khd->qhd", fwd_weights, values_heads, preferred_element_type=jnp.float32
    ).astype(jnp.bfloat16)
    mixed_flat = mixed.reshape(row_count, local_width)
    attn_part = jnp.dot(mixed_flat, proj_t.T, preferred_element_type=jnp.float32)
    residual = inputs + pair_sum(attn_part, "tensor", 0)
    normed_mlp, spread_mlp = layer_norm(residual)
    hidden_mlp = (normed_mlp * mlp_scale).astype(jnp.bfloat16)
    gate_up = jnp.dot(hidden_mlp, gelu_flat, preferred_element_type=jnp.float32).reshape(
        row_count, 2, hidden
    )
    gate_pre, up_pre = (gate_up[:, 0], gate_up[:, 1])
    gelu_val, gelu_slope = gelu_parts(gate_pre)
    activ = (gelu_val * up_pre).astype(jnp.bfloat16)
    mlp_part = jnp.dot(activ, down_t.T, preferred_element_type=jnp.float32)
    block_output = (
        residual + pair_sum(mlp_part.astype(jnp.bfloat16), "tensor", 1)
    ).astype(jnp.bfloat16)
    act_grad = jnp.dot(out_cotangent, down_t, preferred_element_type=jnp.float32)
    down_grad_t = jnp.dot(out_cotangent.T, activ, preferred_element_type=jnp.float32)
    gate_up_grad = (
        jnp.stack([act_grad * up_pre * gelu_slope, act_grad * gelu_val], axis=1)
        .astype(jnp.bfloat16)
        .reshape(row_count, 2 * hidden)
    )
    gelu_grad = jnp.dot(hidden_mlp.T, gate_up_grad, preferred_element_type=jnp.float32).reshape(
        feature_count, 2, hidden
    )
    mlp_in_grad = pair_sum(
        jnp.dot(gate_up_grad, gelu_flat.T, preferred_element_type=jnp.float32), "tensor", 2
    )
    mlpgain_grad = jnp.sum(mlp_in_grad * normed_mlp, axis=0)
    resid_grad = out_cotangent.astype(jnp.float32) + norm_back(
        mlp_in_grad, normed_mlp, spread_mlp, mlp_scale
    )
    resid_bf = resid_grad.astype(jnp.bfloat16)
    out_grad = jnp.dot(resid_bf, proj_t, preferred_element_type=jnp.float32).astype(
        jnp.bfloat16
    )
    proj_grad_t = jnp.dot(resid_bf.T, mixed_flat, preferred_element_type=jnp.float32)
    out_heads = out_grad.reshape(row_count, head_count, HD)
    delta = jnp.transpose(
        jnp.sum(out_heads.astype(jnp.float32) * mixed.astype(jnp.float32), axis=2)
    )

    prob_grad = jnp.einsum(
        "qhd,khd->hqk", out_heads, values_heads, preferred_element_type=jnp.float32
    )
    score_grad = (fwd_probs * (prob_grad - delta[:, :, None])).astype(jnp.bfloat16)
    query_grad = (
        jnp.einsum("hqk,khd->qhd", score_grad, keys_heads, preferred_element_type=jnp.float32)
        * 0.125
    )
    key_all = (
        jnp.einsum("hqk,qhd->khd", score_grad, query_bf, preferred_element_type=jnp.float32)
        * 0.125
    ).reshape(group_rows, local_width)
    value_all = jnp.einsum(
        "hqk,qhd->khd", fwd_weights, out_heads, preferred_element_type=jnp.float32
    ).reshape(group_rows, local_width)
    kv_grad = context_scatter_sum(
        jnp.concatenate([key_all, value_all], axis=1).astype(jnp.bfloat16), "context"
    )
    key_grad, value_grad = (kv_grad[:, :local_width], kv_grad[:, local_width:])
    key_grad = key_grad.reshape(row_count, head_count, HD)
    value_grad = value_grad.reshape(row_count, head_count, HD)
    qkv_rows = (
        jnp.stack(
            [
                rotate_back(query_grad, cosine, sine_tab),
                rotate_back(key_grad, cosine, sine_tab),
                value_grad,
            ],
            axis=1,
        )
        .astype(jnp.bfloat16)
        .reshape(row_count, 3 * local_width)
    )
    qkv_grad = jnp.dot(hidden_attn.T, qkv_rows, preferred_element_type=jnp.float32).reshape(
        feature_count, 3, local_width
    )
    attn_in_grad = pair_sum(
        jnp.dot(qkv_rows, qkv_flat.T, preferred_element_type=jnp.float32).astype(jnp.bfloat16),
        "tensor",
        3,
    )
    attngain_grad = jnp.sum(attn_in_grad * normed_attn, axis=0)
    input_grad = resid_grad + norm_back(attn_in_grad, normed_attn, spread_attn, attn_scale)
    def reduce_pack(members):
        packed = jnp.concatenate(members, axis=1).astype(jnp.bfloat16)
        packed = lax.psum_scatter(packed, "fsdp", scatter_dimension=0, tiled=True)
        packed = context_gather(
            context_scatter_sum(packed, "context").astype(jnp.bfloat16), "context"
        ).astype(jnp.float32)
        pieces = []
        start = 0
        for member in members:
            pieces.append(packed[:, start : start + member.shape[1]])
            start += member.shape[1]
        return pieces

    mlp_pieces = reduce_pack(
        [mlpgain_grad[:, None], gelu_grad.reshape(feature_count, 2 * hidden), down_grad_t]
    )
    attn_pieces = reduce_pack(
        [attngain_grad[:, None], qkv_grad.reshape(feature_count, 3 * local_width), proj_grad_t]
    )
    shares = (
        attn_pieces[0][:, 0],
        attn_pieces[1].reshape(shard_rows, 3, local_width),
        attn_pieces[2].T,
        mlp_pieces[0][:, 0],
        mlp_pieces[1].reshape(shard_rows, 2, hidden),
        mlp_pieces[2].T,
    )
    return (
        block_output,
        input_grad,
        shares[0],
        shares[1],
        shares[2],
        shares[3],
        shares[4],
        shares[5],
    )


def solution(mesh):
    in_specs = (
        P(("fsdp", "context"), None),
        P("fsdp", None),
        P("fsdp"),
        P("fsdp", None, "tensor"),
        P("tensor", "fsdp"),
        P("fsdp"),
        P("fsdp", None, "tensor"),
        P("tensor", "fsdp"),
        P(("fsdp", "context"), None),
    )
    out_specs = (
        P(("fsdp", "context"), None),
        P(("fsdp", "context"), None),
        P("fsdp"),
        P("fsdp", None, "tensor"),
        P("tensor", "fsdp"),
        P("fsdp"),
        P("fsdp", None, "tensor"),
        P("tensor", "fsdp"),
    )
    return jax.shard_map(
        on_device, mesh=mesh, in_specs=in_specs, out_specs=out_specs, check_vma=False
    )
```

```python
import jax
import jax.numpy as jnp
from jax import lax
from jax.sharding import PartitionSpec as P

HD = 64


EPSILON = 1e-05
THETA = 160000.0
MASKED_LOW = -1e30


def layer_norm(values):
    centre = values - jnp.mean(values, axis=-1, keepdims=True)
    spread = lax.rsqrt(jnp.mean(centre * centre, axis=-1, keepdims=True) + EPSILON)
    return (centre * spread, spread)


def norm_back(grad_out, normed, spread, gain):
    scaled = grad_out * gain
    inner = jnp.mean(scaled, axis=-1, keepdims=True) + normed * jnp.mean(
        scaled * normed, axis=-1, keepdims=True
    )
    return spread * (scaled - inner)


def segments_of(row_ids, lengths):
    ends = jnp.cumsum(lengths)
    segment = jnp.sum((row_ids[:, None] >= ends[None, :]).astype(jnp.int32), axis=1)
    starts = ends - lengths
    picked = segment[:, None] == jnp.arange(lengths.shape[0], dtype=jnp.int32)[None, :]
    begin = jnp.sum(jnp.where(picked, starts[None, :], 0), axis=1)
    return (segment, row_ids - begin)


def rope_tables(positions, head_dim):
    half_dim = head_dim // 2
    exponent = jnp.arange(half_dim, dtype=jnp.float32) * (-2.0 / head_dim)
    frequency = jnp.power(jnp.float32(THETA), exponent)
    angles = positions.astype(jnp.float32)[:, None] * frequency[None, :]
    return (jnp.cos(angles)[:, None, :], jnp.sin(angles)[:, None, :])


def rotate(values, cosine, sine_tab):
    half_dim = values.shape[-1] // 2
    lower_half, upper_half = (values[..., :half_dim], values[..., half_dim:])
    return jnp.concatenate(
        [lower_half * cosine - upper_half * sine_tab, upper_half * cosine + lower_half * sine_tab],
        axis=-1,
    )


def rotate_back(grads, cosine, sine_tab):
    half_dim = grads.shape[-1] // 2
    lower_half, upper_half = (grads[..., :half_dim], grads[..., half_dim:])
    return jnp.concatenate(
        [lower_half * cosine + upper_half * sine_tab, upper_half * cosine - lower_half * sine_tab],
        axis=-1,
    )


def gelu_parts(gate_pre):
    normal_cdf = 0.5 * (1.0 + jax.scipy.special.erf(gate_pre * 0.7071067811865476))
    density = jnp.exp(-0.5 * gate_pre * gate_pre) * 0.3989422804014327
    return (gate_pre * normal_cdf, normal_cdf + gate_pre * density)


def pair_sum(values, axis_name):
    if lax.axis_size(axis_name) != 2:
        return lax.psum(values, axis_name)
    other = lax.ppermute(values, axis_name, perm=[(0, 1), (1, 0)])
    return values.astype(jnp.float32) + other.astype(jnp.float32)


def context_gather(values, axis_name):
    count = lax.axis_size(axis_name)
    spread = jnp.broadcast_to(values[None], (count,) + values.shape)
    gathered = lax.all_to_all(spread, axis_name, 0, 0, tiled=True)
    return gathered.reshape((count * values.shape[0],) + values.shape[1:])


def context_scatter_sum(values, axis_name):
    count = lax.axis_size(axis_name)
    rows = values.shape[0] // count
    parts = lax.all_to_all(
        values.reshape((count, rows) + values.shape[1:]), axis_name, 0, 0, tiled=True
    )
    return jnp.sum(parts.astype(jnp.float32), axis=0)


def on_device(
    block_input,
    seq_lengths,
    attn_gain,
    qkv_weight,
    proj_weight,
    mlp_gain,
    gelu_weight,
    down_weight,
    out_cotangent,
):
    row_count = block_input.shape[0]
    feature_count = block_input.shape[1]
    lengths = seq_lengths[0]
    group_rows = row_count * lax.axis_size("context")
    own_first = lax.axis_index("context") * row_count
    own_rows = own_first + jnp.arange(row_count, dtype=jnp.int32)
    own_segment, positions = segments_of(own_rows, lengths)
    cosine, sine_tab = rope_tables(positions, HD)
    shard_rows = qkv_weight.shape[0]
    local_width = qkv_weight.shape[2]
    head_count = local_width // HD
    hidden = gelu_weight.shape[2]
    first_pack = lax.all_gather(
        jnp.concatenate(
            [
                qkv_weight.reshape(shard_rows, 3 * local_width),
                attn_gain[:, None],
                mlp_gain[:, None],
            ],
            axis=1,
        ),
        "fsdp",
        axis=0,
        tiled=True,
    )
    second_pack = lax.all_gather(
        jnp.concatenate(
            [proj_weight.T, gelu_weight.reshape(shard_rows, 2 * hidden), down_weight.T], axis=1
        ),
        "fsdp",
        axis=0,
        tiled=True,
    )
    qkv_flat = first_pack[:, : 3 * local_width]
    attn_full = first_pack[:, 3 * local_width]
    mlp_full = first_pack[:, 3 * local_width + 1]
    proj_t = second_pack[:, :local_width]
    gelu_flat = second_pack[:, local_width : local_width + 2 * hidden]
    down_t = second_pack[:, local_width + 2 * hidden :]
    attn_scale = attn_full.astype(jnp.float32)
    mlp_scale = mlp_full.astype(jnp.float32)
    inputs = block_input.astype(jnp.float32)
    normed_attn, spread_attn = layer_norm(inputs)
    hidden_attn = (normed_attn * attn_scale).astype(jnp.bfloat16)
    projected = jnp.dot(hidden_attn, qkv_flat, preferred_element_type=jnp.float32).reshape(
        row_count, 3, head_count, HD
    )
    query_bf = rotate(projected[:, 0], cosine, sine_tab).astype(jnp.bfloat16)
    key_bf = rotate(projected[:, 1], cosine, sine_tab).astype(jnp.bfloat16)
    value_bf = projected[:, 2].astype(jnp.bfloat16)
    key_flat = key_bf.reshape(row_count, local_width)
    value_flat = value_bf.reshape(row_count, local_width)
    kv_group = context_gather(jnp.concatenate([key_flat, value_flat], axis=1), "context")
    keys_group, values_group = (kv_group[:, :local_width], kv_group[:, local_width:])
    keys_heads = keys_group.reshape(group_rows, head_count, HD)
    values_heads = values_group.reshape(group_rows, head_count, HD)
    group_segment, unused_pos = segments_of(jnp.arange(group_rows, dtype=jnp.int32), lengths)
    same_group = (own_segment[:, None] == group_segment[None, :])[None]
    fwd_scores = (
        jnp.einsum("qhd,khd->hqk", query_bf, keys_heads, preferred_element_type=jnp.float32) * 0.125
    )
    row_max = jnp.max(jnp.where(same_group, fwd_scores, MASKED_LOW), axis=2)
    denom_sum = jnp.sum(
        jnp.where(same_group, jnp.exp(fwd_scores - row_max[:, :, None]), 0.0), axis=2
    )
    log_total = row_max + jnp.log(denom_sum)
    fwd_probs = jnp.where(same_group, jnp.exp(fwd_scores - log_total[:, :, None]), 0.0)
    fwd_weights = fwd_probs.astype(jnp.bfloat16)
    mixed = jnp.einsum(
        "hqk,khd->qhd", fwd_weights, values_heads, preferred_element_type=jnp.float32
    ).astype(jnp.bfloat16)
    mixed_flat = mixed.reshape(row_count, local_width)
    attn_part = jnp.dot(mixed_flat, proj_t.T, preferred_element_type=jnp.float32)
    residual = inputs + pair_sum(attn_part.astype(jnp.bfloat16), "tensor")
    normed_mlp, spread_mlp = layer_norm(residual)
    hidden_mlp = (normed_mlp * mlp_scale).astype(jnp.bfloat16)
    gate_up = jnp.dot(hidden_mlp, gelu_flat, preferred_element_type=jnp.float32).reshape(
        row_count, 2, hidden
    )
    gate_pre, up_pre = (gate_up[:, 0], gate_up[:, 1])
    gelu_val, gelu_slope = gelu_parts(gate_pre)
    activ = (gelu_val * up_pre).astype(jnp.bfloat16)
    mlp_part = jnp.dot(activ, down_t.T, preferred_element_type=jnp.float32)
    block_output = (
        residual + pair_sum(mlp_part.astype(jnp.bfloat16), "tensor")
    ).astype(jnp.bfloat16)
    act_grad = jnp.dot(out_cotangent, down_t, preferred_element_type=jnp.float32)
    down_grad_t = jnp.dot(out_cotangent.T, activ, preferred_element_type=jnp.float32)
    gate_up_grad = (
        jnp.stack([act_grad * up_pre * gelu_slope, act_grad * gelu_val], axis=1)
        .astype(jnp.bfloat16)
        .reshape(row_count, 2 * hidden)
    )
    gelu_grad = jnp.dot(hidden_mlp.T, gate_up_grad, preferred_element_type=jnp.float32).reshape(
        feature_count, 2, hidden
    )
    mlp_in_grad = pair_sum(
        jnp.dot(gate_up_grad, gelu_flat.T, preferred_element_type=jnp.float32).astype(
            jnp.bfloat16
        ),
        "tensor",
    )
    mlpgain_grad = jnp.sum(mlp_in_grad * normed_mlp, axis=0)
    resid_grad = out_cotangent.astype(jnp.float32) + norm_back(
        mlp_in_grad, normed_mlp, spread_mlp, mlp_scale
    )
    resid_bf = resid_grad.astype(jnp.bfloat16)
    out_grad = jnp.dot(resid_bf, proj_t, preferred_element_type=jnp.float32).astype(
        jnp.bfloat16
    )
    proj_grad_t = jnp.dot(resid_bf.T, mixed_flat, preferred_element_type=jnp.float32)
    out_heads = out_grad.reshape(row_count, head_count, HD)
    delta = jnp.transpose(
        jnp.sum(out_heads.astype(jnp.float32) * mixed.astype(jnp.float32), axis=2)
    )

    prob_grad = jnp.einsum(
        "qhd,khd->hqk", out_heads, values_heads, preferred_element_type=jnp.float32
    )
    score_grad = (fwd_probs * (prob_grad - delta[:, :, None])).astype(jnp.bfloat16)
    query_grad = (
        jnp.einsum("hqk,khd->qhd", score_grad, keys_heads, preferred_element_type=jnp.float32)
        * 0.125
    )
    key_all = (
        jnp.einsum("hqk,qhd->khd", score_grad, query_bf, preferred_element_type=jnp.float32)
        * 0.125
    ).reshape(group_rows, local_width)
    value_all = jnp.einsum(
        "hqk,qhd->khd", fwd_weights, out_heads, preferred_element_type=jnp.float32
    ).reshape(group_rows, local_width)
    kv_grad = context_scatter_sum(
        jnp.concatenate([key_all, value_all], axis=1).astype(jnp.bfloat16), "context"
    )
    key_grad, value_grad = (kv_grad[:, :local_width], kv_grad[:, local_width:])
    key_grad = key_grad.reshape(row_count, head_count, HD)
    value_grad = value_grad.reshape(row_count, head_count, HD)
    qkv_rows = (
        jnp.stack(
            [
                rotate_back(query_grad, cosine, sine_tab),
                rotate_back(key_grad, cosine, sine_tab),
                value_grad,
            ],
            axis=1,
        )
        .astype(jnp.bfloat16)
        .reshape(row_count, 3 * local_width)
    )
    qkv_grad = jnp.dot(hidden_attn.T, qkv_rows, preferred_element_type=jnp.float32).reshape(
        feature_count, 3, local_width
    )
    attn_in_grad = pair_sum(
        jnp.dot(qkv_rows, qkv_flat.T, preferred_element_type=jnp.float32).astype(jnp.bfloat16),
        "tensor",
    )
    attngain_grad = jnp.sum(attn_in_grad * normed_attn, axis=0)
    input_grad = resid_grad + norm_back(attn_in_grad, normed_attn, spread_attn, attn_scale)
    def reduce_pack(members):
        packed = jnp.concatenate(members, axis=1).astype(jnp.bfloat16)
        packed = lax.psum_scatter(packed, "fsdp", scatter_dimension=0, tiled=True)
        packed = context_gather(
            context_scatter_sum(packed, "context").astype(jnp.bfloat16), "context"
        ).astype(jnp.float32)
        pieces = []
        start = 0
        for member in members:
            pieces.append(packed[:, start : start + member.shape[1]])
            start += member.shape[1]
        return pieces

    mlp_pieces = reduce_pack(
        [
            mlpgain_grad[:, None],
            gelu_grad.reshape(feature_count, 2 * hidden),
            down_grad_t,
            proj_grad_t,
        ]
    )
    attn_pieces = reduce_pack(
        [attngain_grad[:, None], qkv_grad.reshape(feature_count, 3 * local_width)]
    )
    shares = (
        attn_pieces[0][:, 0],
        attn_pieces[1].reshape(shard_rows, 3, local_width),
        mlp_pieces[3].T,
        mlp_pieces[0][:, 0],
        mlp_pieces[1].reshape(shard_rows, 2, hidden),
        mlp_pieces[2].T,
    )
    return (
        block_output,
        input_grad,
        shares[0],
        shares[1],
        shares[2],
        shares[3],
        shares[4],
        shares[5],
    )


def solution(mesh):
    in_specs = (
        P(("fsdp", "context"), None),
        P("fsdp", None),
        P("fsdp"),
        P("fsdp", None, "tensor"),
        P("tensor", "fsdp"),
        P("fsdp"),
        P("fsdp", None, "tensor"),
        P("tensor", "fsdp"),
        P(("fsdp", "context"), None),
    )
    out_specs = (
        P(("fsdp", "context"), None),
        P(("fsdp", "context"), None),
        P("fsdp"),
        P("fsdp", None, "tensor"),
        P("tensor", "fsdp"),
        P("fsdp"),
        P("fsdp", None, "tensor"),
        P("tensor", "fsdp"),
    )
    return jax.shard_map(
        on_device, mesh=mesh, in_specs=in_specs, out_specs=out_specs, check_vma=False
    )
```

```python
import jax
import jax.numpy as jnp
from jax import lax
from jax.sharding import PartitionSpec as P

HD = 64


EPSILON = 1e-05
THETA = 160000.0
MASKED_LOW = -1e30


def layer_norm(values):
    centre = values - jnp.mean(values, axis=-1, keepdims=True)
    spread = lax.rsqrt(jnp.mean(centre * centre, axis=-1, keepdims=True) + EPSILON)
    return (centre * spread, spread)


def norm_back(grad_out, normed, spread, gain):
    scaled = grad_out * gain
    inner = jnp.mean(scaled, axis=-1, keepdims=True) + normed * jnp.mean(
        scaled * normed, axis=-1, keepdims=True
    )
    return spread * (scaled - inner)


def segments_of(row_ids, lengths):
    ends = jnp.cumsum(lengths)
    segment = jnp.sum((row_ids[:, None] >= ends[None, :]).astype(jnp.int32), axis=1)
    starts = ends - lengths
    picked = segment[:, None] == jnp.arange(lengths.shape[0], dtype=jnp.int32)[None, :]
    begin = jnp.sum(jnp.where(picked, starts[None, :], 0), axis=1)
    return (segment, row_ids - begin)


def rope_tables(positions, head_dim):
    half_dim = head_dim // 2
    exponent = jnp.arange(half_dim, dtype=jnp.float32) * (-2.0 / head_dim)
    frequency = jnp.power(jnp.float32(THETA), exponent)
    angles = positions.astype(jnp.float32)[:, None] * frequency[None, :]
    return (jnp.cos(angles)[:, None, :], jnp.sin(angles)[:, None, :])


def rotate(values, cosine, sine_tab):
    half_dim = values.shape[-1] // 2
    lower_half, upper_half = (values[..., :half_dim], values[..., half_dim:])
    return jnp.concatenate(
        [lower_half * cosine - upper_half * sine_tab, upper_half * cosine + lower_half * sine_tab],
        axis=-1,
    )


def rotate_back(grads, cosine, sine_tab):
    half_dim = grads.shape[-1] // 2
    lower_half, upper_half = (grads[..., :half_dim], grads[..., half_dim:])
    return jnp.concatenate(
        [lower_half * cosine + upper_half * sine_tab, upper_half * cosine - lower_half * sine_tab],
        axis=-1,
    )


def gelu_parts(gate_pre):
    normal_cdf = 0.5 * (1.0 + jax.scipy.special.erf(gate_pre * 0.7071067811865476))
    density = jnp.exp(-0.5 * gate_pre * gate_pre) * 0.3989422804014327
    return (gate_pre * normal_cdf, normal_cdf + gate_pre * density)


def pair_sum(values, axis_name):
    if lax.axis_size(axis_name) != 2:
        return lax.psum(values, axis_name)
    other = lax.ppermute(values, axis_name, perm=[(0, 1), (1, 0)])
    return values.astype(jnp.float32) + other.astype(jnp.float32)


def context_gather(values, axis_name):
    count = lax.axis_size(axis_name)
    spread = jnp.broadcast_to(values[None], (count,) + values.shape)
    gathered = lax.all_to_all(spread, axis_name, 0, 0, tiled=True)
    return gathered.reshape((count * values.shape[0],) + values.shape[1:])


def context_scatter_sum(values, axis_name):
    count = lax.axis_size(axis_name)
    rows = values.shape[0] // count
    parts = lax.all_to_all(
        values.reshape((count, rows) + values.shape[1:]), axis_name, 0, 0, tiled=True
    )
    return jnp.sum(parts.astype(jnp.float32), axis=0)


def on_device(
    block_input,
    seq_lengths,
    attn_gain,
    qkv_weight,
    proj_weight,
    mlp_gain,
    gelu_weight,
    down_weight,
    out_cotangent,
):
    row_count = block_input.shape[0]
    feature_count = block_input.shape[1]
    lengths = seq_lengths[0]
    group_rows = row_count * lax.axis_size("context")
    own_first = lax.axis_index("context") * row_count
    own_rows = own_first + jnp.arange(row_count, dtype=jnp.int32)
    own_segment, positions = segments_of(own_rows, lengths)
    cosine, sine_tab = rope_tables(positions, HD)
    shard_rows = qkv_weight.shape[0]
    local_width = qkv_weight.shape[2]
    head_count = local_width // HD
    hidden = gelu_weight.shape[2]
    first_pack = lax.all_gather(
        jnp.concatenate(
            [
                qkv_weight.reshape(shard_rows, 3 * local_width),
                attn_gain[:, None],
                mlp_gain[:, None],
            ],
            axis=1,
        ),
        "fsdp",
        axis=0,
        tiled=True,
    )
    second_pack = lax.all_gather(
        jnp.concatenate(
            [proj_weight.T, gelu_weight.reshape(shard_rows, 2 * hidden), down_weight.T], axis=1
        ),
        "fsdp",
        axis=0,
        tiled=True,
    )
    qkv_flat = first_pack[:, : 3 * local_width]
    attn_full = first_pack[:, 3 * local_width]
    mlp_full = first_pack[:, 3 * local_width + 1]
    proj_t = second_pack[:, :local_width]
    gelu_flat = second_pack[:, local_width : local_width + 2 * hidden]
    down_t = second_pack[:, local_width + 2 * hidden :]
    attn_scale = attn_full.astype(jnp.float32)
    mlp_scale = mlp_full.astype(jnp.float32)
    inputs = block_input.astype(jnp.float32)
    normed_attn, spread_attn = layer_norm(inputs)
    hidden_attn = (normed_attn * attn_scale).astype(jnp.bfloat16)
    projected = jnp.dot(hidden_attn, qkv_flat, preferred_element_type=jnp.float32).reshape(
        row_count, 3, head_count, HD
    )
    query_bf = rotate(projected[:, 0], cosine, sine_tab).astype(jnp.bfloat16)
    key_bf = rotate(projected[:, 1], cosine, sine_tab).astype(jnp.bfloat16)
    value_bf = projected[:, 2].astype(jnp.bfloat16)
    key_flat = key_bf.reshape(row_count, local_width)
    value_flat = value_bf.reshape(row_count, local_width)
    kv_group = context_gather(jnp.concatenate([key_flat, value_flat], axis=1), "context")
    keys_group, values_group = (kv_group[:, :local_width], kv_group[:, local_width:])
    keys_heads = keys_group.reshape(group_rows, head_count, HD)
    values_heads = values_group.reshape(group_rows, head_count, HD)
    group_segment, unused_pos = segments_of(jnp.arange(group_rows, dtype=jnp.int32), lengths)
    same_group = (own_segment[:, None] == group_segment[None, :])[None]
    fwd_scores = (
        jnp.einsum("qhd,khd->hqk", query_bf, keys_heads, preferred_element_type=jnp.float32) * 0.125
    )
    row_max = jnp.max(jnp.where(same_group, fwd_scores, MASKED_LOW), axis=2)
    denom_sum = jnp.sum(
        jnp.where(same_group, jnp.exp(fwd_scores - row_max[:, :, None]), 0.0), axis=2
    )
    log_total = row_max + jnp.log(denom_sum)
    fwd_probs = jnp.where(same_group, jnp.exp(fwd_scores - log_total[:, :, None]), 0.0)
    fwd_weights = fwd_probs.astype(jnp.bfloat16)
    mixed = jnp.einsum(
        "hqk,khd->qhd", fwd_weights, values_heads, preferred_element_type=jnp.float32
    ).astype(jnp.bfloat16)
    mixed_flat = mixed.reshape(row_count, local_width)
    attn_part = jnp.dot(mixed_flat, proj_t.T, preferred_element_type=jnp.float32)
    residual = inputs + pair_sum(attn_part.astype(jnp.bfloat16), "tensor")
    normed_mlp, spread_mlp = layer_norm(residual)
    hidden_mlp = (normed_mlp * mlp_scale).astype(jnp.bfloat16)
    gate_up = jnp.dot(hidden_mlp, gelu_flat, preferred_element_type=jnp.float32).reshape(
        row_count, 2, hidden
    )
    gate_pre, up_pre = (gate_up[:, 0], gate_up[:, 1])
    gelu_val, gelu_slope = gelu_parts(gate_pre)
    activ = (gelu_val * up_pre).astype(jnp.bfloat16)
    mlp_part = jnp.dot(activ, down_t.T, preferred_element_type=jnp.float32)
    block_output = (
        residual + pair_sum(mlp_part.astype(jnp.bfloat16), "tensor")
    ).astype(jnp.bfloat16)
    act_grad = jnp.dot(out_cotangent, down_t, preferred_element_type=jnp.float32)
    down_grad_t = jnp.dot(out_cotangent.T, activ, preferred_element_type=jnp.float32)
    gate_up_grad = (
        jnp.stack([act_grad * up_pre * gelu_slope, act_grad * gelu_val], axis=1)
        .astype(jnp.bfloat16)
        .reshape(row_count, 2 * hidden)
    )
    gelu_grad = jnp.dot(hidden_mlp.T, gate_up_grad, preferred_element_type=jnp.float32).reshape(
        feature_count, 2, hidden
    )
    mlp_in_grad = pair_sum(
        jnp.dot(gate_up_grad, gelu_flat.T, preferred_element_type=jnp.float32).astype(
            jnp.bfloat16
        ),
        "tensor",
    )
    mlpgain_grad = jnp.sum(mlp_in_grad * normed_mlp, axis=0)
    resid_grad = out_cotangent.astype(jnp.float32) + norm_back(
        mlp_in_grad, normed_mlp, spread_mlp, mlp_scale
    )
    resid_bf = resid_grad.astype(jnp.bfloat16)
    out_grad = jnp.dot(resid_bf, proj_t, preferred_element_type=jnp.float32).astype(
        jnp.bfloat16
    )
    proj_grad_t = jnp.dot(resid_bf.T, mixed_flat, preferred_element_type=jnp.float32)

    def reduce_pack(packed, members):
        packed = context_gather(
            context_scatter_sum(packed, "context").astype(jnp.bfloat16), "context"
        ).astype(jnp.float32)
        pieces = []
        start = 0
        for member in members:
            pieces.append(packed[:, start : start + member.shape[1]])
            start += member.shape[1]
        return pieces

    mlp_members = [
        mlpgain_grad[:, None],
        gelu_grad.reshape(feature_count, 2 * hidden),
        down_grad_t,
        proj_grad_t,
    ]
    mlp_packed, out_grad = lax.optimization_barrier(
        (jnp.concatenate(mlp_members, axis=1).astype(jnp.bfloat16), out_grad)
    )
    mlp_shard = lax.psum_scatter(mlp_packed, "fsdp", scatter_dimension=0, tiled=True)
    out_heads = out_grad.reshape(row_count, head_count, HD)
    delta = jnp.transpose(
        jnp.sum(out_heads.astype(jnp.float32) * mixed.astype(jnp.float32), axis=2)
    )

    prob_grad = jnp.einsum(
        "qhd,khd->hqk", out_heads, values_heads, preferred_element_type=jnp.float32
    )
    score_grad = (fwd_probs * (prob_grad - delta[:, :, None])).astype(jnp.bfloat16)
    query_grad = (
        jnp.einsum("hqk,khd->qhd", score_grad, keys_heads, preferred_element_type=jnp.float32)
        * 0.125
    )
    key_all = (
        jnp.einsum("hqk,qhd->khd", score_grad, query_bf, preferred_element_type=jnp.float32)
        * 0.125
    ).reshape(group_rows, local_width)
    value_all = jnp.einsum(
        "hqk,qhd->khd", fwd_weights, out_heads, preferred_element_type=jnp.float32
    ).reshape(group_rows, local_width)
    kv_partial, mlp_shard = lax.optimization_barrier(
        (jnp.concatenate([key_all, value_all], axis=1).astype(jnp.bfloat16), mlp_shard)
    )
    kv_grad = context_scatter_sum(kv_partial, "context")
    mlp_pieces = reduce_pack(mlp_shard, mlp_members)
    key_grad, value_grad = (kv_grad[:, :local_width], kv_grad[:, local_width:])
    key_grad = key_grad.reshape(row_count, head_count, HD)
    value_grad = value_grad.reshape(row_count, head_count, HD)
    qkv_rows = (
        jnp.stack(
            [
                rotate_back(query_grad, cosine, sine_tab),
                rotate_back(key_grad, cosine, sine_tab),
                value_grad,
            ],
            axis=1,
        )
        .astype(jnp.bfloat16)
        .reshape(row_count, 3 * local_width)
    )
    qkv_grad = jnp.dot(hidden_attn.T, qkv_rows, preferred_element_type=jnp.float32).reshape(
        feature_count, 3, local_width
    )
    attn_in_grad = pair_sum(
        jnp.dot(qkv_rows, qkv_flat.T, preferred_element_type=jnp.float32).astype(jnp.bfloat16),
        "tensor",
    )
    attngain_grad = jnp.sum(attn_in_grad * normed_attn, axis=0)
    input_grad = resid_grad + norm_back(attn_in_grad, normed_attn, spread_attn, attn_scale)
    attn_members = [attngain_grad[:, None], qkv_grad.reshape(feature_count, 3 * local_width)]
    attn_pieces = reduce_pack(
        lax.psum_scatter(
            jnp.concatenate(attn_members, axis=1).astype(jnp.bfloat16),
            "fsdp",
            scatter_dimension=0,
            tiled=True,
        ),
        attn_members,
    )
    shares = (
        attn_pieces[0][:, 0],
        attn_pieces[1].reshape(shard_rows, 3, local_width),
        mlp_pieces[3].T,
        mlp_pieces[0][:, 0],
        mlp_pieces[1].reshape(shard_rows, 2, hidden),
        mlp_pieces[2].T,
    )
    return (
        block_output,
        input_grad,
        shares[0],
        shares[1],
        shares[2],
        shares[3],
        shares[4],
        shares[5],
    )


def solution(mesh):
    in_specs = (
        P(("fsdp", "context"), None),
        P("fsdp", None),
        P("fsdp"),
        P("fsdp", None, "tensor"),
        P("tensor", "fsdp"),
        P("fsdp"),
        P("fsdp", None, "tensor"),
        P("tensor", "fsdp"),
        P(("fsdp", "context"), None),
    )
    out_specs = (
        P(("fsdp", "context"), None),
        P(("fsdp", "context"), None),
        P("fsdp"),
        P("fsdp", None, "tensor"),
        P("tensor", "fsdp"),
        P("fsdp"),
        P("fsdp", None, "tensor"),
        P("tensor", "fsdp"),
    )
    return jax.shard_map(
        on_device, mesh=mesh, in_specs=in_specs, out_specs=out_specs, check_vma=False
    )
```

```python
import jax
import jax.numpy as jnp
from jax import lax
from jax.sharding import PartitionSpec as P

HD = 64


EPSILON = 1e-05
THETA = 160000.0
MASKED_LOW = -1e30


def layer_norm(values):
    centre = values - jnp.mean(values, axis=-1, keepdims=True)
    spread = lax.rsqrt(jnp.mean(centre * centre, axis=-1, keepdims=True) + EPSILON)
    return (centre * spread, spread)


def norm_back(grad_out, normed, spread, gain):
    scaled = grad_out * gain
    inner = jnp.mean(scaled, axis=-1, keepdims=True) + normed * jnp.mean(
        scaled * normed, axis=-1, keepdims=True
    )
    return spread * (scaled - inner)


def segments_of(row_ids, lengths):
    ends = jnp.cumsum(lengths)
    segment = jnp.sum((row_ids[:, None] >= ends[None, :]).astype(jnp.int32), axis=1)
    starts = ends - lengths
    picked = segment[:, None] == jnp.arange(lengths.shape[0], dtype=jnp.int32)[None, :]
    begin = jnp.sum(jnp.where(picked, starts[None, :], 0), axis=1)
    return (segment, row_ids - begin)


def rope_tables(positions, head_dim):
    half_dim = head_dim // 2
    exponent = jnp.arange(half_dim, dtype=jnp.float32) * (-2.0 / head_dim)
    frequency = jnp.power(jnp.float32(THETA), exponent)
    angles = positions.astype(jnp.float32)[:, None] * frequency[None, :]
    return (jnp.cos(angles)[:, None, :], jnp.sin(angles)[:, None, :])


def rotate(values, cosine, sine_tab):
    half_dim = values.shape[-1] // 2
    lower_half, upper_half = (values[..., :half_dim], values[..., half_dim:])
    return jnp.concatenate(
        [lower_half * cosine - upper_half * sine_tab, upper_half * cosine + lower_half * sine_tab],
        axis=-1,
    )


def rotate_back(grads, cosine, sine_tab):
    half_dim = grads.shape[-1] // 2
    lower_half, upper_half = (grads[..., :half_dim], grads[..., half_dim:])
    return jnp.concatenate(
        [lower_half * cosine + upper_half * sine_tab, upper_half * cosine - lower_half * sine_tab],
        axis=-1,
    )


def gelu_parts(gate_pre):
    normal_cdf = 0.5 * (1.0 + jax.scipy.special.erf(gate_pre * 0.7071067811865476))
    density = jnp.exp(-0.5 * gate_pre * gate_pre) * 0.3989422804014327
    return (gate_pre * normal_cdf, normal_cdf + gate_pre * density)


def pair_sum(values, axis_name):
    if lax.axis_size(axis_name) != 2:
        return lax.psum(values, axis_name)
    other = lax.ppermute(values, axis_name, perm=[(0, 1), (1, 0)])
    return values.astype(jnp.float32) + other.astype(jnp.float32)


def context_gather(values, axis_name):
    count = lax.axis_size(axis_name)
    spread = jnp.broadcast_to(values[None], (count,) + values.shape)
    gathered = lax.all_to_all(spread, axis_name, 0, 0, tiled=True)
    return gathered.reshape((count * values.shape[0],) + values.shape[1:])


def context_scatter_sum(values, axis_name):
    count = lax.axis_size(axis_name)
    rows = values.shape[0] // count
    parts = lax.all_to_all(
        values.reshape((count, rows) + values.shape[1:]), axis_name, 0, 0, tiled=True
    )
    return jnp.sum(parts.astype(jnp.float32), axis=0)


def on_device(
    block_input,
    seq_lengths,
    attn_gain,
    qkv_weight,
    proj_weight,
    mlp_gain,
    gelu_weight,
    down_weight,
    out_cotangent,
):
    row_count = block_input.shape[0]
    feature_count = block_input.shape[1]
    lengths = seq_lengths[0]
    group_rows = row_count * lax.axis_size("context")
    own_first = lax.axis_index("context") * row_count
    own_rows = own_first + jnp.arange(row_count, dtype=jnp.int32)
    own_segment, positions = segments_of(own_rows, lengths)
    cosine, sine_tab = rope_tables(positions, HD)
    shard_rows = qkv_weight.shape[0]
    local_width = qkv_weight.shape[2]
    head_count = local_width // HD
    hidden = gelu_weight.shape[2]
    first_pack = lax.all_gather(
        jnp.concatenate(
            [
                qkv_weight.reshape(shard_rows, 3 * local_width),
                attn_gain[:, None],
                mlp_gain[:, None],
            ],
            axis=1,
        ),
        "fsdp",
        axis=0,
        tiled=True,
    )
    second_pack = lax.all_gather(
        jnp.concatenate(
            [proj_weight.T, gelu_weight.reshape(shard_rows, 2 * hidden), down_weight.T], axis=1
        ),
        "fsdp",
        axis=0,
        tiled=True,
    )
    qkv_flat = first_pack[:, : 3 * local_width]
    attn_full = first_pack[:, 3 * local_width]
    mlp_full = first_pack[:, 3 * local_width + 1]
    proj_t = second_pack[:, :local_width]
    gelu_flat = second_pack[:, local_width : local_width + 2 * hidden]
    down_t = second_pack[:, local_width + 2 * hidden :]
    attn_scale = attn_full.astype(jnp.float32)
    mlp_scale = mlp_full.astype(jnp.float32)
    inputs = block_input.astype(jnp.float32)
    normed_attn, spread_attn = layer_norm(inputs)
    hidden_attn = (normed_attn * attn_scale).astype(jnp.bfloat16)
    projected = jnp.dot(hidden_attn, qkv_flat, preferred_element_type=jnp.float32).reshape(
        row_count, 3, head_count, HD
    )
    query_bf = rotate(projected[:, 0], cosine, sine_tab).astype(jnp.bfloat16)
    key_bf = rotate(projected[:, 1], cosine, sine_tab).astype(jnp.bfloat16)
    value_bf = projected[:, 2].astype(jnp.bfloat16)
    key_flat = key_bf.reshape(row_count, local_width)
    value_flat = value_bf.reshape(row_count, local_width)
    keys_group = context_gather(key_flat, "context")
    values_group = context_gather(value_flat, "context")
    keys_heads = keys_group.reshape(group_rows, head_count, HD)
    values_heads = values_group.reshape(group_rows, head_count, HD)
    group_segment, unused_pos = segments_of(jnp.arange(group_rows, dtype=jnp.int32), lengths)
    same_group = (own_segment[:, None] == group_segment[None, :])[None]
    fwd_scores = (
        jnp.einsum("qhd,khd->hqk", query_bf, keys_heads, preferred_element_type=jnp.float32) * 0.125
    )
    row_max = jnp.max(jnp.where(same_group, fwd_scores, MASKED_LOW), axis=2)
    denom_sum = jnp.sum(
        jnp.where(same_group, jnp.exp(fwd_scores - row_max[:, :, None]), 0.0), axis=2
    )
    log_total = row_max + jnp.log(denom_sum)
    fwd_probs = jnp.where(same_group, jnp.exp(fwd_scores - log_total[:, :, None]), 0.0)
    fwd_weights = fwd_probs.astype(jnp.bfloat16)
    mixed = jnp.einsum(
        "hqk,khd->qhd", fwd_weights, values_heads, preferred_element_type=jnp.float32
    ).astype(jnp.bfloat16)
    mixed_flat = mixed.reshape(row_count, local_width)
    attn_part = jnp.dot(mixed_flat, proj_t.T, preferred_element_type=jnp.float32)
    residual = inputs + pair_sum(attn_part.astype(jnp.bfloat16), "tensor")
    normed_mlp, spread_mlp = layer_norm(residual)
    hidden_mlp = (normed_mlp * mlp_scale).astype(jnp.bfloat16)
    gate_up = jnp.dot(hidden_mlp, gelu_flat, preferred_element_type=jnp.float32).reshape(
        row_count, 2, hidden
    )
    gate_pre, up_pre = (gate_up[:, 0], gate_up[:, 1])
    gelu_val, gelu_slope = gelu_parts(gate_pre)
    activ = (gelu_val * up_pre).astype(jnp.bfloat16)
    mlp_part = jnp.dot(activ, down_t.T, preferred_element_type=jnp.float32)
    block_output = (
        residual + pair_sum(mlp_part.astype(jnp.bfloat16), "tensor")
    ).astype(jnp.bfloat16)
    act_grad = jnp.dot(out_cotangent, down_t, preferred_element_type=jnp.float32)
    down_grad_t = jnp.dot(out_cotangent.T, activ, preferred_element_type=jnp.float32)
    gate_up_grad = (
        jnp.stack([act_grad * up_pre * gelu_slope, act_grad * gelu_val], axis=1)
        .astype(jnp.bfloat16)
        .reshape(row_count, 2 * hidden)
    )
    gelu_grad = jnp.dot(hidden_mlp.T, gate_up_grad, preferred_element_type=jnp.float32).reshape(
        feature_count, 2, hidden
    )
    mlp_in_grad = pair_sum(
        jnp.dot(gate_up_grad, gelu_flat.T, preferred_element_type=jnp.float32).astype(
            jnp.bfloat16
        ),
        "tensor",
    )
    mlpgain_grad = jnp.sum(mlp_in_grad * normed_mlp, axis=0)
    resid_grad = out_cotangent.astype(jnp.float32) + norm_back(
        mlp_in_grad, normed_mlp, spread_mlp, mlp_scale
    )
    resid_bf = resid_grad.astype(jnp.bfloat16)
    out_grad = jnp.dot(resid_bf, proj_t, preferred_element_type=jnp.float32).astype(
        jnp.bfloat16
    )
    proj_grad_t = jnp.dot(resid_bf.T, mixed_flat, preferred_element_type=jnp.float32)

    def reduce_pack(packed, members):
        packed = context_gather(
            context_scatter_sum(packed, "context").astype(jnp.bfloat16), "context"
        ).astype(jnp.float32)
        pieces = []
        start = 0
        for member in members:
            pieces.append(packed[:, start : start + member.shape[1]])
            start += member.shape[1]
        return pieces

    mlp_members = [
        mlpgain_grad[:, None],
        gelu_grad.reshape(feature_count, 2 * hidden),
        down_grad_t,
        proj_grad_t,
    ]
    mlp_packed, out_grad = lax.optimization_barrier(
        (jnp.concatenate(mlp_members, axis=1).astype(jnp.bfloat16), out_grad)
    )
    mlp_shard = lax.psum_scatter(mlp_packed, "fsdp", scatter_dimension=0, tiled=True)
    out_heads = out_grad.reshape(row_count, head_count, HD)
    delta = jnp.transpose(
        jnp.sum(out_heads.astype(jnp.float32) * mixed.astype(jnp.float32), axis=2)
    )

    prob_grad = jnp.einsum(
        "qhd,khd->hqk", out_heads, values_heads, preferred_element_type=jnp.float32
    )
    score_grad = (fwd_probs * (prob_grad - delta[:, :, None])).astype(jnp.bfloat16)
    query_grad = (
        jnp.einsum("hqk,khd->qhd", score_grad, keys_heads, preferred_element_type=jnp.float32)
        * 0.125
    )
    key_all = (
        jnp.einsum("hqk,qhd->khd", score_grad, query_bf, preferred_element_type=jnp.float32)
        * 0.125
    ).reshape(group_rows, local_width)
    value_all = jnp.einsum(
        "hqk,qhd->khd", fwd_weights, out_heads, preferred_element_type=jnp.float32
    ).reshape(group_rows, local_width)
    value_partial, mlp_shard = lax.optimization_barrier(
        (value_all.astype(jnp.bfloat16), mlp_shard)
    )
    value_grad = context_scatter_sum(value_partial, "context")
    key_grad = context_scatter_sum(key_all.astype(jnp.bfloat16), "context")
    mlp_pieces = reduce_pack(mlp_shard, mlp_members)
    key_grad = key_grad.reshape(row_count, head_count, HD)
    value_grad = value_grad.reshape(row_count, head_count, HD)
    qkv_rows = (
        jnp.stack(
            [
                rotate_back(query_grad, cosine, sine_tab),
                rotate_back(key_grad, cosine, sine_tab),
                value_grad,
            ],
            axis=1,
        )
        .astype(jnp.bfloat16)
        .reshape(row_count, 3 * local_width)
    )
    qkv_grad = jnp.dot(hidden_attn.T, qkv_rows, preferred_element_type=jnp.float32).reshape(
        feature_count, 3, local_width
    )
    attn_in_grad = pair_sum(
        jnp.dot(qkv_rows, qkv_flat.T, preferred_element_type=jnp.float32).astype(jnp.bfloat16),
        "tensor",
    )
    attngain_grad = jnp.sum(attn_in_grad * normed_attn, axis=0)
    input_grad = resid_grad + norm_back(attn_in_grad, normed_attn, spread_attn, attn_scale)
    attn_members = [attngain_grad[:, None], qkv_grad.reshape(feature_count, 3 * local_width)]
    attn_pieces = reduce_pack(
        lax.psum_scatter(
            jnp.concatenate(attn_members, axis=1).astype(jnp.bfloat16),
            "fsdp",
            scatter_dimension=0,
            tiled=True,
        ),
        attn_members,
    )
    shares = (
        attn_pieces[0][:, 0],
        attn_pieces[1].reshape(shard_rows, 3, local_width),
        mlp_pieces[3].T,
        mlp_pieces[0][:, 0],
        mlp_pieces[1].reshape(shard_rows, 2, hidden),
        mlp_pieces[2].T,
    )
    return (
        block_output,
        input_grad,
        shares[0],
        shares[1],
        shares[2],
        shares[3],
        shares[4],
        shares[5],
    )


def solution(mesh):
    in_specs = (
        P(("fsdp", "context"), None),
        P("fsdp", None),
        P("fsdp"),
        P("fsdp", None, "tensor"),
        P("tensor", "fsdp"),
        P("fsdp"),
        P("fsdp", None, "tensor"),
        P("tensor", "fsdp"),
        P(("fsdp", "context"), None),
    )
    out_specs = (
        P(("fsdp", "context"), None),
        P(("fsdp", "context"), None),
        P("fsdp"),
        P("fsdp", None, "tensor"),
        P("tensor", "fsdp"),
        P("fsdp"),
        P("fsdp", None, "tensor"),
        P("tensor", "fsdp"),
    )
    return jax.shard_map(
        on_device, mesh=mesh, in_specs=in_specs, out_specs=out_specs, check_vma=False
    )
```

```python
import jax
import jax.numpy as jnp
from jax import lax
from jax.sharding import PartitionSpec as P

HD = 64


EPSILON = 1e-05
THETA = 160000.0
MASKED_LOW = -1e30


def layer_norm(values):
    centre = values - jnp.mean(values, axis=-1, keepdims=True)
    spread = lax.rsqrt(jnp.mean(centre * centre, axis=-1, keepdims=True) + EPSILON)
    return (centre * spread, spread)


def norm_back(grad_out, normed, spread, gain):
    scaled = grad_out * gain
    inner = jnp.mean(scaled, axis=-1, keepdims=True) + normed * jnp.mean(
        scaled * normed, axis=-1, keepdims=True
    )
    return spread * (scaled - inner)


def segments_of(row_ids, lengths):
    ends = jnp.cumsum(lengths)
    segment = jnp.sum((row_ids[:, None] >= ends[None, :]).astype(jnp.int32), axis=1)
    starts = ends - lengths
    picked = segment[:, None] == jnp.arange(lengths.shape[0], dtype=jnp.int32)[None, :]
    begin = jnp.sum(jnp.where(picked, starts[None, :], 0), axis=1)
    return (segment, row_ids - begin)


def rope_tables(positions, head_dim):
    half_dim = head_dim // 2
    exponent = jnp.arange(half_dim, dtype=jnp.float32) * (-2.0 / head_dim)
    frequency = jnp.power(jnp.float32(THETA), exponent)
    angles = positions.astype(jnp.float32)[:, None] * frequency[None, :]
    return (jnp.cos(angles)[:, None, :], jnp.sin(angles)[:, None, :])


def rotate(values, cosine, sine_tab):
    half_dim = values.shape[-1] // 2
    lower_half, upper_half = (values[..., :half_dim], values[..., half_dim:])
    return jnp.concatenate(
        [lower_half * cosine - upper_half * sine_tab, upper_half * cosine + lower_half * sine_tab],
        axis=-1,
    )


def rotate_back(grads, cosine, sine_tab):
    half_dim = grads.shape[-1] // 2
    lower_half, upper_half = (grads[..., :half_dim], grads[..., half_dim:])
    return jnp.concatenate(
        [lower_half * cosine + upper_half * sine_tab, upper_half * cosine - lower_half * sine_tab],
        axis=-1,
    )


def gelu_parts(gate_pre):
    normal_cdf = 0.5 * (1.0 + jax.scipy.special.erf(gate_pre * 0.7071067811865476))
    density = jnp.exp(-0.5 * gate_pre * gate_pre) * 0.3989422804014327
    return (gate_pre * normal_cdf, normal_cdf + gate_pre * density)


def pair_sum(values, axis_name):
    if lax.axis_size(axis_name) != 2:
        return lax.psum(values, axis_name)
    other = lax.ppermute(values, axis_name, perm=[(0, 1), (1, 0)])
    return values.astype(jnp.float32) + other.astype(jnp.float32)


def context_gather(values, axis_name):
    count = lax.axis_size(axis_name)
    spread = jnp.broadcast_to(values[None], (count,) + values.shape)
    gathered = lax.all_to_all(spread, axis_name, 0, 0, tiled=True)
    return gathered.reshape((count * values.shape[0],) + values.shape[1:])


def context_scatter_sum(values, axis_name):
    count = lax.axis_size(axis_name)
    rows = values.shape[0] // count
    parts = lax.all_to_all(
        values.reshape((count, rows) + values.shape[1:]), axis_name, 0, 0, tiled=True
    )
    return jnp.sum(parts.astype(jnp.float32), axis=0)


def on_device(
    block_input,
    seq_lengths,
    attn_gain,
    qkv_weight,
    proj_weight,
    mlp_gain,
    gelu_weight,
    down_weight,
    out_cotangent,
):
    row_count = block_input.shape[0]
    feature_count = block_input.shape[1]
    lengths = seq_lengths[0]
    group_rows = row_count * lax.axis_size("context")
    own_first = lax.axis_index("context") * row_count
    own_rows = own_first + jnp.arange(row_count, dtype=jnp.int32)
    own_segment, positions = segments_of(own_rows, lengths)
    cosine, sine_tab = rope_tables(positions, HD)
    shard_rows = qkv_weight.shape[0]
    local_width = qkv_weight.shape[2]
    head_count = local_width // HD
    hidden = gelu_weight.shape[2]
    first_pack = lax.all_gather(
        jnp.concatenate(
            [
                qkv_weight.reshape(shard_rows, 3 * local_width),
                attn_gain[:, None],
                mlp_gain[:, None],
            ],
            axis=1,
        ),
        "fsdp",
        axis=0,
        tiled=True,
    )
    second_pack = lax.all_gather(
        jnp.concatenate(
            [proj_weight.T, gelu_weight.reshape(shard_rows, 2 * hidden), down_weight.T], axis=1
        ),
        "fsdp",
        axis=0,
        tiled=True,
    )
    qkv_flat = first_pack[:, : 3 * local_width]
    attn_full = first_pack[:, 3 * local_width]
    mlp_full = first_pack[:, 3 * local_width + 1]
    proj_t = second_pack[:, :local_width]
    gelu_flat = second_pack[:, local_width : local_width + 2 * hidden]
    down_t = second_pack[:, local_width + 2 * hidden :]
    attn_scale = attn_full.astype(jnp.float32)
    mlp_scale = mlp_full.astype(jnp.float32)
    inputs = block_input.astype(jnp.float32)
    normed_attn, spread_attn = layer_norm(inputs)
    hidden_attn = (normed_attn * attn_scale).astype(jnp.bfloat16)
    projected = jnp.dot(hidden_attn, qkv_flat, preferred_element_type=jnp.float32).reshape(
        row_count, 3, head_count, HD
    )
    query_bf = rotate(projected[:, 0], cosine, sine_tab).astype(jnp.bfloat16)
    key_bf = rotate(projected[:, 1], cosine, sine_tab).astype(jnp.bfloat16)
    value_bf = projected[:, 2].astype(jnp.bfloat16)
    key_flat = key_bf.reshape(row_count, local_width)
    value_flat = value_bf.reshape(row_count, local_width)
    kv_group = context_gather(jnp.concatenate([key_flat, value_flat], axis=1), "context")
    keys_group, values_group = (kv_group[:, :local_width], kv_group[:, local_width:])
    keys_heads = keys_group.reshape(group_rows, head_count, HD)
    values_heads = values_group.reshape(group_rows, head_count, HD)
    group_segment, unused_pos = segments_of(jnp.arange(group_rows, dtype=jnp.int32), lengths)
    same_group = (own_segment[:, None] == group_segment[None, :])[None]
    fwd_scores = (
        jnp.einsum("qhd,khd->hqk", query_bf, keys_heads, preferred_element_type=jnp.float32) * 0.125
    )
    row_max = jnp.max(jnp.where(same_group, fwd_scores, MASKED_LOW), axis=2)
    denom_sum = jnp.sum(
        jnp.where(same_group, jnp.exp(fwd_scores - row_max[:, :, None]), 0.0), axis=2
    )
    log_total = row_max + jnp.log(denom_sum)
    fwd_probs = jnp.where(same_group, jnp.exp(fwd_scores - log_total[:, :, None]), 0.0)
    fwd_weights = fwd_probs.astype(jnp.bfloat16)
    mixed = jnp.einsum(
        "hqk,khd->qhd", fwd_weights, values_heads, preferred_element_type=jnp.float32
    ).astype(jnp.bfloat16)
    mixed_flat = mixed.reshape(row_count, local_width)
    attn_part = jnp.dot(mixed_flat, proj_t.T, preferred_element_type=jnp.float32)
    residual = inputs + pair_sum(attn_part.astype(jnp.bfloat16), "tensor")
    normed_mlp, spread_mlp = layer_norm(residual)
    hidden_mlp = (normed_mlp * mlp_scale).astype(jnp.bfloat16)
    gate_up = jnp.dot(hidden_mlp, gelu_flat, preferred_element_type=jnp.float32).reshape(
        row_count, 2, hidden
    )
    gate_pre, up_pre = (gate_up[:, 0], gate_up[:, 1])
    gelu_val, gelu_slope = gelu_parts(gate_pre)
    activ = (gelu_val * up_pre).astype(jnp.bfloat16)
    mlp_part = jnp.dot(activ, down_t.T, preferred_element_type=jnp.float32)
    block_output = (
        residual + pair_sum(mlp_part.astype(jnp.bfloat16), "tensor")
    ).astype(jnp.bfloat16)
    act_grad = jnp.dot(out_cotangent, down_t, preferred_element_type=jnp.float32)
    down_grad_t = jnp.dot(out_cotangent.T, activ, preferred_element_type=jnp.float32)
    gate_up_grad = (
        jnp.stack([act_grad * up_pre * gelu_slope, act_grad * gelu_val], axis=1)
        .astype(jnp.bfloat16)
        .reshape(row_count, 2 * hidden)
    )
    gelu_grad = jnp.dot(hidden_mlp.T, gate_up_grad, preferred_element_type=jnp.float32).reshape(
        feature_count, 2, hidden
    )
    mlp_in_grad = pair_sum(
        jnp.dot(gate_up_grad, gelu_flat.T, preferred_element_type=jnp.float32).astype(
            jnp.bfloat16
        ),
        "tensor",
    )
    mlpgain_grad = jnp.sum(mlp_in_grad * normed_mlp, axis=0)
    resid_grad = out_cotangent.astype(jnp.float32) + norm_back(
        mlp_in_grad, normed_mlp, spread_mlp, mlp_scale
    )
    resid_bf = resid_grad.astype(jnp.bfloat16)
    out_grad = jnp.dot(resid_bf, proj_t, preferred_element_type=jnp.float32).astype(
        jnp.bfloat16
    )
    proj_grad_t = jnp.dot(resid_bf.T, mixed_flat, preferred_element_type=jnp.float32)

    def reduce_pack(packed, members):
        packed = context_gather(
            context_scatter_sum(packed, "context").astype(jnp.bfloat16), "context"
        ).astype(jnp.float32)
        pieces = []
        start = 0
        for member in members:
            pieces.append(packed[:, start : start + member.shape[1]])
            start += member.shape[1]
        return pieces

    mlp_members = [
        mlpgain_grad[:, None],
        gelu_grad.reshape(feature_count, 2 * hidden),
        down_grad_t,
        proj_grad_t,
    ]
    mlp_packed, out_grad = lax.optimization_barrier(
        (jnp.concatenate(mlp_members, axis=1).astype(jnp.bfloat16), out_grad)
    )
    mlp_shard = lax.psum_scatter(mlp_packed, "fsdp", scatter_dimension=0, tiled=True)
    out_heads = out_grad.reshape(row_count, head_count, HD)
    delta = jnp.transpose(
        jnp.sum(out_heads.astype(jnp.float32) * mixed.astype(jnp.float32), axis=2)
    )

    prob_grad = jnp.einsum(
        "qhd,khd->hqk", out_heads, values_heads, preferred_element_type=jnp.float32
    )
    score_grad = (fwd_probs * (prob_grad - delta[:, :, None])).astype(jnp.bfloat16)
    query_grad = (
        jnp.einsum("hqk,khd->qhd", score_grad, keys_heads, preferred_element_type=jnp.float32)
        * 0.125
    )
    key_all = (
        jnp.einsum("hqk,qhd->khd", score_grad, query_bf, preferred_element_type=jnp.float32)
        * 0.125
    ).reshape(group_rows, local_width)
    value_all = jnp.einsum(
        "hqk,qhd->khd", fwd_weights, out_heads, preferred_element_type=jnp.float32
    ).reshape(group_rows, local_width)
    value_partial, mlp_shard = lax.optimization_barrier(
        (value_all.astype(jnp.bfloat16), mlp_shard)
    )
    value_grad = context_scatter_sum(value_partial, "context")
    key_grad = context_scatter_sum(key_all.astype(jnp.bfloat16), "context")
    mlp_pieces = reduce_pack(mlp_shard, mlp_members)
    key_grad = key_grad.reshape(row_count, head_count, HD)
    value_grad = value_grad.reshape(row_count, head_count, HD)
    qkv_rows = (
        jnp.stack(
            [
                rotate_back(query_grad, cosine, sine_tab),
                rotate_back(key_grad, cosine, sine_tab),
                value_grad,
            ],
            axis=1,
        )
        .astype(jnp.bfloat16)
        .reshape(row_count, 3 * local_width)
    )
    qkv_grad = jnp.dot(hidden_attn.T, qkv_rows, preferred_element_type=jnp.float32).reshape(
        feature_count, 3, local_width
    )
    attn_in_grad = pair_sum(
        jnp.dot(qkv_rows, qkv_flat.T, preferred_element_type=jnp.float32).astype(jnp.bfloat16),
        "tensor",
    )
    attngain_grad = jnp.sum(attn_in_grad * normed_attn, axis=0)
    input_grad = resid_grad + norm_back(attn_in_grad, normed_attn, spread_attn, attn_scale)
    attn_members = [attngain_grad[:, None], qkv_grad.reshape(feature_count, 3 * local_width)]
    attn_pieces = reduce_pack(
        lax.psum_scatter(
            jnp.concatenate(attn_members, axis=1).astype(jnp.bfloat16),
            "fsdp",
            scatter_dimension=0,
            tiled=True,
        ),
        attn_members,
    )
    shares = (
        attn_pieces[0][:, 0],
        attn_pieces[1].reshape(shard_rows, 3, local_width),
        mlp_pieces[3].T,
        mlp_pieces[0][:, 0],
        mlp_pieces[1].reshape(shard_rows, 2, hidden),
        mlp_pieces[2].T,
    )
    return (
        block_output,
        input_grad,
        shares[0],
        shares[1],
        shares[2],
        shares[3],
        shares[4],
        shares[5],
    )


def solution(mesh):
    in_specs = (
        P(("fsdp", "context"), None),
        P("fsdp", None),
        P("fsdp"),
        P("fsdp", None, "tensor"),
        P("tensor", "fsdp"),
        P("fsdp"),
        P("fsdp", None, "tensor"),
        P("tensor", "fsdp"),
        P(("fsdp", "context"), None),
    )
    out_specs = (
        P(("fsdp", "context"), None),
        P(("fsdp", "context"), None),
        P("fsdp"),
        P("fsdp", None, "tensor"),
        P("tensor", "fsdp"),
        P("fsdp"),
        P("fsdp", None, "tensor"),
        P("tensor", "fsdp"),
    )
    return jax.shard_map(
        on_device, mesh=mesh, in_specs=in_specs, out_specs=out_specs, check_vma=False
    )
```

```python
import jax
import jax.numpy as jnp
from jax import lax
from jax.sharding import PartitionSpec as P

HD = 64


EPSILON = 1e-05
THETA = 160000.0
MASKED_LOW = -1e30


def layer_norm(values):
    centre = values - jnp.mean(values, axis=-1, keepdims=True)
    spread = lax.rsqrt(jnp.mean(centre * centre, axis=-1, keepdims=True) + EPSILON)
    return (centre * spread, spread)


def norm_back(grad_out, normed, spread, gain):
    scaled = grad_out * gain
    inner = jnp.mean(scaled, axis=-1, keepdims=True) + normed * jnp.mean(
        scaled * normed, axis=-1, keepdims=True
    )
    return spread * (scaled - inner)


def segments_of(row_ids, lengths):
    ends = jnp.cumsum(lengths)
    segment = jnp.sum((row_ids[:, None] >= ends[None, :]).astype(jnp.int32), axis=1)
    starts = ends - lengths
    picked = segment[:, None] == jnp.arange(lengths.shape[0], dtype=jnp.int32)[None, :]
    begin = jnp.sum(jnp.where(picked, starts[None, :], 0), axis=1)
    return (segment, row_ids - begin)


def rope_tables(positions, head_dim):
    half_dim = head_dim // 2
    exponent = jnp.arange(half_dim, dtype=jnp.float32) * (-2.0 / head_dim)
    frequency = jnp.power(jnp.float32(THETA), exponent)
    angles = positions.astype(jnp.float32)[:, None] * frequency[None, :]
    return (jnp.cos(angles)[:, None, :], jnp.sin(angles)[:, None, :])


def rotate(values, cosine, sine_tab):
    half_dim = values.shape[-1] // 2
    lower_half, upper_half = (values[..., :half_dim], values[..., half_dim:])
    return jnp.concatenate(
        [lower_half * cosine - upper_half * sine_tab, upper_half * cosine + lower_half * sine_tab],
        axis=-1,
    )


def rotate_back(grads, cosine, sine_tab):
    half_dim = grads.shape[-1] // 2
    lower_half, upper_half = (grads[..., :half_dim], grads[..., half_dim:])
    return jnp.concatenate(
        [lower_half * cosine + upper_half * sine_tab, upper_half * cosine - lower_half * sine_tab],
        axis=-1,
    )


def gelu_parts(gate_pre):
    normal_cdf = 0.5 * (1.0 + jax.scipy.special.erf(gate_pre * 0.7071067811865476))
    density = jnp.exp(-0.5 * gate_pre * gate_pre) * 0.3989422804014327
    return (gate_pre * normal_cdf, normal_cdf + gate_pre * density)


def pair_sum(values, axis_name):
    if lax.axis_size(axis_name) != 2:
        return lax.psum(values, axis_name)
    other = lax.ppermute(values, axis_name, perm=[(0, 1), (1, 0)])
    return values.astype(jnp.float32) + other.astype(jnp.float32)


def context_gather(values, axis_name):
    count = lax.axis_size(axis_name)
    spread = jnp.broadcast_to(values[None], (count,) + values.shape)
    gathered = lax.all_to_all(spread, axis_name, 0, 0, tiled=True)
    return gathered.reshape((count * values.shape[0],) + values.shape[1:])


def context_scatter_sum(values, axis_name):
    count = lax.axis_size(axis_name)
    rows = values.shape[0] // count
    parts = lax.all_to_all(
        values.reshape((count, rows) + values.shape[1:]), axis_name, 0, 0, tiled=True
    )
    return jnp.sum(parts.astype(jnp.float32), axis=0)


def on_device(
    block_input,
    seq_lengths,
    attn_gain,
    qkv_weight,
    proj_weight,
    mlp_gain,
    gelu_weight,
    down_weight,
    out_cotangent,
):
    row_count = block_input.shape[0]
    feature_count = block_input.shape[1]
    lengths = seq_lengths[0]
    group_rows = row_count * lax.axis_size("context")
    own_first = lax.axis_index("context") * row_count
    own_rows = own_first + jnp.arange(row_count, dtype=jnp.int32)
    own_segment, positions = segments_of(own_rows, lengths)
    inputs_group = context_gather(block_input, "context")
    cosine, sine_tab = rope_tables(positions, HD)
    shard_rows = qkv_weight.shape[0]
    local_width = qkv_weight.shape[2]
    head_count = local_width // HD
    hidden = gelu_weight.shape[2]
    first_pack = lax.all_gather(
        jnp.concatenate(
            [
                qkv_weight.reshape(shard_rows, 3 * local_width),
                attn_gain[:, None],
                mlp_gain[:, None],
            ],
            axis=1,
        ),
        "fsdp",
        axis=0,
        tiled=True,
    )
    second_pack = lax.all_gather(
        jnp.concatenate(
            [proj_weight.T, gelu_weight.reshape(shard_rows, 2 * hidden), down_weight.T], axis=1
        ),
        "fsdp",
        axis=0,
        tiled=True,
    )
    qkv_flat = first_pack[:, : 3 * local_width]
    attn_full = first_pack[:, 3 * local_width]
    mlp_full = first_pack[:, 3 * local_width + 1]
    proj_t = second_pack[:, :local_width]
    gelu_flat = second_pack[:, local_width : local_width + 2 * hidden]
    down_t = second_pack[:, local_width + 2 * hidden :]
    attn_scale = attn_full.astype(jnp.float32)
    mlp_scale = mlp_full.astype(jnp.float32)
    inputs = block_input.astype(jnp.float32)
    normed_attn, spread_attn = layer_norm(inputs)
    hidden_attn = (normed_attn * attn_scale).astype(jnp.bfloat16)
    query_bf = rotate(
        jnp.dot(
            hidden_attn, qkv_flat[:, :local_width], preferred_element_type=jnp.float32
        ).reshape(row_count, head_count, HD),
        cosine,
        sine_tab,
    ).astype(jnp.bfloat16)
    group_normed, unused_spread = layer_norm(inputs_group.astype(jnp.float32))
    hidden_group = (group_normed * attn_scale).astype(jnp.bfloat16)
    group_segment, group_pos = segments_of(jnp.arange(group_rows, dtype=jnp.int32), lengths)
    group_cos, group_sin = rope_tables(group_pos, HD)
    kv_projected = jnp.dot(
        hidden_group, qkv_flat[:, local_width:], preferred_element_type=jnp.float32
    ).reshape(group_rows, 2, head_count, HD)
    keys_heads = rotate(kv_projected[:, 0], group_cos, group_sin).astype(jnp.bfloat16)
    values_heads = kv_projected[:, 1].astype(jnp.bfloat16)
    same_group = (own_segment[:, None] == group_segment[None, :])[None]
    fwd_scores = (
        jnp.einsum("qhd,khd->hqk", query_bf, keys_heads, preferred_element_type=jnp.float32) * 0.125
    )
    row_max = jnp.max(jnp.where(same_group, fwd_scores, MASKED_LOW), axis=2)
    denom_sum = jnp.sum(
        jnp.where(same_group, jnp.exp(fwd_scores - row_max[:, :, None]), 0.0), axis=2
    )
    log_total = row_max + jnp.log(denom_sum)
    fwd_probs = jnp.where(same_group, jnp.exp(fwd_scores - log_total[:, :, None]), 0.0)
    fwd_weights = fwd_probs.astype(jnp.bfloat16)
    mixed = jnp.einsum(
        "hqk,khd->qhd", fwd_weights, values_heads, preferred_element_type=jnp.float32
    ).astype(jnp.bfloat16)
    mixed_flat = mixed.reshape(row_count, local_width)
    attn_part = jnp.dot(mixed_flat, proj_t.T, preferred_element_type=jnp.float32)
    residual = inputs + pair_sum(attn_part.astype(jnp.bfloat16), "tensor")
    normed_mlp, spread_mlp = layer_norm(residual)
    hidden_mlp = (normed_mlp * mlp_scale).astype(jnp.bfloat16)
    gate_up = jnp.dot(hidden_mlp, gelu_flat, preferred_element_type=jnp.float32).reshape(
        row_count, 2, hidden
    )
    gate_pre, up_pre = (gate_up[:, 0], gate_up[:, 1])
    gelu_val, gelu_slope = gelu_parts(gate_pre)
    activ = (gelu_val * up_pre).astype(jnp.bfloat16)
    mlp_part = jnp.dot(activ, down_t.T, preferred_element_type=jnp.float32)
    block_output = (
        residual + pair_sum(mlp_part.astype(jnp.bfloat16), "tensor")
    ).astype(jnp.bfloat16)
    act_grad = jnp.dot(out_cotangent, down_t, preferred_element_type=jnp.float32)
    down_grad_t = jnp.dot(out_cotangent.T, activ, preferred_element_type=jnp.float32)
    gate_up_grad = (
        jnp.stack([act_grad * up_pre * gelu_slope, act_grad * gelu_val], axis=1)
        .astype(jnp.bfloat16)
        .reshape(row_count, 2 * hidden)
    )
    gelu_grad = jnp.dot(hidden_mlp.T, gate_up_grad, preferred_element_type=jnp.float32).reshape(
        feature_count, 2, hidden
    )
    mlp_in_grad = pair_sum(
        jnp.dot(gate_up_grad, gelu_flat.T, preferred_element_type=jnp.float32).astype(
            jnp.bfloat16
        ),
        "tensor",
    )
    mlpgain_grad = jnp.sum(mlp_in_grad * normed_mlp, axis=0)
    resid_grad = out_cotangent.astype(jnp.float32) + norm_back(
        mlp_in_grad, normed_mlp, spread_mlp, mlp_scale
    )
    resid_bf = resid_grad.astype(jnp.bfloat16)
    out_grad = jnp.dot(resid_bf, proj_t, preferred_element_type=jnp.float32).astype(
        jnp.bfloat16
    )
    proj_grad_t = jnp.dot(resid_bf.T, mixed_flat, preferred_element_type=jnp.float32)

    def reduce_pack(packed, members):
        packed = context_gather(
            context_scatter_sum(packed, "context").astype(jnp.bfloat16), "context"
        ).astype(jnp.float32)
        pieces = []
        start = 0
        for member in members:
            pieces.append(packed[:, start : start + member.shape[1]])
            start += member.shape[1]
        return pieces

    mlp_members = [
        mlpgain_grad[:, None],
        gelu_grad.reshape(feature_count, 2 * hidden),
        down_grad_t,
        proj_grad_t,
    ]
    mlp_packed, out_grad = lax.optimization_barrier(
        (jnp.concatenate(mlp_members, axis=1).astype(jnp.bfloat16), out_grad)
    )
    mlp_shard = lax.psum_scatter(mlp_packed, "fsdp", scatter_dimension=0, tiled=True)
    out_heads = out_grad.reshape(row_count, head_count, HD)
    delta = jnp.transpose(
        jnp.sum(out_heads.astype(jnp.float32) * mixed.astype(jnp.float32), axis=2)
    )

    prob_grad = jnp.einsum(
        "qhd,khd->hqk", out_heads, values_heads, preferred_element_type=jnp.float32
    )
    score_grad = (fwd_probs * (prob_grad - delta[:, :, None])).astype(jnp.bfloat16)
    query_grad = (
        jnp.einsum("hqk,khd->qhd", score_grad, keys_heads, preferred_element_type=jnp.float32)
        * 0.125
    )
    key_all = (
        jnp.einsum("hqk,qhd->khd", score_grad, query_bf, preferred_element_type=jnp.float32)
        * 0.125
    ).reshape(group_rows, local_width)
    value_all = jnp.einsum(
        "hqk,qhd->khd", fwd_weights, out_heads, preferred_element_type=jnp.float32
    ).reshape(group_rows, local_width)
    value_partial, mlp_shard = lax.optimization_barrier(
        (value_all.astype(jnp.bfloat16), mlp_shard)
    )
    value_grad = context_scatter_sum(value_partial, "context")
    key_grad = context_scatter_sum(key_all.astype(jnp.bfloat16), "context")
    mlp_pieces = reduce_pack(mlp_shard, mlp_members)
    key_grad = key_grad.reshape(row_count, head_count, HD)
    value_grad = value_grad.reshape(row_count, head_count, HD)
    qkv_rows = (
        jnp.stack(
            [
                rotate_back(query_grad, cosine, sine_tab),
                rotate_back(key_grad, cosine, sine_tab),
                value_grad,
            ],
            axis=1,
        )
        .astype(jnp.bfloat16)
        .reshape(row_count, 3 * local_width)
    )
    qkv_grad = jnp.dot(hidden_attn.T, qkv_rows, preferred_element_type=jnp.float32).reshape(
        feature_count, 3, local_width
    )
    attn_in_grad = pair_sum(
        jnp.dot(qkv_rows, qkv_flat.T, preferred_element_type=jnp.float32).astype(jnp.bfloat16),
        "tensor",
    )
    attngain_grad = jnp.sum(attn_in_grad * normed_attn, axis=0)
    input_grad = resid_grad + norm_back(attn_in_grad, normed_attn, spread_attn, attn_scale)
    attn_members = [attngain_grad[:, None], qkv_grad.reshape(feature_count, 3 * local_width)]
    attn_pieces = reduce_pack(
        lax.psum_scatter(
            jnp.concatenate(attn_members, axis=1).astype(jnp.bfloat16),
            "fsdp",
            scatter_dimension=0,
            tiled=True,
        ),
        attn_members,
    )
    shares = (
        attn_pieces[0][:, 0],
        attn_pieces[1].reshape(shard_rows, 3, local_width),
        mlp_pieces[3].T,
        mlp_pieces[0][:, 0],
        mlp_pieces[1].reshape(shard_rows, 2, hidden),
        mlp_pieces[2].T,
    )
    return (
        block_output,
        input_grad,
        shares[0],
        shares[1],
        shares[2],
        shares[3],
        shares[4],
        shares[5],
    )


def solution(mesh):
    in_specs = (
        P(("fsdp", "context"), None),
        P("fsdp", None),
        P("fsdp"),
        P("fsdp", None, "tensor"),
        P("tensor", "fsdp"),
        P("fsdp"),
        P("fsdp", None, "tensor"),
        P("tensor", "fsdp"),
        P(("fsdp", "context"), None),
    )
    out_specs = (
        P(("fsdp", "context"), None),
        P(("fsdp", "context"), None),
        P("fsdp"),
        P("fsdp", None, "tensor"),
        P("tensor", "fsdp"),
        P("fsdp"),
        P("fsdp", None, "tensor"),
        P("tensor", "fsdp"),
    )
    return jax.shard_map(
        on_device, mesh=mesh, in_specs=in_specs, out_specs=out_specs, check_vma=False
    )
```

```python
import jax
import jax.numpy as jnp
from jax import lax
from jax.sharding import PartitionSpec as P

HD = 64


EPSILON = 1e-05
THETA = 160000.0
MASKED_LOW = -1e30


def layer_norm(values):
    centre = values - jnp.mean(values, axis=-1, keepdims=True)
    spread = lax.rsqrt(jnp.mean(centre * centre, axis=-1, keepdims=True) + EPSILON)
    return (centre * spread, spread)


def norm_back(grad_out, normed, spread, gain):
    scaled = grad_out * gain
    inner = jnp.mean(scaled, axis=-1, keepdims=True) + normed * jnp.mean(
        scaled * normed, axis=-1, keepdims=True
    )
    return spread * (scaled - inner)


def segments_of(row_ids, lengths):
    ends = jnp.cumsum(lengths)
    segment = jnp.sum((row_ids[:, None] >= ends[None, :]).astype(jnp.int32), axis=1)
    starts = ends - lengths
    picked = segment[:, None] == jnp.arange(lengths.shape[0], dtype=jnp.int32)[None, :]
    begin = jnp.sum(jnp.where(picked, starts[None, :], 0), axis=1)
    return (segment, row_ids - begin)


def rope_tables(positions, head_dim):
    half_dim = head_dim // 2
    exponent = jnp.arange(half_dim, dtype=jnp.float32) * (-2.0 / head_dim)
    frequency = jnp.power(jnp.float32(THETA), exponent)
    angles = positions.astype(jnp.float32)[:, None] * frequency[None, :]
    return (jnp.cos(angles)[:, None, :], jnp.sin(angles)[:, None, :])


def rotate(values, cosine, sine_tab):
    half_dim = values.shape[-1] // 2
    lower_half, upper_half = (values[..., :half_dim], values[..., half_dim:])
    return jnp.concatenate(
        [lower_half * cosine - upper_half * sine_tab, upper_half * cosine + lower_half * sine_tab],
        axis=-1,
    )


def rotate_back(grads, cosine, sine_tab):
    half_dim = grads.shape[-1] // 2
    lower_half, upper_half = (grads[..., :half_dim], grads[..., half_dim:])
    return jnp.concatenate(
        [lower_half * cosine + upper_half * sine_tab, upper_half * cosine - lower_half * sine_tab],
        axis=-1,
    )


def gelu_parts(gate_pre):
    normal_cdf = 0.5 * (1.0 + jax.scipy.special.erf(gate_pre * 0.7071067811865476))
    density = jnp.exp(-0.5 * gate_pre * gate_pre) * 0.3989422804014327
    return (gate_pre * normal_cdf, normal_cdf + gate_pre * density)


def pair_sum(values, axis_name):
    if lax.axis_size(axis_name) != 2:
        return lax.psum(values, axis_name)
    other = lax.ppermute(values, axis_name, perm=[(0, 1), (1, 0)])
    return values.astype(jnp.float32) + other.astype(jnp.float32)


def context_gather(values, axis_name):
    count = lax.axis_size(axis_name)
    spread = jnp.broadcast_to(values[None], (count,) + values.shape)
    gathered = lax.all_to_all(spread, axis_name, 0, 0, tiled=True)
    return gathered.reshape((count * values.shape[0],) + values.shape[1:])


def context_scatter_sum(values, axis_name):
    count = lax.axis_size(axis_name)
    rows = values.shape[0] // count
    parts = lax.all_to_all(
        values.reshape((count, rows) + values.shape[1:]), axis_name, 0, 0, tiled=True
    )
    return jnp.sum(parts.astype(jnp.float32), axis=0)


def on_device(
    block_input,
    seq_lengths,
    attn_gain,
    qkv_weight,
    proj_weight,
    mlp_gain,
    gelu_weight,
    down_weight,
    out_cotangent,
):
    row_count = block_input.shape[0]
    feature_count = block_input.shape[1]
    lengths = seq_lengths[0]
    group_rows = row_count * lax.axis_size("context")
    own_first = lax.axis_index("context") * row_count
    own_rows = own_first + jnp.arange(row_count, dtype=jnp.int32)
    own_segment, positions = segments_of(own_rows, lengths)
    inputs_group = context_gather(block_input, "context")
    cosine, sine_tab = rope_tables(positions, HD)
    shard_rows = qkv_weight.shape[0]
    local_width = qkv_weight.shape[2]
    head_count = local_width // HD
    hidden = gelu_weight.shape[2]
    first_pack = lax.all_gather(
        jnp.concatenate(
            [
                qkv_weight.reshape(shard_rows, 3 * local_width),
                attn_gain[:, None],
                mlp_gain[:, None],
            ],
            axis=1,
        ),
        "fsdp",
        axis=0,
        tiled=True,
    )
    second_pack = lax.all_gather(
        jnp.concatenate(
            [proj_weight.T, gelu_weight.reshape(shard_rows, 2 * hidden), down_weight.T], axis=1
        ),
        "fsdp",
        axis=0,
        tiled=True,
    )
    qkv_flat = first_pack[:, : 3 * local_width]
    attn_full = first_pack[:, 3 * local_width]
    mlp_full = first_pack[:, 3 * local_width + 1]
    proj_t = second_pack[:, :local_width]
    gelu_flat = second_pack[:, local_width : local_width + 2 * hidden]
    down_t = second_pack[:, local_width + 2 * hidden :]
    attn_scale = attn_full.astype(jnp.float32)
    mlp_scale = mlp_full.astype(jnp.float32)
    inputs = block_input.astype(jnp.float32)
    normed_attn, spread_attn = layer_norm(inputs)
    hidden_attn = (normed_attn * attn_scale).astype(jnp.bfloat16)
    query_bf = rotate(
        jnp.dot(
            hidden_attn, qkv_flat[:, :local_width], preferred_element_type=jnp.float32
        ).reshape(row_count, head_count, HD),
        cosine,
        sine_tab,
    ).astype(jnp.bfloat16)
    group_normed, unused_spread = layer_norm(inputs_group.astype(jnp.float32))
    hidden_group = (group_normed * attn_scale).astype(jnp.bfloat16)
    group_segment, group_pos = segments_of(jnp.arange(group_rows, dtype=jnp.int32), lengths)
    group_cos, group_sin = rope_tables(group_pos, HD)
    kv_projected = jnp.dot(
        hidden_group, qkv_flat[:, local_width:], preferred_element_type=jnp.float32
    ).reshape(group_rows, 2, head_count, HD)
    keys_heads = rotate(kv_projected[:, 0], group_cos, group_sin).astype(jnp.bfloat16)
    values_heads = kv_projected[:, 1].astype(jnp.bfloat16)
    same_group = (own_segment[:, None] == group_segment[None, :])[None]
    fwd_scores = (
        jnp.einsum("qhd,khd->hqk", query_bf, keys_heads, preferred_element_type=jnp.float32) * 0.125
    )
    row_max = jnp.max(jnp.where(same_group, fwd_scores, MASKED_LOW), axis=2)
    denom_sum = jnp.sum(
        jnp.where(same_group, jnp.exp(fwd_scores - row_max[:, :, None]), 0.0), axis=2
    )
    log_total = row_max + jnp.log(denom_sum)
    fwd_probs = jnp.where(same_group, jnp.exp(fwd_scores - log_total[:, :, None]), 0.0)
    fwd_weights = fwd_probs.astype(jnp.bfloat16)
    mixed = jnp.einsum(
        "hqk,khd->qhd", fwd_weights, values_heads, preferred_element_type=jnp.float32
    ).astype(jnp.bfloat16)
    mixed_flat = mixed.reshape(row_count, local_width)
    attn_part = jnp.dot(mixed_flat, proj_t.T, preferred_element_type=jnp.float32)
    residual = inputs + pair_sum(attn_part.astype(jnp.bfloat16), "tensor")
    normed_mlp, spread_mlp = layer_norm(residual)
    hidden_mlp = (normed_mlp * mlp_scale).astype(jnp.bfloat16)
    gate_up = jnp.dot(hidden_mlp, gelu_flat, preferred_element_type=jnp.float32).reshape(
        row_count, 2, hidden
    )
    gate_pre, up_pre = (gate_up[:, 0], gate_up[:, 1])
    gelu_val, gelu_slope = gelu_parts(gate_pre)
    activ = (gelu_val * up_pre).astype(jnp.bfloat16)
    mlp_part = jnp.dot(activ, down_t.T, preferred_element_type=jnp.float32)
    block_output = (
        residual + pair_sum(mlp_part.astype(jnp.bfloat16), "tensor")
    ).astype(jnp.bfloat16)
    act_grad = jnp.dot(out_cotangent, down_t, preferred_element_type=jnp.float32)
    down_grad_t = jnp.dot(out_cotangent.T, activ, preferred_element_type=jnp.float32)
    gate_up_grad = (
        jnp.stack([act_grad * up_pre * gelu_slope, act_grad * gelu_val], axis=1)
        .astype(jnp.bfloat16)
        .reshape(row_count, 2 * hidden)
    )
    gelu_grad = jnp.dot(hidden_mlp.T, gate_up_grad, preferred_element_type=jnp.float32).reshape(
        feature_count, 2, hidden
    )
    mlp_in_grad = pair_sum(
        jnp.dot(gate_up_grad, gelu_flat.T, preferred_element_type=jnp.float32).astype(
            jnp.bfloat16
        ),
        "tensor",
    )
    mlpgain_grad = jnp.sum(mlp_in_grad * normed_mlp, axis=0)
    resid_grad = out_cotangent.astype(jnp.float32) + norm_back(
        mlp_in_grad, normed_mlp, spread_mlp, mlp_scale
    )
    resid_bf = resid_grad.astype(jnp.bfloat16)
    out_grad = jnp.dot(resid_bf, proj_t, preferred_element_type=jnp.float32).astype(
        jnp.bfloat16
    )
    proj_grad_t = jnp.dot(resid_bf.T, mixed_flat, preferred_element_type=jnp.float32)

    def reduce_pack(packed, members):
        packed = context_gather(
            context_scatter_sum(packed, "context").astype(jnp.bfloat16), "context"
        ).astype(jnp.float32)
        pieces = []
        start = 0
        for member in members:
            pieces.append(packed[:, start : start + member.shape[1]])
            start += member.shape[1]
        return pieces

    mlp_members = [
        mlpgain_grad[:, None],
        gelu_grad.reshape(feature_count, 2 * hidden),
        down_grad_t,
        proj_grad_t,
    ]
    mlp_packed, out_grad = lax.optimization_barrier(
        (jnp.concatenate(mlp_members, axis=1).astype(jnp.bfloat16), out_grad)
    )
    mlp_shard = lax.psum_scatter(mlp_packed, "fsdp", scatter_dimension=0, tiled=True)
    out_heads = out_grad.reshape(row_count, head_count, HD)
    delta = jnp.transpose(
        jnp.sum(out_heads.astype(jnp.float32) * mixed.astype(jnp.float32), axis=2)
    )

    prob_grad = jnp.einsum(
        "qhd,khd->hqk", out_heads, values_heads, preferred_element_type=jnp.float32
    )
    score_grad = (fwd_probs * (prob_grad - delta[:, :, None])).astype(jnp.bfloat16)
    query_grad = (
        jnp.einsum("hqk,khd->qhd", score_grad, keys_heads, preferred_element_type=jnp.float32)
        * 0.125
    )
    key_all = (
        jnp.einsum("hqk,qhd->khd", score_grad, query_bf, preferred_element_type=jnp.float32)
        * 0.125
    ).reshape(group_rows, local_width)
    value_all = jnp.einsum(
        "hqk,qhd->khd", fwd_weights, out_heads, preferred_element_type=jnp.float32
    ).reshape(group_rows, local_width)
    value_partial, mlp_shard = lax.optimization_barrier(
        (value_all.astype(jnp.bfloat16), mlp_shard)
    )
    value_grad = context_scatter_sum(value_partial, "context")
    key_grad = context_scatter_sum(key_all.astype(jnp.bfloat16), "context")
    key_grad = key_grad.reshape(row_count, head_count, HD)
    value_grad = value_grad.reshape(row_count, head_count, HD)
    qkv_rows = (
        jnp.stack(
            [
                rotate_back(query_grad, cosine, sine_tab),
                rotate_back(key_grad, cosine, sine_tab),
                value_grad,
            ],
            axis=1,
        )
        .astype(jnp.bfloat16)
        .reshape(row_count, 3 * local_width)
    )
    qkv_grad = jnp.dot(hidden_attn.T, qkv_rows, preferred_element_type=jnp.float32).reshape(
        feature_count, 3, local_width
    )
    attn_in_grad = pair_sum(
        jnp.dot(qkv_rows, qkv_flat.T, preferred_element_type=jnp.float32).astype(jnp.bfloat16),
        "tensor",
    )
    attngain_grad = jnp.sum(attn_in_grad * normed_attn, axis=0)
    input_grad = resid_grad + norm_back(attn_in_grad, normed_attn, spread_attn, attn_scale)
    attn_members = [attngain_grad[:, None], qkv_grad.reshape(feature_count, 3 * local_width)]
    attn_shard = lax.psum_scatter(
        jnp.concatenate(attn_members, axis=1).astype(jnp.bfloat16),
        "fsdp",
        scatter_dimension=0,
        tiled=True,
    )
    all_pieces = reduce_pack(
        jnp.concatenate([mlp_shard, attn_shard], axis=1), mlp_members + attn_members
    )
    mlp_pieces = all_pieces[: len(mlp_members)]
    attn_pieces = all_pieces[len(mlp_members) :]
    shares = (
        attn_pieces[0][:, 0],
        attn_pieces[1].reshape(shard_rows, 3, local_width),
        mlp_pieces[3].T,
        mlp_pieces[0][:, 0],
        mlp_pieces[1].reshape(shard_rows, 2, hidden),
        mlp_pieces[2].T,
    )
    return (
        block_output,
        input_grad,
        shares[0],
        shares[1],
        shares[2],
        shares[3],
        shares[4],
        shares[5],
    )


def solution(mesh):
    in_specs = (
        P(("fsdp", "context"), None),
        P("fsdp", None),
        P("fsdp"),
        P("fsdp", None, "tensor"),
        P("tensor", "fsdp"),
        P("fsdp"),
        P("fsdp", None, "tensor"),
        P("tensor", "fsdp"),
        P(("fsdp", "context"), None),
    )
    out_specs = (
        P(("fsdp", "context"), None),
        P(("fsdp", "context"), None),
        P("fsdp"),
        P("fsdp", None, "tensor"),
        P("tensor", "fsdp"),
        P("fsdp"),
        P("fsdp", None, "tensor"),
        P("tensor", "fsdp"),
    )
    return jax.shard_map(
        on_device, mesh=mesh, in_specs=in_specs, out_specs=out_specs, check_vma=False
    )
```

```python
import jax
import jax.numpy as jnp
from jax import lax
from jax.sharding import PartitionSpec as P

HD = 64


EPSILON = 1e-05
THETA = 160000.0
MASKED_LOW = -1e30


def layer_norm(values):
    centre = values - jnp.mean(values, axis=-1, keepdims=True)
    spread = lax.rsqrt(jnp.mean(centre * centre, axis=-1, keepdims=True) + EPSILON)
    return (centre * spread, spread)


def norm_back(grad_out, normed, spread, gain):
    scaled = grad_out * gain
    inner = jnp.mean(scaled, axis=-1, keepdims=True) + normed * jnp.mean(
        scaled * normed, axis=-1, keepdims=True
    )
    return spread * (scaled - inner)


def segments_of(row_ids, lengths):
    ends = jnp.cumsum(lengths)
    segment = jnp.sum((row_ids[:, None] >= ends[None, :]).astype(jnp.int32), axis=1)
    starts = ends - lengths
    picked = segment[:, None] == jnp.arange(lengths.shape[0], dtype=jnp.int32)[None, :]
    begin = jnp.sum(jnp.where(picked, starts[None, :], 0), axis=1)
    return (segment, row_ids - begin)


def rope_tables(positions, head_dim):
    half_dim = head_dim // 2
    exponent = jnp.arange(half_dim, dtype=jnp.float32) * (-2.0 / head_dim)
    frequency = jnp.power(jnp.float32(THETA), exponent)
    angles = positions.astype(jnp.float32)[:, None] * frequency[None, :]
    return (jnp.cos(angles)[:, None, :], jnp.sin(angles)[:, None, :])


def rotate(values, cosine, sine_tab):
    half_dim = values.shape[-1] // 2
    lower_half, upper_half = (values[..., :half_dim], values[..., half_dim:])
    return jnp.concatenate(
        [lower_half * cosine - upper_half * sine_tab, upper_half * cosine + lower_half * sine_tab],
        axis=-1,
    )


def rotate_back(grads, cosine, sine_tab):
    half_dim = grads.shape[-1] // 2
    lower_half, upper_half = (grads[..., :half_dim], grads[..., half_dim:])
    return jnp.concatenate(
        [lower_half * cosine + upper_half * sine_tab, upper_half * cosine - lower_half * sine_tab],
        axis=-1,
    )


def gelu_parts(gate_pre):
    normal_cdf = 0.5 * (1.0 + jax.scipy.special.erf(gate_pre * 0.7071067811865476))
    density = jnp.exp(-0.5 * gate_pre * gate_pre) * 0.3989422804014327
    return (gate_pre * normal_cdf, normal_cdf + gate_pre * density)


def pair_sum(values, axis_name):
    if lax.axis_size(axis_name) != 2:
        return lax.psum(values, axis_name)
    other = lax.ppermute(values, axis_name, perm=[(0, 1), (1, 0)])
    return values.astype(jnp.float32) + other.astype(jnp.float32)


def context_gather(values, axis_name):
    count = lax.axis_size(axis_name)
    spread = jnp.broadcast_to(values[None], (count,) + values.shape)
    gathered = lax.all_to_all(spread, axis_name, 0, 0, tiled=True)
    return gathered.reshape((count * values.shape[0],) + values.shape[1:])


def context_scatter_sum(values, axis_name):
    count = lax.axis_size(axis_name)
    rows = values.shape[0] // count
    parts = lax.all_to_all(
        values.reshape((count, rows) + values.shape[1:]), axis_name, 0, 0, tiled=True
    )
    return jnp.sum(parts.astype(jnp.float32), axis=0)


def on_device(
    block_input,
    seq_lengths,
    attn_gain,
    qkv_weight,
    proj_weight,
    mlp_gain,
    gelu_weight,
    down_weight,
    out_cotangent,
):
    row_count = block_input.shape[0]
    feature_count = block_input.shape[1]
    lengths = seq_lengths[0]
    group_rows = row_count * lax.axis_size("context")
    own_first = lax.axis_index("context") * row_count
    own_rows = own_first + jnp.arange(row_count, dtype=jnp.int32)
    own_segment, positions = segments_of(own_rows, lengths)
    inputs_group = context_gather(block_input, "context")
    cosine, sine_tab = rope_tables(positions, HD)
    shard_rows = qkv_weight.shape[0]
    local_width = qkv_weight.shape[2]
    head_count = local_width // HD
    hidden = gelu_weight.shape[2]
    first_pack = lax.all_gather(
        jnp.concatenate(
            [
                qkv_weight.reshape(shard_rows, 3 * local_width),
                attn_gain[:, None],
                mlp_gain[:, None],
            ],
            axis=1,
        ),
        "fsdp",
        axis=0,
        tiled=True,
    )
    second_pack = lax.all_gather(
        jnp.concatenate(
            [proj_weight.T, gelu_weight.reshape(shard_rows, 2 * hidden), down_weight.T], axis=1
        ),
        "fsdp",
        axis=0,
        tiled=True,
    )
    qkv_flat = first_pack[:, : 3 * local_width]
    attn_full = first_pack[:, 3 * local_width]
    mlp_full = first_pack[:, 3 * local_width + 1]
    proj_t = second_pack[:, :local_width]
    gelu_flat = second_pack[:, local_width : local_width + 2 * hidden]
    down_t = second_pack[:, local_width + 2 * hidden :]
    attn_scale = attn_full.astype(jnp.float32)
    mlp_scale = mlp_full.astype(jnp.float32)
    inputs = block_input.astype(jnp.float32)
    normed_attn, spread_attn = layer_norm(inputs)
    hidden_attn = (normed_attn * attn_scale).astype(jnp.bfloat16)
    query_bf = rotate(
        jnp.dot(
            hidden_attn, qkv_flat[:, :local_width], preferred_element_type=jnp.float32
        ).reshape(row_count, head_count, HD),
        cosine,
        sine_tab,
    ).astype(jnp.bfloat16)
    group_normed, unused_spread = layer_norm(inputs_group.astype(jnp.float32))
    hidden_group = (group_normed * attn_scale).astype(jnp.bfloat16)
    group_segment, group_pos = segments_of(jnp.arange(group_rows, dtype=jnp.int32), lengths)
    group_cos, group_sin = rope_tables(group_pos, HD)
    kv_projected = jnp.dot(
        hidden_group, qkv_flat[:, local_width:], preferred_element_type=jnp.float32
    ).reshape(group_rows, 2, head_count, HD)
    keys_heads = rotate(kv_projected[:, 0], group_cos, group_sin).astype(jnp.bfloat16)
    values_heads = kv_projected[:, 1].astype(jnp.bfloat16)
    same_group = (own_segment[:, None] == group_segment[None, :])[None]
    fwd_scores = (
        jnp.einsum("qhd,khd->hqk", query_bf, keys_heads, preferred_element_type=jnp.float32) * 0.125
    )
    row_max = jnp.max(jnp.where(same_group, fwd_scores, MASKED_LOW), axis=2)
    denom_sum = jnp.sum(
        jnp.where(same_group, jnp.exp(fwd_scores - row_max[:, :, None]), 0.0), axis=2
    )
    log_total = row_max + jnp.log(denom_sum)
    fwd_probs = jnp.where(same_group, jnp.exp(fwd_scores - log_total[:, :, None]), 0.0)
    fwd_weights = fwd_probs.astype(jnp.bfloat16)
    mixed = jnp.einsum(
        "hqk,khd->qhd", fwd_weights, values_heads, preferred_element_type=jnp.float32
    ).astype(jnp.bfloat16)
    mixed_flat = mixed.reshape(row_count, local_width)
    attn_part = jnp.dot(mixed_flat, proj_t.T, preferred_element_type=jnp.float32)
    residual = inputs + pair_sum(attn_part.astype(jnp.bfloat16), "tensor")
    normed_mlp, spread_mlp = layer_norm(residual)
    hidden_mlp = (normed_mlp * mlp_scale).astype(jnp.bfloat16)
    gate_up = jnp.dot(hidden_mlp, gelu_flat, preferred_element_type=jnp.float32).reshape(
        row_count, 2, hidden
    )
    gate_pre, up_pre = (gate_up[:, 0], gate_up[:, 1])
    gelu_val, gelu_slope = gelu_parts(gate_pre)
    activ = (gelu_val * up_pre).astype(jnp.bfloat16)
    mlp_part = jnp.dot(activ, down_t.T, preferred_element_type=jnp.float32)
    block_output = (
        residual + pair_sum(mlp_part.astype(jnp.bfloat16), "tensor")
    ).astype(jnp.bfloat16)
    act_grad = jnp.dot(out_cotangent, down_t, preferred_element_type=jnp.float32)
    down_grad_t = jnp.dot(out_cotangent.T, activ, preferred_element_type=jnp.float32)
    gate_up_grad = (
        jnp.stack([act_grad * up_pre * gelu_slope, act_grad * gelu_val], axis=1)
        .astype(jnp.bfloat16)
        .reshape(row_count, 2 * hidden)
    )
    gelu_grad = jnp.dot(hidden_mlp.T, gate_up_grad, preferred_element_type=jnp.float32).reshape(
        feature_count, 2, hidden
    )
    mlp_in_grad = pair_sum(
        jnp.dot(gate_up_grad, gelu_flat.T, preferred_element_type=jnp.float32).astype(
            jnp.bfloat16
        ),
        "tensor",
    )
    mlpgain_grad = jnp.sum(mlp_in_grad * normed_mlp, axis=0)
    resid_grad = out_cotangent.astype(jnp.float32) + norm_back(
        mlp_in_grad, normed_mlp, spread_mlp, mlp_scale
    )
    resid_bf = resid_grad.astype(jnp.bfloat16)
    out_grad = jnp.dot(resid_bf, proj_t, preferred_element_type=jnp.float32).astype(
        jnp.bfloat16
    )
    proj_grad_t = jnp.dot(resid_bf.T, mixed_flat, preferred_element_type=jnp.float32)

    def reduce_pack(packed, members):
        packed = context_gather(
            context_scatter_sum(packed, "context").astype(jnp.bfloat16), "context"
        ).astype(jnp.float32)
        pieces = []
        start = 0
        for member in members:
            pieces.append(packed[:, start : start + member.shape[1]])
            start += member.shape[1]
        return pieces

    mlp_members = [
        mlpgain_grad[:, None],
        gelu_grad.reshape(feature_count, 2 * hidden),
        down_grad_t,
        proj_grad_t,
    ]
    mlp_packed, out_grad = lax.optimization_barrier(
        (jnp.concatenate(mlp_members, axis=1).astype(jnp.bfloat16), out_grad)
    )
    mlp_shard = lax.psum_scatter(mlp_packed, "fsdp", scatter_dimension=0, tiled=True)
    out_heads = out_grad.reshape(row_count, head_count, HD)
    delta = jnp.transpose(
        jnp.sum(out_heads.astype(jnp.float32) * mixed.astype(jnp.float32), axis=2)
    )

    prob_grad = jnp.einsum(
        "qhd,khd->hqk", out_heads, values_heads, preferred_element_type=jnp.float32
    )
    score_grad = (fwd_probs * (prob_grad - delta[:, :, None])).astype(jnp.bfloat16)
    query_grad = (
        jnp.einsum("hqk,khd->qhd", score_grad, keys_heads, preferred_element_type=jnp.float32)
        * 0.125
    )
    key_all = (
        jnp.einsum("hqk,qhd->khd", score_grad, query_bf, preferred_element_type=jnp.float32)
        * 0.125
    ).reshape(group_rows, local_width)
    value_all = jnp.einsum(
        "hqk,qhd->khd", fwd_weights, out_heads, preferred_element_type=jnp.float32
    ).reshape(group_rows, local_width)
    value_partial, mlp_shard = lax.optimization_barrier(
        (value_all.astype(jnp.bfloat16), mlp_shard)
    )
    value_grad = context_scatter_sum(value_partial, "context")
    mlp_pieces = reduce_pack(mlp_shard, mlp_members)
    key_partial, mlp_pieces = lax.optimization_barrier(
        (key_all.astype(jnp.bfloat16), mlp_pieces)
    )
    key_grad = context_scatter_sum(key_partial, "context")
    key_grad = key_grad.reshape(row_count, head_count, HD)
    value_grad = value_grad.reshape(row_count, head_count, HD)
    qkv_rows = (
        jnp.stack(
            [
                rotate_back(query_grad, cosine, sine_tab),
                rotate_back(key_grad, cosine, sine_tab),
                value_grad,
            ],
            axis=1,
        )
        .astype(jnp.bfloat16)
        .reshape(row_count, 3 * local_width)
    )
    qkv_grad = jnp.dot(hidden_attn.T, qkv_rows, preferred_element_type=jnp.float32).reshape(
        feature_count, 3, local_width
    )
    attn_in_grad = pair_sum(
        jnp.dot(qkv_rows, qkv_flat.T, preferred_element_type=jnp.float32).astype(jnp.bfloat16),
        "tensor",
    )
    attngain_grad = jnp.sum(attn_in_grad * normed_attn, axis=0)
    input_grad = resid_grad + norm_back(attn_in_grad, normed_attn, spread_attn, attn_scale)
    attn_members = [attngain_grad[:, None], qkv_grad.reshape(feature_count, 3 * local_width)]
    attn_pieces = reduce_pack(
        lax.psum_scatter(
            jnp.concatenate(attn_members, axis=1).astype(jnp.bfloat16),
            "fsdp",
            scatter_dimension=0,
            tiled=True,
        ),
        attn_members,
    )
    shares = (
        attn_pieces[0][:, 0],
        attn_pieces[1].reshape(shard_rows, 3, local_width),
        mlp_pieces[3].T,
        mlp_pieces[0][:, 0],
        mlp_pieces[1].reshape(shard_rows, 2, hidden),
        mlp_pieces[2].T,
    )
    return (
        block_output,
        input_grad,
        shares[0],
        shares[1],
        shares[2],
        shares[3],
        shares[4],
        shares[5],
    )


def solution(mesh):
    in_specs = (
        P(("fsdp", "context"), None),
        P("fsdp", None),
        P("fsdp"),
        P("fsdp", None, "tensor"),
        P("tensor", "fsdp"),
        P("fsdp"),
        P("fsdp", None, "tensor"),
        P("tensor", "fsdp"),
        P(("fsdp", "context"), None),
    )
    out_specs = (
        P(("fsdp", "context"), None),
        P(("fsdp", "context"), None),
        P("fsdp"),
        P("fsdp", None, "tensor"),
        P("tensor", "fsdp"),
        P("fsdp"),
        P("fsdp", None, "tensor"),
        P("tensor", "fsdp"),
    )
    return jax.shard_map(
        on_device, mesh=mesh, in_specs=in_specs, out_specs=out_specs, check_vma=False
    )
```

```python
import jax
import jax.numpy as jnp
from jax import lax
from jax.sharding import PartitionSpec as P

HD = 64


EPSILON = 1e-05
THETA = 160000.0
MASKED_LOW = -1e30


def layer_norm(values):
    centre = values - jnp.mean(values, axis=-1, keepdims=True)
    spread = lax.rsqrt(jnp.mean(centre * centre, axis=-1, keepdims=True) + EPSILON)
    return (centre * spread, spread)


def norm_back(grad_out, normed, spread, gain):
    scaled = grad_out * gain
    inner = jnp.mean(scaled, axis=-1, keepdims=True) + normed * jnp.mean(
        scaled * normed, axis=-1, keepdims=True
    )
    return spread * (scaled - inner)


def segments_of(row_ids, lengths):
    ends = jnp.cumsum(lengths)
    segment = jnp.sum((row_ids[:, None] >= ends[None, :]).astype(jnp.int32), axis=1)
    starts = ends - lengths
    picked = segment[:, None] == jnp.arange(lengths.shape[0], dtype=jnp.int32)[None, :]
    begin = jnp.sum(jnp.where(picked, starts[None, :], 0), axis=1)
    return (segment, row_ids - begin)


def rope_tables(positions, head_dim):
    half_dim = head_dim // 2
    exponent = jnp.arange(half_dim, dtype=jnp.float32) * (-2.0 / head_dim)
    frequency = jnp.power(jnp.float32(THETA), exponent)
    angles = positions.astype(jnp.float32)[:, None] * frequency[None, :]
    return (jnp.cos(angles)[:, None, :], jnp.sin(angles)[:, None, :])


def rotate(values, cosine, sine_tab):
    half_dim = values.shape[-1] // 2
    lower_half, upper_half = (values[..., :half_dim], values[..., half_dim:])
    return jnp.concatenate(
        [lower_half * cosine - upper_half * sine_tab, upper_half * cosine + lower_half * sine_tab],
        axis=-1,
    )


def rotate_back(grads, cosine, sine_tab):
    half_dim = grads.shape[-1] // 2
    lower_half, upper_half = (grads[..., :half_dim], grads[..., half_dim:])
    return jnp.concatenate(
        [lower_half * cosine + upper_half * sine_tab, upper_half * cosine - lower_half * sine_tab],
        axis=-1,
    )


def gelu_parts(gate_pre):
    normal_cdf = 0.5 * (1.0 + jax.scipy.special.erf(gate_pre * 0.7071067811865476))
    density = jnp.exp(-0.5 * gate_pre * gate_pre) * 0.3989422804014327
    return (gate_pre * normal_cdf, normal_cdf + gate_pre * density)


def pair_sum(values, axis_name):
    if lax.axis_size(axis_name) != 2:
        return lax.psum(values, axis_name)
    other = lax.ppermute(values, axis_name, perm=[(0, 1), (1, 0)])
    return values.astype(jnp.float32) + other.astype(jnp.float32)


def context_gather(values, axis_name):
    count = lax.axis_size(axis_name)
    spread = jnp.broadcast_to(values[None], (count,) + values.shape)
    gathered = lax.all_to_all(spread, axis_name, 0, 0, tiled=True)
    return gathered.reshape((count * values.shape[0],) + values.shape[1:])


def context_scatter_sum(values, axis_name):
    count = lax.axis_size(axis_name)
    rows = values.shape[0] // count
    parts = lax.all_to_all(
        values.reshape((count, rows) + values.shape[1:]), axis_name, 0, 0, tiled=True
    )
    return jnp.sum(parts.astype(jnp.float32), axis=0)


def on_device(
    block_input,
    seq_lengths,
    attn_gain,
    qkv_weight,
    proj_weight,
    mlp_gain,
    gelu_weight,
    down_weight,
    out_cotangent,
):
    row_count = block_input.shape[0]
    feature_count = block_input.shape[1]
    lengths = seq_lengths[0]
    group_rows = row_count * lax.axis_size("context")
    own_first = lax.axis_index("context") * row_count
    own_rows = own_first + jnp.arange(row_count, dtype=jnp.int32)
    own_segment, positions = segments_of(own_rows, lengths)
    inputs_group = context_gather(block_input, "context")
    cosine, sine_tab = rope_tables(positions, HD)
    shard_rows = qkv_weight.shape[0]
    local_width = qkv_weight.shape[2]
    head_count = local_width // HD
    hidden = gelu_weight.shape[2]
    first_pack = lax.all_gather(
        jnp.concatenate(
            [
                qkv_weight.reshape(shard_rows, 3 * local_width),
                attn_gain[:, None],
                mlp_gain[:, None],
            ],
            axis=1,
        ),
        "fsdp",
        axis=0,
        tiled=True,
    )
    second_pack = lax.all_gather(
        jnp.concatenate(
            [proj_weight.T, gelu_weight.reshape(shard_rows, 2 * hidden), down_weight.T], axis=1
        ),
        "fsdp",
        axis=0,
        tiled=True,
    )
    qkv_flat = first_pack[:, : 3 * local_width]
    attn_full = first_pack[:, 3 * local_width]
    mlp_full = first_pack[:, 3 * local_width + 1]
    proj_t = second_pack[:, :local_width]
    gelu_flat = second_pack[:, local_width : local_width + 2 * hidden]
    down_t = second_pack[:, local_width + 2 * hidden :]
    attn_scale = attn_full.astype(jnp.float32)
    mlp_scale = mlp_full.astype(jnp.float32)
    inputs = block_input.astype(jnp.float32)
    normed_attn, spread_attn = layer_norm(inputs)
    hidden_attn = (normed_attn * attn_scale).astype(jnp.bfloat16)
    query_bf = rotate(
        jnp.dot(
            hidden_attn, qkv_flat[:, :local_width], preferred_element_type=jnp.float32
        ).reshape(row_count, head_count, HD),
        cosine,
        sine_tab,
    ).astype(jnp.bfloat16)
    group_normed, unused_spread = layer_norm(inputs_group.astype(jnp.float32))
    hidden_group = (group_normed * attn_scale).astype(jnp.bfloat16)
    group_segment, group_pos = segments_of(jnp.arange(group_rows, dtype=jnp.int32), lengths)
    group_cos, group_sin = rope_tables(group_pos, HD)
    kv_projected = jnp.dot(
        hidden_group, qkv_flat[:, local_width:], preferred_element_type=jnp.float32
    ).reshape(group_rows, 2, head_count, HD)
    keys_heads = rotate(kv_projected[:, 0], group_cos, group_sin).astype(jnp.bfloat16)
    values_heads = kv_projected[:, 1].astype(jnp.bfloat16)
    same_group = (own_segment[:, None] == group_segment[None, :])[None]
    fwd_scores = (
        jnp.einsum("qhd,khd->hqk", query_bf, keys_heads, preferred_element_type=jnp.float32) * 0.125
    )
    row_max = jnp.max(jnp.where(same_group, fwd_scores, MASKED_LOW), axis=2)
    denom_sum = jnp.sum(
        jnp.where(same_group, jnp.exp(fwd_scores - row_max[:, :, None]), 0.0), axis=2
    )
    log_total = row_max + jnp.log(denom_sum)
    fwd_probs = jnp.where(same_group, jnp.exp(fwd_scores - log_total[:, :, None]), 0.0)
    fwd_weights = fwd_probs.astype(jnp.bfloat16)
    mixed = jnp.einsum(
        "hqk,khd->qhd", fwd_weights, values_heads, preferred_element_type=jnp.float32
    ).astype(jnp.bfloat16)
    mixed_flat = mixed.reshape(row_count, local_width)
    attn_part = jnp.dot(mixed_flat, proj_t.T, preferred_element_type=jnp.float32)
    residual = inputs + pair_sum(attn_part.astype(jnp.bfloat16), "tensor")
    normed_mlp, spread_mlp = layer_norm(residual)
    hidden_mlp = (normed_mlp * mlp_scale).astype(jnp.bfloat16)
    gate_up = jnp.dot(hidden_mlp, gelu_flat, preferred_element_type=jnp.float32).reshape(
        row_count, 2, hidden
    )
    gate_pre, up_pre = (gate_up[:, 0], gate_up[:, 1])
    gelu_val, gelu_slope = gelu_parts(gate_pre)
    activ = (gelu_val * up_pre).astype(jnp.bfloat16)
    mlp_part = jnp.dot(activ, down_t.T, preferred_element_type=jnp.float32)
    block_output = (
        residual + pair_sum(mlp_part.astype(jnp.bfloat16), "tensor")
    ).astype(jnp.bfloat16)
    act_grad = jnp.dot(out_cotangent, down_t, preferred_element_type=jnp.float32)
    down_grad_t = jnp.dot(out_cotangent.T, activ, preferred_element_type=jnp.float32)
    gate_up_grad = (
        jnp.stack([act_grad * up_pre * gelu_slope, act_grad * gelu_val], axis=1)
        .astype(jnp.bfloat16)
        .reshape(row_count, 2 * hidden)
    )
    gelu_grad = jnp.dot(hidden_mlp.T, gate_up_grad, preferred_element_type=jnp.float32).reshape(
        feature_count, 2, hidden
    )
    mlp_in_grad = pair_sum(
        jnp.dot(gate_up_grad, gelu_flat.T, preferred_element_type=jnp.float32).astype(
            jnp.bfloat16
        ),
        "tensor",
    )
    mlpgain_grad = jnp.sum(mlp_in_grad * normed_mlp, axis=0)
    resid_grad = out_cotangent.astype(jnp.float32) + norm_back(
        mlp_in_grad, normed_mlp, spread_mlp, mlp_scale
    )
    resid_bf = resid_grad.astype(jnp.bfloat16)
    out_grad = jnp.dot(resid_bf, proj_t, preferred_element_type=jnp.float32).astype(
        jnp.bfloat16
    )
    proj_grad_t = jnp.dot(resid_bf.T, mixed_flat, preferred_element_type=jnp.float32)

    def reduce_pack(packed, members):
        packed = context_gather(
            context_scatter_sum(packed, "context").astype(jnp.bfloat16), "context"
        ).astype(jnp.float32)
        pieces = []
        start = 0
        for member in members:
            pieces.append(packed[:, start : start + member.shape[1]])
            start += member.shape[1]
        return pieces

    mlp_members = [
        mlpgain_grad[:, None],
        gelu_grad.reshape(feature_count, 2 * hidden),
        down_grad_t,
        proj_grad_t,
    ]
    mlp_packed, out_grad = lax.optimization_barrier(
        (jnp.concatenate(mlp_members, axis=1).astype(jnp.bfloat16), out_grad)
    )
    mlp_shard = lax.psum_scatter(mlp_packed, "fsdp", scatter_dimension=0, tiled=True)
    out_heads = out_grad.reshape(row_count, head_count, HD)
    delta = jnp.transpose(
        jnp.sum(out_heads.astype(jnp.float32) * mixed.astype(jnp.float32), axis=2)
    )

    prob_grad = jnp.einsum(
        "qhd,khd->hqk", out_heads, values_heads, preferred_element_type=jnp.float32
    )
    score_grad = (fwd_probs * (prob_grad - delta[:, :, None])).astype(jnp.bfloat16)
    query_grad = (
        jnp.einsum("hqk,khd->qhd", score_grad, keys_heads, preferred_element_type=jnp.float32)
        * 0.125
    )
    key_all = (
        jnp.einsum("hqk,qhd->khd", score_grad, query_bf, preferred_element_type=jnp.float32)
        * 0.125
    ).reshape(group_rows, local_width)
    value_all = jnp.einsum(
        "hqk,qhd->khd", fwd_weights, out_heads, preferred_element_type=jnp.float32
    ).reshape(group_rows, local_width)
    value_grad = context_scatter_sum(value_all.astype(jnp.bfloat16), "context")
    key_partial, mlp_shard = lax.optimization_barrier((key_all.astype(jnp.bfloat16), mlp_shard))
    key_grad = context_scatter_sum(key_partial, "context")
    mlp_pieces = reduce_pack(mlp_shard, mlp_members)
    key_grad = key_grad.reshape(row_count, head_count, HD)
    value_grad = value_grad.reshape(row_count, head_count, HD)
    qkv_rows = (
        jnp.stack(
            [
                rotate_back(query_grad, cosine, sine_tab),
                rotate_back(key_grad, cosine, sine_tab),
                value_grad,
            ],
            axis=1,
        )
        .astype(jnp.bfloat16)
        .reshape(row_count, 3 * local_width)
    )
    qkv_grad = jnp.dot(hidden_attn.T, qkv_rows, preferred_element_type=jnp.float32).reshape(
        feature_count, 3, local_width
    )
    attn_in_grad = pair_sum(
        jnp.dot(qkv_rows, qkv_flat.T, preferred_element_type=jnp.float32).astype(jnp.bfloat16),
        "tensor",
    )
    attngain_grad = jnp.sum(attn_in_grad * normed_attn, axis=0)
    input_grad = resid_grad + norm_back(attn_in_grad, normed_attn, spread_attn, attn_scale)
    attn_members = [attngain_grad[:, None], qkv_grad.reshape(feature_count, 3 * local_width)]
    attn_pieces = reduce_pack(
        lax.psum_scatter(
            jnp.concatenate(attn_members, axis=1).astype(jnp.bfloat16),
            "fsdp",
            scatter_dimension=0,
            tiled=True,
        ),
        attn_members,
    )
    shares = (
        attn_pieces[0][:, 0],
        attn_pieces[1].reshape(shard_rows, 3, local_width),
        mlp_pieces[3].T,
        mlp_pieces[0][:, 0],
        mlp_pieces[1].reshape(shard_rows, 2, hidden),
        mlp_pieces[2].T,
    )
    return (
        block_output,
        input_grad,
        shares[0],
        shares[1],
        shares[2],
        shares[3],
        shares[4],
        shares[5],
    )


def solution(mesh):
    in_specs = (
        P(("fsdp", "context"), None),
        P("fsdp", None),
        P("fsdp"),
        P("fsdp", None, "tensor"),
        P("tensor", "fsdp"),
        P("fsdp"),
        P("fsdp", None, "tensor"),
        P("tensor", "fsdp"),
        P(("fsdp", "context"), None),
    )
    out_specs = (
        P(("fsdp", "context"), None),
        P(("fsdp", "context"), None),
        P("fsdp"),
        P("fsdp", None, "tensor"),
        P("tensor", "fsdp"),
        P("fsdp"),
        P("fsdp", None, "tensor"),
        P("tensor", "fsdp"),
    )
    return jax.shard_map(
        on_device, mesh=mesh, in_specs=in_specs, out_specs=out_specs, check_vma=False
    )
```

```python
import jax
import jax.numpy as jnp
from jax import lax
from jax.sharding import PartitionSpec as P

HD = 64


EPSILON = 1e-05
THETA = 160000.0
MASKED_LOW = -1e30


def layer_norm(values):
    centre = values - jnp.mean(values, axis=-1, keepdims=True)
    spread = lax.rsqrt(jnp.mean(centre * centre, axis=-1, keepdims=True) + EPSILON)
    return (centre * spread, spread)


def norm_back(grad_out, normed, spread, gain):
    scaled = grad_out * gain
    inner = jnp.mean(scaled, axis=-1, keepdims=True) + normed * jnp.mean(
        scaled * normed, axis=-1, keepdims=True
    )
    return spread * (scaled - inner)


def segments_of(row_ids, lengths):
    ends = jnp.cumsum(lengths)
    segment = jnp.sum((row_ids[:, None] >= ends[None, :]).astype(jnp.int32), axis=1)
    starts = ends - lengths
    picked = segment[:, None] == jnp.arange(lengths.shape[0], dtype=jnp.int32)[None, :]
    begin = jnp.sum(jnp.where(picked, starts[None, :], 0), axis=1)
    return (segment, row_ids - begin)


def rope_tables(positions, head_dim):
    half_dim = head_dim // 2
    exponent = jnp.arange(half_dim, dtype=jnp.float32) * (-2.0 / head_dim)
    frequency = jnp.power(jnp.float32(THETA), exponent)
    angles = positions.astype(jnp.float32)[:, None] * frequency[None, :]
    return (jnp.cos(angles)[:, None, :], jnp.sin(angles)[:, None, :])


def rotate(values, cosine, sine_tab):
    half_dim = values.shape[-1] // 2
    lower_half, upper_half = (values[..., :half_dim], values[..., half_dim:])
    return jnp.concatenate(
        [lower_half * cosine - upper_half * sine_tab, upper_half * cosine + lower_half * sine_tab],
        axis=-1,
    )


def rotate_back(grads, cosine, sine_tab):
    half_dim = grads.shape[-1] // 2
    lower_half, upper_half = (grads[..., :half_dim], grads[..., half_dim:])
    return jnp.concatenate(
        [lower_half * cosine + upper_half * sine_tab, upper_half * cosine - lower_half * sine_tab],
        axis=-1,
    )


def gelu_parts(gate_pre):
    normal_cdf = 0.5 * (1.0 + jax.scipy.special.erf(gate_pre * 0.7071067811865476))
    density = jnp.exp(-0.5 * gate_pre * gate_pre) * 0.3989422804014327
    return (gate_pre * normal_cdf, normal_cdf + gate_pre * density)


def pair_sum(values, axis_name):
    if lax.axis_size(axis_name) != 2:
        return lax.psum(values, axis_name)
    other = lax.ppermute(values, axis_name, perm=[(0, 1), (1, 0)])
    return values.astype(jnp.float32) + other.astype(jnp.float32)


def context_gather(values, axis_name):
    count = lax.axis_size(axis_name)
    spread = jnp.broadcast_to(values[None], (count,) + values.shape)
    gathered = lax.all_to_all(spread, axis_name, 0, 0, tiled=True)
    return gathered.reshape((count * values.shape[0],) + values.shape[1:])


def context_scatter_sum(values, axis_name):
    count = lax.axis_size(axis_name)
    rows = values.shape[0] // count
    parts = lax.all_to_all(
        values.reshape((count, rows) + values.shape[1:]), axis_name, 0, 0, tiled=True
    )
    return jnp.sum(parts.astype(jnp.float32), axis=0)


def on_device(
    block_input,
    seq_lengths,
    attn_gain,
    qkv_weight,
    proj_weight,
    mlp_gain,
    gelu_weight,
    down_weight,
    out_cotangent,
):
    row_count = block_input.shape[0]
    feature_count = block_input.shape[1]
    lengths = seq_lengths[0]
    group_rows = row_count * lax.axis_size("context")
    own_first = lax.axis_index("context") * row_count
    own_rows = own_first + jnp.arange(row_count, dtype=jnp.int32)
    own_segment, positions = segments_of(own_rows, lengths)
    inputs_group = context_gather(block_input, "context")
    cosine, sine_tab = rope_tables(positions, HD)
    shard_rows = qkv_weight.shape[0]
    local_width = qkv_weight.shape[2]
    head_count = local_width // HD
    hidden = gelu_weight.shape[2]
    first_pack = lax.all_gather(
        jnp.concatenate(
            [
                qkv_weight.reshape(shard_rows, 3 * local_width),
                attn_gain[:, None],
                mlp_gain[:, None],
            ],
            axis=1,
        ),
        "fsdp",
        axis=0,
        tiled=True,
    )
    second_pack = lax.all_gather(
        jnp.concatenate(
            [proj_weight.T, gelu_weight.reshape(shard_rows, 2 * hidden), down_weight.T], axis=1
        ),
        "fsdp",
        axis=0,
        tiled=True,
    )
    qkv_flat = first_pack[:, : 3 * local_width]
    attn_full = first_pack[:, 3 * local_width]
    mlp_full = first_pack[:, 3 * local_width + 1]
    proj_t = second_pack[:, :local_width]
    gelu_flat = second_pack[:, local_width : local_width + 2 * hidden]
    down_t = second_pack[:, local_width + 2 * hidden :]
    attn_scale = attn_full.astype(jnp.float32)
    mlp_scale = mlp_full.astype(jnp.float32)
    inputs = block_input.astype(jnp.float32)
    normed_attn, spread_attn = layer_norm(inputs)
    hidden_attn = (normed_attn * attn_scale).astype(jnp.bfloat16)
    query_bf = rotate(
        jnp.dot(
            hidden_attn, qkv_flat[:, :local_width], preferred_element_type=jnp.float32
        ).reshape(row_count, head_count, HD),
        cosine,
        sine_tab,
    ).astype(jnp.bfloat16)
    group_normed, unused_spread = layer_norm(inputs_group.astype(jnp.float32))
    hidden_group = (group_normed * attn_scale).astype(jnp.bfloat16)
    group_segment, group_pos = segments_of(jnp.arange(group_rows, dtype=jnp.int32), lengths)
    group_cos, group_sin = rope_tables(group_pos, HD)
    kv_projected = jnp.dot(
        hidden_group, qkv_flat[:, local_width:], preferred_element_type=jnp.float32
    ).reshape(group_rows, 2, head_count, HD)
    keys_heads = rotate(kv_projected[:, 0], group_cos, group_sin).astype(jnp.bfloat16)
    values_heads = kv_projected[:, 1].astype(jnp.bfloat16)
    same_group = (own_segment[:, None] == group_segment[None, :])[None]
    fwd_scores = (
        jnp.einsum("qhd,khd->hqk", query_bf, keys_heads, preferred_element_type=jnp.float32) * 0.125
    )
    row_max = jnp.max(jnp.where(same_group, fwd_scores, MASKED_LOW), axis=2)
    denom_sum = jnp.sum(
        jnp.where(same_group, jnp.exp(fwd_scores - row_max[:, :, None]), 0.0), axis=2
    )
    log_total = row_max + jnp.log(denom_sum)
    fwd_probs = jnp.where(same_group, jnp.exp(fwd_scores - log_total[:, :, None]), 0.0)
    fwd_weights = fwd_probs.astype(jnp.bfloat16)
    mixed = jnp.einsum(
        "hqk,khd->qhd", fwd_weights, values_heads, preferred_element_type=jnp.float32
    ).astype(jnp.bfloat16)
    mixed_flat = mixed.reshape(row_count, local_width)
    attn_part = jnp.dot(mixed_flat, proj_t.T, preferred_element_type=jnp.float32)
    residual = inputs + pair_sum(attn_part.astype(jnp.bfloat16), "tensor")
    normed_mlp, spread_mlp = layer_norm(residual)
    hidden_mlp = (normed_mlp * mlp_scale).astype(jnp.bfloat16)
    gate_up = jnp.dot(hidden_mlp, gelu_flat, preferred_element_type=jnp.float32).reshape(
        row_count, 2, hidden
    )
    gate_pre, up_pre = (gate_up[:, 0], gate_up[:, 1])
    gelu_val, gelu_slope = gelu_parts(gate_pre)
    activ = (gelu_val * up_pre).astype(jnp.bfloat16)
    mlp_part = jnp.dot(activ, down_t.T, preferred_element_type=jnp.float32)
    block_output = (
        residual + pair_sum(mlp_part.astype(jnp.bfloat16), "tensor")
    ).astype(jnp.bfloat16)
    act_grad = jnp.dot(out_cotangent, down_t, preferred_element_type=jnp.float32)
    down_grad_t = jnp.dot(out_cotangent.T, activ, preferred_element_type=jnp.float32)
    gate_up_grad = (
        jnp.stack([act_grad * up_pre * gelu_slope, act_grad * gelu_val], axis=1)
        .astype(jnp.bfloat16)
        .reshape(row_count, 2 * hidden)
    )
    gelu_grad = jnp.dot(hidden_mlp.T, gate_up_grad, preferred_element_type=jnp.float32).reshape(
        feature_count, 2, hidden
    )
    mlp_in_grad = pair_sum(
        jnp.dot(gate_up_grad, gelu_flat.T, preferred_element_type=jnp.float32).astype(
            jnp.bfloat16
        ),
        "tensor",
    )
    mlpgain_grad = jnp.sum(mlp_in_grad * normed_mlp, axis=0)
    resid_grad = out_cotangent.astype(jnp.float32) + norm_back(
        mlp_in_grad, normed_mlp, spread_mlp, mlp_scale
    )
    resid_bf = resid_grad.astype(jnp.bfloat16)
    out_grad = jnp.dot(resid_bf, proj_t, preferred_element_type=jnp.float32).astype(
        jnp.bfloat16
    )
    proj_grad_t = jnp.dot(resid_bf.T, mixed_flat, preferred_element_type=jnp.float32)

    mlp_members = [
        mlpgain_grad[:, None],
        gelu_grad.reshape(feature_count, 2 * hidden),
        down_grad_t,
        proj_grad_t,
    ]
    mlp_packed, out_grad = lax.optimization_barrier(
        (jnp.concatenate(mlp_members, axis=1).astype(jnp.bfloat16), out_grad)
    )
    mlp_shard = lax.psum_scatter(mlp_packed, "fsdp", scatter_dimension=0, tiled=True)
    out_heads = out_grad.reshape(row_count, head_count, HD)
    delta = jnp.transpose(
        jnp.sum(out_heads.astype(jnp.float32) * mixed.astype(jnp.float32), axis=2)
    )

    prob_grad = jnp.einsum(
        "qhd,khd->hqk", out_heads, values_heads, preferred_element_type=jnp.float32
    )
    score_grad = (fwd_probs * (prob_grad - delta[:, :, None])).astype(jnp.bfloat16)
    query_grad = (
        jnp.einsum("hqk,khd->qhd", score_grad, keys_heads, preferred_element_type=jnp.float32)
        * 0.125
    )
    key_all = (
        jnp.einsum("hqk,qhd->khd", score_grad, query_bf, preferred_element_type=jnp.float32)
        * 0.125
    ).reshape(group_rows, local_width)
    value_all = jnp.einsum(
        "hqk,qhd->khd", fwd_weights, out_heads, preferred_element_type=jnp.float32
    ).reshape(group_rows, local_width)
    value_partial, mlp_shard = lax.optimization_barrier(
        (value_all.astype(jnp.bfloat16), mlp_shard)
    )
    value_grad = context_scatter_sum(value_partial, "context")
    key_grad = context_scatter_sum(key_all.astype(jnp.bfloat16), "context")
    mlp_chunk = context_scatter_sum(mlp_shard, "context").astype(jnp.bfloat16)
    key_grad = key_grad.reshape(row_count, head_count, HD)
    value_grad = value_grad.reshape(row_count, head_count, HD)
    qkv_rows = (
        jnp.stack(
            [
                rotate_back(query_grad, cosine, sine_tab),
                rotate_back(key_grad, cosine, sine_tab),
                value_grad,
            ],
            axis=1,
        )
        .astype(jnp.bfloat16)
        .reshape(row_count, 3 * local_width)
    )
    qkv_grad = jnp.dot(hidden_attn.T, qkv_rows, preferred_element_type=jnp.float32).reshape(
        feature_count, 3, local_width
    )
    attn_in_grad = pair_sum(
        jnp.dot(qkv_rows, qkv_flat.T, preferred_element_type=jnp.float32).astype(jnp.bfloat16),
        "tensor",
    )
    attngain_grad = jnp.sum(attn_in_grad * normed_attn, axis=0)
    input_grad = resid_grad + norm_back(attn_in_grad, normed_attn, spread_attn, attn_scale)
    attn_members = [attngain_grad[:, None], qkv_grad.reshape(feature_count, 3 * local_width)]
    attn_chunk = context_scatter_sum(
        lax.psum_scatter(
            jnp.concatenate(attn_members, axis=1).astype(jnp.bfloat16),
            "fsdp",
            scatter_dimension=0,
            tiled=True,
        ),
        "context",
    ).astype(jnp.bfloat16)
    summed = context_gather(
        jnp.concatenate([mlp_chunk, attn_chunk], axis=1), "context"
    ).astype(jnp.float32)
    all_pieces = []
    start = 0
    for member in mlp_members + attn_members:
        all_pieces.append(summed[:, start : start + member.shape[1]])
        start += member.shape[1]
    mlp_pieces = all_pieces[: len(mlp_members)]
    attn_pieces = all_pieces[len(mlp_members) :]
    shares = (
        attn_pieces[0][:, 0],
        attn_pieces[1].reshape(shard_rows, 3, local_width),
        mlp_pieces[3].T,
        mlp_pieces[0][:, 0],
        mlp_pieces[1].reshape(shard_rows, 2, hidden),
        mlp_pieces[2].T,
    )
    return (
        block_output,
        input_grad,
        shares[0],
        shares[1],
        shares[2],
        shares[3],
        shares[4],
        shares[5],
    )


def solution(mesh):
    in_specs = (
        P(("fsdp", "context"), None),
        P("fsdp", None),
        P("fsdp"),
        P("fsdp", None, "tensor"),
        P("tensor", "fsdp"),
        P("fsdp"),
        P("fsdp", None, "tensor"),
        P("tensor", "fsdp"),
        P(("fsdp", "context"), None),
    )
    out_specs = (
        P(("fsdp", "context"), None),
        P(("fsdp", "context"), None),
        P("fsdp"),
        P("fsdp", None, "tensor"),
        P("tensor", "fsdp"),
        P("fsdp"),
        P("fsdp", None, "tensor"),
        P("tensor", "fsdp"),
    )
    return jax.shard_map(
        on_device, mesh=mesh, in_specs=in_specs, out_specs=out_specs, check_vma=False
    )
```

```python
import jax
import jax.numpy as jnp
from jax import lax
from jax.sharding import PartitionSpec as P

HD = 64


EPSILON = 1e-05
THETA = 160000.0
MASKED_LOW = -1e30


def layer_norm(values):
    centre = values - jnp.mean(values, axis=-1, keepdims=True)
    spread = lax.rsqrt(jnp.mean(centre * centre, axis=-1, keepdims=True) + EPSILON)
    return (centre * spread, spread)


def norm_back(grad_out, normed, spread, gain):
    scaled = grad_out * gain
    inner = jnp.mean(scaled, axis=-1, keepdims=True) + normed * jnp.mean(
        scaled * normed, axis=-1, keepdims=True
    )
    return spread * (scaled - inner)


def segments_of(row_ids, lengths):
    ends = jnp.cumsum(lengths)
    segment = jnp.sum((row_ids[:, None] >= ends[None, :]).astype(jnp.int32), axis=1)
    starts = ends - lengths
    picked = segment[:, None] == jnp.arange(lengths.shape[0], dtype=jnp.int32)[None, :]
    begin = jnp.sum(jnp.where(picked, starts[None, :], 0), axis=1)
    return (segment, row_ids - begin)


def rope_tables(positions, head_dim):
    half_dim = head_dim // 2
    exponent = jnp.arange(half_dim, dtype=jnp.float32) * (-2.0 / head_dim)
    frequency = jnp.power(jnp.float32(THETA), exponent)
    angles = positions.astype(jnp.float32)[:, None] * frequency[None, :]
    return (jnp.cos(angles)[:, None, :], jnp.sin(angles)[:, None, :])


def rotate(values, cosine, sine_tab):
    half_dim = values.shape[-1] // 2
    lower_half, upper_half = (values[..., :half_dim], values[..., half_dim:])
    return jnp.concatenate(
        [lower_half * cosine - upper_half * sine_tab, upper_half * cosine + lower_half * sine_tab],
        axis=-1,
    )


def rotate_back(grads, cosine, sine_tab):
    half_dim = grads.shape[-1] // 2
    lower_half, upper_half = (grads[..., :half_dim], grads[..., half_dim:])
    return jnp.concatenate(
        [lower_half * cosine + upper_half * sine_tab, upper_half * cosine - lower_half * sine_tab],
        axis=-1,
    )


def gelu_parts(gate_pre):
    normal_cdf = 0.5 * (1.0 + jax.scipy.special.erf(gate_pre * 0.7071067811865476))
    density = jnp.exp(-0.5 * gate_pre * gate_pre) * 0.3989422804014327
    return (gate_pre * normal_cdf, normal_cdf + gate_pre * density)


def pair_sum(values, axis_name):
    if lax.axis_size(axis_name) != 2:
        return lax.psum(values, axis_name)
    other = lax.ppermute(values, axis_name, perm=[(0, 1), (1, 0)])
    return values.astype(jnp.float32) + other.astype(jnp.float32)


def context_gather(values, axis_name):
    count = lax.axis_size(axis_name)
    spread = jnp.broadcast_to(values[None], (count,) + values.shape)
    gathered = lax.all_to_all(spread, axis_name, 0, 0, tiled=True)
    return gathered.reshape((count * values.shape[0],) + values.shape[1:])


def context_scatter_sum(values, axis_name):
    count = lax.axis_size(axis_name)
    rows = values.shape[0] // count
    parts = lax.all_to_all(
        values.reshape((count, rows) + values.shape[1:]), axis_name, 0, 0, tiled=True
    )
    return jnp.sum(parts.astype(jnp.float32), axis=0)


def on_device(
    block_input,
    seq_lengths,
    attn_gain,
    qkv_weight,
    proj_weight,
    mlp_gain,
    gelu_weight,
    down_weight,
    out_cotangent,
):
    row_count = block_input.shape[0]
    feature_count = block_input.shape[1]
    lengths = seq_lengths[0]
    group_rows = row_count * lax.axis_size("context")
    own_first = lax.axis_index("context") * row_count
    own_rows = own_first + jnp.arange(row_count, dtype=jnp.int32)
    own_segment, positions = segments_of(own_rows, lengths)
    inputs_group = context_gather(block_input, "context")
    cosine, sine_tab = rope_tables(positions, HD)
    shard_rows = qkv_weight.shape[0]
    local_width = qkv_weight.shape[2]
    head_count = local_width // HD
    hidden = gelu_weight.shape[2]
    first_pack = lax.all_gather(
        jnp.concatenate(
            [
                qkv_weight.reshape(shard_rows, 3 * local_width),
                attn_gain[:, None],
                mlp_gain[:, None],
            ],
            axis=1,
        ),
        "fsdp",
        axis=0,
        tiled=True,
    )
    second_pack = lax.all_gather(
        jnp.concatenate(
            [proj_weight.T, gelu_weight.reshape(shard_rows, 2 * hidden), down_weight.T], axis=1
        ),
        "fsdp",
        axis=0,
        tiled=True,
    )
    qkv_flat = first_pack[:, : 3 * local_width]
    attn_full = first_pack[:, 3 * local_width]
    mlp_full = first_pack[:, 3 * local_width + 1]
    proj_t = second_pack[:, :local_width]
    gelu_flat = second_pack[:, local_width : local_width + 2 * hidden]
    down_t = second_pack[:, local_width + 2 * hidden :]
    attn_scale = attn_full.astype(jnp.float32)
    mlp_scale = mlp_full.astype(jnp.float32)
    inputs = block_input.astype(jnp.float32)
    normed_attn, spread_attn = layer_norm(inputs)
    hidden_attn = (normed_attn * attn_scale).astype(jnp.bfloat16)
    query_bf = rotate(
        jnp.dot(
            hidden_attn, qkv_flat[:, :local_width], preferred_element_type=jnp.float32
        ).reshape(row_count, head_count, HD),
        cosine,
        sine_tab,
    ).astype(jnp.bfloat16)
    group_normed, unused_spread = layer_norm(inputs_group.astype(jnp.float32))
    hidden_group = (group_normed * attn_scale).astype(jnp.bfloat16)
    group_segment, group_pos = segments_of(jnp.arange(group_rows, dtype=jnp.int32), lengths)
    group_cos, group_sin = rope_tables(group_pos, HD)
    kv_projected = jnp.dot(
        hidden_group, qkv_flat[:, local_width:], preferred_element_type=jnp.float32
    ).reshape(group_rows, 2, head_count, HD)
    keys_heads = rotate(kv_projected[:, 0], group_cos, group_sin).astype(jnp.bfloat16)
    values_heads = kv_projected[:, 1].astype(jnp.bfloat16)
    same_group = (own_segment[:, None] == group_segment[None, :])[None]
    fwd_scores = (
        jnp.einsum("qhd,khd->hqk", query_bf, keys_heads, preferred_element_type=jnp.float32) * 0.125
    )
    row_max = jnp.max(jnp.where(same_group, fwd_scores, MASKED_LOW), axis=2)
    denom_sum = jnp.sum(
        jnp.where(same_group, jnp.exp(fwd_scores - row_max[:, :, None]), 0.0), axis=2
    )
    log_total = row_max + jnp.log(denom_sum)
    fwd_probs = jnp.where(same_group, jnp.exp(fwd_scores - log_total[:, :, None]), 0.0)
    fwd_weights = fwd_probs.astype(jnp.bfloat16)
    mixed = jnp.einsum(
        "hqk,khd->qhd", fwd_weights, values_heads, preferred_element_type=jnp.float32
    ).astype(jnp.bfloat16)
    mixed_flat = mixed.reshape(row_count, local_width)
    attn_part = jnp.dot(mixed_flat, proj_t.T, preferred_element_type=jnp.float32)
    residual = inputs + pair_sum(attn_part.astype(jnp.bfloat16), "tensor")
    normed_mlp, spread_mlp = layer_norm(residual)
    hidden_mlp = (normed_mlp * mlp_scale).astype(jnp.bfloat16)
    gate_up = jnp.dot(hidden_mlp, gelu_flat, preferred_element_type=jnp.float32).reshape(
        row_count, 2, hidden
    )
    gate_pre, up_pre = (gate_up[:, 0], gate_up[:, 1])
    gelu_val, gelu_slope = gelu_parts(gate_pre)
    activ = (gelu_val * up_pre).astype(jnp.bfloat16)
    mlp_part = jnp.dot(activ, down_t.T, preferred_element_type=jnp.float32)
    block_output = (
        residual + pair_sum(mlp_part.astype(jnp.bfloat16), "tensor")
    ).astype(jnp.bfloat16)
    act_grad = jnp.dot(out_cotangent, down_t, preferred_element_type=jnp.float32)
    down_grad_t = jnp.dot(out_cotangent.T, activ, preferred_element_type=jnp.float32)
    gate_up_grad = (
        jnp.stack([act_grad * up_pre * gelu_slope, act_grad * gelu_val], axis=1)
        .astype(jnp.bfloat16)
        .reshape(row_count, 2 * hidden)
    )
    gelu_grad = jnp.dot(hidden_mlp.T, gate_up_grad, preferred_element_type=jnp.float32).reshape(
        feature_count, 2, hidden
    )
    mlp_in_grad = pair_sum(
        jnp.dot(gate_up_grad, gelu_flat.T, preferred_element_type=jnp.float32).astype(
            jnp.bfloat16
        ),
        "tensor",
    )
    mlpgain_grad = jnp.sum(mlp_in_grad * normed_mlp, axis=0)
    resid_grad = out_cotangent.astype(jnp.float32) + norm_back(
        mlp_in_grad, normed_mlp, spread_mlp, mlp_scale
    )
    resid_bf = resid_grad.astype(jnp.bfloat16)
    out_grad = jnp.dot(resid_bf, proj_t, preferred_element_type=jnp.float32).astype(
        jnp.bfloat16
    )
    proj_grad_t = jnp.dot(resid_bf.T, mixed_flat, preferred_element_type=jnp.float32)

    def reduce_pack(packed, members):
        packed = context_gather(
            context_scatter_sum(packed, "context").astype(jnp.bfloat16), "context"
        ).astype(jnp.float32)
        pieces = []
        start = 0
        for member in members:
            pieces.append(packed[:, start : start + member.shape[1]])
            start += member.shape[1]
        return pieces

    mlp_members = [
        mlpgain_grad[:, None],
        gelu_grad.reshape(feature_count, 2 * hidden),
        down_grad_t,
        proj_grad_t,
    ]
    mlp_packed, out_grad = lax.optimization_barrier(
        (jnp.concatenate(mlp_members, axis=1).astype(jnp.bfloat16), out_grad)
    )
    mlp_shard = lax.psum_scatter(mlp_packed, "fsdp", scatter_dimension=0, tiled=True)
    out_heads = out_grad.reshape(row_count, head_count, HD)
    delta = jnp.transpose(
        jnp.sum(out_heads.astype(jnp.float32) * mixed.astype(jnp.float32), axis=2)
    )

    prob_grad = jnp.einsum(
        "qhd,khd->hqk", out_heads, values_heads, preferred_element_type=jnp.float32
    )
    score_grad = (fwd_probs * (prob_grad - delta[:, :, None])).astype(jnp.bfloat16)
    query_grad = (
        jnp.einsum("hqk,khd->qhd", score_grad, keys_heads, preferred_element_type=jnp.float32)
        * 0.125
    )
    key_all = (
        jnp.einsum("hqk,qhd->khd", score_grad, query_bf, preferred_element_type=jnp.float32)
        * 0.125
    ).reshape(group_rows, local_width)
    value_all = jnp.einsum(
        "hqk,qhd->khd", fwd_weights, out_heads, preferred_element_type=jnp.float32
    ).reshape(group_rows, local_width)
    value_partial, mlp_shard = lax.optimization_barrier(
        (value_all.astype(jnp.bfloat16), mlp_shard)
    )
    value_grad = context_scatter_sum(value_partial, "context")
    key_grad = context_scatter_sum(key_all.astype(jnp.bfloat16), "context")
    mlp_pieces = reduce_pack(mlp_shard, mlp_members)
    key_grad = key_grad.reshape(row_count, head_count, HD)
    value_grad = value_grad.reshape(row_count, head_count, HD)
    qkv_rows = (
        jnp.stack(
            [
                rotate_back(query_grad, cosine, sine_tab),
                rotate_back(key_grad, cosine, sine_tab),
                value_grad,
            ],
            axis=1,
        )
        .astype(jnp.bfloat16)
        .reshape(row_count, 3 * local_width)
    )
    qkv_grad = jnp.dot(hidden_attn.T, qkv_rows, preferred_element_type=jnp.float32).reshape(
        feature_count, 3, local_width
    )
    qkv_shard = lax.psum_scatter(
        qkv_grad.reshape(feature_count, 3 * local_width).astype(jnp.bfloat16),
        "fsdp",
        scatter_dimension=0,
        tiled=True,
    )
    attn_in_part, qkv_shard = lax.optimization_barrier(
        (
            jnp.dot(qkv_rows, qkv_flat.T, preferred_element_type=jnp.float32).astype(
                jnp.bfloat16
            ),
            qkv_shard,
        )
    )
    attn_in_grad = pair_sum(attn_in_part, "tensor")
    attngain_grad = jnp.sum(attn_in_grad * normed_attn, axis=0)
    input_grad = resid_grad + norm_back(attn_in_grad, normed_attn, spread_attn, attn_scale)
    attn_members = [attngain_grad[:, None], qkv_grad.reshape(feature_count, 3 * local_width)]
    gain_shard = lax.psum_scatter(
        attn_members[0].astype(jnp.bfloat16), "fsdp", scatter_dimension=0, tiled=True
    )
    attn_pieces = reduce_pack(jnp.concatenate([gain_shard, qkv_shard], axis=1), attn_members)
    shares = (
        attn_pieces[0][:, 0],
        attn_pieces[1].reshape(shard_rows, 3, local_width),
        mlp_pieces[3].T,
        mlp_pieces[0][:, 0],
        mlp_pieces[1].reshape(shard_rows, 2, hidden),
        mlp_pieces[2].T,
    )
    return (
        block_output,
        input_grad,
        shares[0],
        shares[1],
        shares[2],
        shares[3],
        shares[4],
        shares[5],
    )


def solution(mesh):
    in_specs = (
        P(("fsdp", "context"), None),
        P("fsdp", None),
        P("fsdp"),
        P("fsdp", None, "tensor"),
        P("tensor", "fsdp"),
        P("fsdp"),
        P("fsdp", None, "tensor"),
        P("tensor", "fsdp"),
        P(("fsdp", "context"), None),
    )
    out_specs = (
        P(("fsdp", "context"), None),
        P(("fsdp", "context"), None),
        P("fsdp"),
        P("fsdp", None, "tensor"),
        P("tensor", "fsdp"),
        P("fsdp"),
        P("fsdp", None, "tensor"),
        P("tensor", "fsdp"),
    )
    return jax.shard_map(
        on_device, mesh=mesh, in_specs=in_specs, out_specs=out_specs, check_vma=False
    )
```

```python
import jax
import jax.numpy as jnp
from jax import lax
from jax.sharding import PartitionSpec as P

HD = 64


EPSILON = 1e-05
THETA = 160000.0
MASKED_LOW = -1e30


def layer_norm(values):
    centre = values - jnp.mean(values, axis=-1, keepdims=True)
    spread = lax.rsqrt(jnp.mean(centre * centre, axis=-1, keepdims=True) + EPSILON)
    return (centre * spread, spread)


def norm_back(grad_out, normed, spread, gain):
    scaled = grad_out * gain
    inner = jnp.mean(scaled, axis=-1, keepdims=True) + normed * jnp.mean(
        scaled * normed, axis=-1, keepdims=True
    )
    return spread * (scaled - inner)


def segments_of(row_ids, lengths):
    ends = jnp.cumsum(lengths)
    segment = jnp.sum((row_ids[:, None] >= ends[None, :]).astype(jnp.int32), axis=1)
    starts = ends - lengths
    picked = segment[:, None] == jnp.arange(lengths.shape[0], dtype=jnp.int32)[None, :]
    begin = jnp.sum(jnp.where(picked, starts[None, :], 0), axis=1)
    return (segment, row_ids - begin)


def rope_tables(positions, head_dim):
    half_dim = head_dim // 2
    exponent = jnp.arange(half_dim, dtype=jnp.float32) * (-2.0 / head_dim)
    frequency = jnp.power(jnp.float32(THETA), exponent)
    angles = positions.astype(jnp.float32)[:, None] * frequency[None, :]
    return (jnp.cos(angles)[:, None, :], jnp.sin(angles)[:, None, :])


def rotate(values, cosine, sine_tab):
    half_dim = values.shape[-1] // 2
    lower_half, upper_half = (values[..., :half_dim], values[..., half_dim:])
    return jnp.concatenate(
        [lower_half * cosine - upper_half * sine_tab, upper_half * cosine + lower_half * sine_tab],
        axis=-1,
    )


def rotate_back(grads, cosine, sine_tab):
    half_dim = grads.shape[-1] // 2
    lower_half, upper_half = (grads[..., :half_dim], grads[..., half_dim:])
    return jnp.concatenate(
        [lower_half * cosine + upper_half * sine_tab, upper_half * cosine - lower_half * sine_tab],
        axis=-1,
    )


def gelu_parts(gate_pre):
    normal_cdf = 0.5 * (1.0 + jax.scipy.special.erf(gate_pre * 0.7071067811865476))
    density = jnp.exp(-0.5 * gate_pre * gate_pre) * 0.3989422804014327
    return (gate_pre * normal_cdf, normal_cdf + gate_pre * density)


def pair_sum(values, axis_name):
    if lax.axis_size(axis_name) != 2:
        return lax.psum(values, axis_name)
    other = lax.ppermute(values, axis_name, perm=[(0, 1), (1, 0)])
    return values.astype(jnp.float32) + other.astype(jnp.float32)


def context_gather(values, axis_name):
    count = lax.axis_size(axis_name)
    spread = jnp.broadcast_to(values[None], (count,) + values.shape)
    gathered = lax.all_to_all(spread, axis_name, 0, 0, tiled=True)
    return gathered.reshape((count * values.shape[0],) + values.shape[1:])


def context_scatter_sum(values, axis_name):
    count = lax.axis_size(axis_name)
    rows = values.shape[0] // count
    parts = lax.all_to_all(
        values.reshape((count, rows) + values.shape[1:]), axis_name, 0, 0, tiled=True
    )
    return jnp.sum(parts.astype(jnp.float32), axis=0)


def on_device(
    block_input,
    seq_lengths,
    attn_gain,
    qkv_weight,
    proj_weight,
    mlp_gain,
    gelu_weight,
    down_weight,
    out_cotangent,
):
    row_count = block_input.shape[0]
    feature_count = block_input.shape[1]
    lengths = seq_lengths[0]
    group_rows = row_count * lax.axis_size("context")
    own_first = lax.axis_index("context") * row_count
    own_rows = own_first + jnp.arange(row_count, dtype=jnp.int32)
    own_segment, positions = segments_of(own_rows, lengths)
    inputs_group = context_gather(block_input, "context")
    cosine, sine_tab = rope_tables(positions, HD)
    shard_rows = qkv_weight.shape[0]
    local_width = qkv_weight.shape[2]
    head_count = local_width // HD
    hidden = gelu_weight.shape[2]
    first_pack = lax.all_gather(
        jnp.concatenate(
            [
                qkv_weight.reshape(shard_rows, 3 * local_width),
                attn_gain[:, None],
                mlp_gain[:, None],
            ],
            axis=1,
        ),
        "fsdp",
        axis=0,
        tiled=True,
    )
    second_pack = lax.all_gather(
        jnp.concatenate(
            [proj_weight.T, gelu_weight.reshape(shard_rows, 2 * hidden), down_weight.T], axis=1
        ),
        "fsdp",
        axis=0,
        tiled=True,
    )
    qkv_flat = first_pack[:, : 3 * local_width]
    attn_full = first_pack[:, 3 * local_width]
    mlp_full = first_pack[:, 3 * local_width + 1]
    proj_t = second_pack[:, :local_width]
    gelu_flat = second_pack[:, local_width : local_width + 2 * hidden]
    down_t = second_pack[:, local_width + 2 * hidden :]
    attn_scale = attn_full.astype(jnp.float32)
    mlp_scale = mlp_full.astype(jnp.float32)
    inputs = block_input.astype(jnp.float32)
    normed_attn, spread_attn = layer_norm(inputs)
    hidden_attn = (normed_attn * attn_scale).astype(jnp.bfloat16)
    query_bf = rotate(
        jnp.dot(
            hidden_attn, qkv_flat[:, :local_width], preferred_element_type=jnp.float32
        ).reshape(row_count, head_count, HD),
        cosine,
        sine_tab,
    ).astype(jnp.bfloat16)
    group_normed, unused_spread = layer_norm(inputs_group.astype(jnp.float32))
    hidden_group = (group_normed * attn_scale).astype(jnp.bfloat16)
    group_segment, group_pos = segments_of(jnp.arange(group_rows, dtype=jnp.int32), lengths)
    group_cos, group_sin = rope_tables(group_pos, HD)
    kv_projected = jnp.dot(
        hidden_group, qkv_flat[:, local_width:], preferred_element_type=jnp.float32
    ).reshape(group_rows, 2, head_count, HD)
    keys_heads = rotate(kv_projected[:, 0], group_cos, group_sin).astype(jnp.bfloat16)
    values_heads = kv_projected[:, 1].astype(jnp.bfloat16)
    same_group = (own_segment[:, None] == group_segment[None, :])[None]
    fwd_scores = (
        jnp.einsum("qhd,khd->hqk", query_bf, keys_heads, preferred_element_type=jnp.float32) * 0.125
    )
    row_max = jnp.max(jnp.where(same_group, fwd_scores, MASKED_LOW), axis=2)
    denom_sum = jnp.sum(
        jnp.where(same_group, jnp.exp(fwd_scores - row_max[:, :, None]), 0.0), axis=2
    )
    log_total = row_max + jnp.log(denom_sum)
    fwd_probs = jnp.where(same_group, jnp.exp(fwd_scores - log_total[:, :, None]), 0.0)
    fwd_weights = fwd_probs.astype(jnp.bfloat16)
    mixed = jnp.einsum(
        "hqk,khd->qhd", fwd_weights, values_heads, preferred_element_type=jnp.float32
    ).astype(jnp.bfloat16)
    mixed_flat = mixed.reshape(row_count, local_width)
    attn_part = jnp.dot(mixed_flat, proj_t.T, preferred_element_type=jnp.float32)
    residual = inputs + pair_sum(attn_part.astype(jnp.bfloat16), "tensor")
    normed_mlp, spread_mlp = layer_norm(residual)
    hidden_mlp = (normed_mlp * mlp_scale).astype(jnp.bfloat16)
    gate_up = jnp.dot(hidden_mlp, gelu_flat, preferred_element_type=jnp.float32).reshape(
        row_count, 2, hidden
    )
    gate_pre, up_pre = (gate_up[:, 0], gate_up[:, 1])
    gelu_val, gelu_slope = gelu_parts(gate_pre)
    activ = (gelu_val * up_pre).astype(jnp.bfloat16)
    mlp_part = jnp.dot(activ, down_t.T, preferred_element_type=jnp.float32)
    block_output = (
        residual + pair_sum(mlp_part.astype(jnp.bfloat16), "tensor")
    ).astype(jnp.bfloat16)
    act_grad = jnp.dot(out_cotangent, down_t, preferred_element_type=jnp.float32)
    down_grad_t = jnp.dot(out_cotangent.T, activ, preferred_element_type=jnp.float32)
    gate_up_grad = (
        jnp.stack([act_grad * up_pre * gelu_slope, act_grad * gelu_val], axis=1)
        .astype(jnp.bfloat16)
        .reshape(row_count, 2 * hidden)
    )
    gelu_grad = jnp.dot(hidden_mlp.T, gate_up_grad, preferred_element_type=jnp.float32).reshape(
        feature_count, 2, hidden
    )
    mlp_in_grad = pair_sum(
        jnp.dot(gate_up_grad, gelu_flat.T, preferred_element_type=jnp.float32).astype(
            jnp.bfloat16
        ),
        "tensor",
    )
    mlpgain_grad = jnp.sum(mlp_in_grad * normed_mlp, axis=0)
    resid_grad = out_cotangent.astype(jnp.float32) + norm_back(
        mlp_in_grad, normed_mlp, spread_mlp, mlp_scale
    )
    resid_bf = resid_grad.astype(jnp.bfloat16)
    out_grad = jnp.dot(resid_bf, proj_t, preferred_element_type=jnp.float32).astype(
        jnp.bfloat16
    )
    proj_grad_t = jnp.dot(resid_bf.T, mixed_flat, preferred_element_type=jnp.float32)

    def reduce_pack(packed, members):
        packed = context_gather(
            context_scatter_sum(packed, "context").astype(jnp.bfloat16), "context"
        ).astype(jnp.float32)
        pieces = []
        start = 0
        for member in members:
            pieces.append(packed[:, start : start + member.shape[1]])
            start += member.shape[1]
        return pieces

    mlp_members = [
        gelu_grad.reshape(feature_count, 2 * hidden),
        proj_grad_t,
        down_grad_t,
        mlpgain_grad[:, None],
    ]
    mlp_packed, out_grad = lax.optimization_barrier(
        (jnp.concatenate(mlp_members, axis=1).astype(jnp.bfloat16), out_grad)
    )
    mlp_shard = lax.psum_scatter(mlp_packed, "fsdp", scatter_dimension=0, tiled=True)
    out_heads = out_grad.reshape(row_count, head_count, HD)
    delta = jnp.transpose(
        jnp.sum(out_heads.astype(jnp.float32) * mixed.astype(jnp.float32), axis=2)
    )

    prob_grad = jnp.einsum(
        "qhd,khd->hqk", out_heads, values_heads, preferred_element_type=jnp.float32
    )
    score_grad = (fwd_probs * (prob_grad - delta[:, :, None])).astype(jnp.bfloat16)
    query_grad = (
        jnp.einsum("hqk,khd->qhd", score_grad, keys_heads, preferred_element_type=jnp.float32)
        * 0.125
    )
    key_all = (
        jnp.einsum("hqk,qhd->khd", score_grad, query_bf, preferred_element_type=jnp.float32)
        * 0.125
    ).reshape(group_rows, local_width)
    value_all = jnp.einsum(
        "hqk,qhd->khd", fwd_weights, out_heads, preferred_element_type=jnp.float32
    ).reshape(group_rows, local_width)
    value_partial, mlp_shard = lax.optimization_barrier(
        (value_all.astype(jnp.bfloat16), mlp_shard)
    )
    value_grad = context_scatter_sum(value_partial, "context")
    key_grad = context_scatter_sum(key_all.astype(jnp.bfloat16), "context")
    mlp_pieces = reduce_pack(mlp_shard, mlp_members)
    key_grad = key_grad.reshape(row_count, head_count, HD)
    value_grad = value_grad.reshape(row_count, head_count, HD)
    qkv_rows = (
        jnp.stack(
            [
                rotate_back(query_grad, cosine, sine_tab),
                rotate_back(key_grad, cosine, sine_tab),
                value_grad,
            ],
            axis=1,
        )
        .astype(jnp.bfloat16)
        .reshape(row_count, 3 * local_width)
    )
    qkv_grad = jnp.dot(hidden_attn.T, qkv_rows, preferred_element_type=jnp.float32).reshape(
        feature_count, 3, local_width
    )
    attn_in_grad = pair_sum(
        jnp.dot(qkv_rows, qkv_flat.T, preferred_element_type=jnp.float32).astype(jnp.bfloat16),
        "tensor",
    )
    attngain_grad = jnp.sum(attn_in_grad * normed_attn, axis=0)
    input_grad = resid_grad + norm_back(attn_in_grad, normed_attn, spread_attn, attn_scale)
    attn_members = [qkv_grad.reshape(feature_count, 3 * local_width), attngain_grad[:, None]]
    attn_pieces = reduce_pack(
        lax.psum_scatter(
            jnp.concatenate(attn_members, axis=1).astype(jnp.bfloat16),
            "fsdp",
            scatter_dimension=0,
            tiled=True,
        ),
        attn_members,
    )
    shares = (
        attn_pieces[1][:, 0],
        attn_pieces[0].reshape(shard_rows, 3, local_width),
        mlp_pieces[1].T,
        mlp_pieces[3][:, 0],
        mlp_pieces[0].reshape(shard_rows, 2, hidden),
        mlp_pieces[2].T,
    )
    return (
        block_output,
        input_grad,
        shares[0],
        shares[1],
        shares[2],
        shares[3],
        shares[4],
        shares[5],
    )


def solution(mesh):
    in_specs = (
        P(("fsdp", "context"), None),
        P("fsdp", None),
        P("fsdp"),
        P("fsdp", None, "tensor"),
        P("tensor", "fsdp"),
        P("fsdp"),
        P("fsdp", None, "tensor"),
        P("tensor", "fsdp"),
        P(("fsdp", "context"), None),
    )
    out_specs = (
        P(("fsdp", "context"), None),
        P(("fsdp", "context"), None),
        P("fsdp"),
        P("fsdp", None, "tensor"),
        P("tensor", "fsdp"),
        P("fsdp"),
        P("fsdp", None, "tensor"),
        P("tensor", "fsdp"),
    )
    return jax.shard_map(
        on_device, mesh=mesh, in_specs=in_specs, out_specs=out_specs, check_vma=False
    )
```

```python
import jax
import jax.numpy as jnp
from jax import lax
from jax.sharding import PartitionSpec as P

HD = 64


EPSILON = 1e-05
THETA = 160000.0
MASKED_LOW = -1e30


def layer_norm(values):
    centre = values - jnp.mean(values, axis=-1, keepdims=True)
    spread = lax.rsqrt(jnp.mean(centre * centre, axis=-1, keepdims=True) + EPSILON)
    return (centre * spread, spread)


def norm_back(grad_out, normed, spread, gain):
    scaled = grad_out * gain
    inner = jnp.mean(scaled, axis=-1, keepdims=True) + normed * jnp.mean(
        scaled * normed, axis=-1, keepdims=True
    )
    return spread * (scaled - inner)


def segments_of(row_ids, lengths):
    ends = jnp.cumsum(lengths)
    segment = jnp.sum((row_ids[:, None] >= ends[None, :]).astype(jnp.int32), axis=1)
    starts = ends - lengths
    picked = segment[:, None] == jnp.arange(lengths.shape[0], dtype=jnp.int32)[None, :]
    begin = jnp.sum(jnp.where(picked, starts[None, :], 0), axis=1)
    return (segment, row_ids - begin)


def rope_tables(positions, head_dim):
    half_dim = head_dim // 2
    exponent = jnp.arange(half_dim, dtype=jnp.float32) * (-2.0 / head_dim)
    frequency = jnp.power(jnp.float32(THETA), exponent)
    angles = positions.astype(jnp.float32)[:, None] * frequency[None, :]
    return (jnp.cos(angles)[:, None, :], jnp.sin(angles)[:, None, :])


def rotate(values, cosine, sine_tab):
    half_dim = values.shape[-1] // 2
    lower_half, upper_half = (values[..., :half_dim], values[..., half_dim:])
    return jnp.concatenate(
        [lower_half * cosine - upper_half * sine_tab, upper_half * cosine + lower_half * sine_tab],
        axis=-1,
    )


def rotate_back(grads, cosine, sine_tab):
    half_dim = grads.shape[-1] // 2
    lower_half, upper_half = (grads[..., :half_dim], grads[..., half_dim:])
    return jnp.concatenate(
        [lower_half * cosine + upper_half * sine_tab, upper_half * cosine - lower_half * sine_tab],
        axis=-1,
    )


def gelu_parts(gate_pre):
    normal_cdf = 0.5 * (1.0 + jax.scipy.special.erf(gate_pre * 0.7071067811865476))
    density = jnp.exp(-0.5 * gate_pre * gate_pre) * 0.3989422804014327
    return (gate_pre * normal_cdf, normal_cdf + gate_pre * density)


def pair_sum(values, axis_name):
    if lax.axis_size(axis_name) != 2:
        return lax.psum(values, axis_name)
    other = lax.ppermute(values, axis_name, perm=[(0, 1), (1, 0)])
    return values.astype(jnp.float32) + other.astype(jnp.float32)


def context_gather(values, axis_name):
    count = lax.axis_size(axis_name)
    spread = jnp.broadcast_to(values[None], (count,) + values.shape)
    gathered = lax.all_to_all(spread, axis_name, 0, 0, tiled=True)
    return gathered.reshape((count * values.shape[0],) + values.shape[1:])


def context_scatter_sum(values, axis_name):
    count = lax.axis_size(axis_name)
    rows = values.shape[0] // count
    parts = lax.all_to_all(
        values.reshape((count, rows) + values.shape[1:]), axis_name, 0, 0, tiled=True
    )
    return jnp.sum(parts.astype(jnp.float32), axis=0)


def on_device(
    block_input,
    seq_lengths,
    attn_gain,
    qkv_weight,
    proj_weight,
    mlp_gain,
    gelu_weight,
    down_weight,
    out_cotangent,
):
    row_count = block_input.shape[0]
    feature_count = block_input.shape[1]
    lengths = seq_lengths[0]
    group_rows = row_count * lax.axis_size("context")
    own_first = lax.axis_index("context") * row_count
    own_rows = own_first + jnp.arange(row_count, dtype=jnp.int32)
    own_segment, positions = segments_of(own_rows, lengths)
    inputs_group = context_gather(block_input, "context")
    cosine, sine_tab = rope_tables(positions, HD)
    shard_rows = qkv_weight.shape[0]
    local_width = qkv_weight.shape[2]
    head_count = local_width // HD
    hidden = gelu_weight.shape[2]
    first_pack = lax.all_gather(
        jnp.concatenate(
            [
                qkv_weight.reshape(shard_rows, 3 * local_width),
                attn_gain[:, None],
                mlp_gain[:, None],
            ],
            axis=1,
        ),
        "fsdp",
        axis=0,
        tiled=True,
    )
    second_pack = lax.all_gather(
        jnp.concatenate(
            [proj_weight.T, gelu_weight.reshape(shard_rows, 2 * hidden), down_weight.T], axis=1
        ),
        "fsdp",
        axis=0,
        tiled=True,
    )
    qkv_flat = first_pack[:, : 3 * local_width]
    attn_full = first_pack[:, 3 * local_width]
    mlp_full = first_pack[:, 3 * local_width + 1]
    proj_t = second_pack[:, :local_width]
    gelu_flat = second_pack[:, local_width : local_width + 2 * hidden]
    down_t = second_pack[:, local_width + 2 * hidden :]
    attn_scale = attn_full.astype(jnp.float32)
    mlp_scale = mlp_full.astype(jnp.float32)
    inputs = block_input.astype(jnp.float32)
    normed_attn, spread_attn = layer_norm(inputs)
    hidden_attn = (normed_attn * attn_scale).astype(jnp.bfloat16)
    group_normed, unused_spread = layer_norm(inputs_group.astype(jnp.float32))
    hidden_group = (group_normed * attn_scale).astype(jnp.bfloat16)
    group_segment, group_pos = segments_of(jnp.arange(group_rows, dtype=jnp.int32), lengths)
    group_cos, group_sin = rope_tables(group_pos, HD)
    group_projected = jnp.dot(
        hidden_group, qkv_flat, preferred_element_type=jnp.float32
    ).reshape(group_rows, 3, head_count, HD)
    query_bf = rotate(
        lax.dynamic_slice_in_dim(group_projected[:, 0], own_first, row_count, 0),
        cosine,
        sine_tab,
    ).astype(jnp.bfloat16)
    keys_heads = rotate(group_projected[:, 1], group_cos, group_sin).astype(jnp.bfloat16)
    values_heads = group_projected[:, 2].astype(jnp.bfloat16)
    same_group = (own_segment[:, None] == group_segment[None, :])[None]
    fwd_scores = (
        jnp.einsum("qhd,khd->hqk", query_bf, keys_heads, preferred_element_type=jnp.float32) * 0.125
    )
    row_max = jnp.max(jnp.where(same_group, fwd_scores, MASKED_LOW), axis=2)
    denom_sum = jnp.sum(
        jnp.where(same_group, jnp.exp(fwd_scores - row_max[:, :, None]), 0.0), axis=2
    )
    log_total = row_max + jnp.log(denom_sum)
    fwd_probs = jnp.where(same_group, jnp.exp(fwd_scores - log_total[:, :, None]), 0.0)
    fwd_weights = fwd_probs.astype(jnp.bfloat16)
    mixed = jnp.einsum(
        "hqk,khd->qhd", fwd_weights, values_heads, preferred_element_type=jnp.float32
    ).astype(jnp.bfloat16)
    mixed_flat = mixed.reshape(row_count, local_width)
    attn_part = jnp.dot(mixed_flat, proj_t.T, preferred_element_type=jnp.float32)
    residual = inputs + pair_sum(attn_part.astype(jnp.bfloat16), "tensor")
    normed_mlp, spread_mlp = layer_norm(residual)
    hidden_mlp = (normed_mlp * mlp_scale).astype(jnp.bfloat16)
    gate_up = jnp.dot(hidden_mlp, gelu_flat, preferred_element_type=jnp.float32).reshape(
        row_count, 2, hidden
    )
    gate_pre, up_pre = (gate_up[:, 0], gate_up[:, 1])
    gelu_val, gelu_slope = gelu_parts(gate_pre)
    activ = (gelu_val * up_pre).astype(jnp.bfloat16)
    mlp_part = jnp.dot(activ, down_t.T, preferred_element_type=jnp.float32)
    block_output = (
        residual + pair_sum(mlp_part.astype(jnp.bfloat16), "tensor")
    ).astype(jnp.bfloat16)
    act_grad = jnp.dot(out_cotangent, down_t, preferred_element_type=jnp.float32)
    down_grad_t = jnp.dot(out_cotangent.T, activ, preferred_element_type=jnp.float32)
    gate_up_grad = (
        jnp.stack([act_grad * up_pre * gelu_slope, act_grad * gelu_val], axis=1)
        .astype(jnp.bfloat16)
        .reshape(row_count, 2 * hidden)
    )
    gelu_grad = jnp.dot(hidden_mlp.T, gate_up_grad, preferred_element_type=jnp.float32).reshape(
        feature_count, 2, hidden
    )
    mlp_in_grad = pair_sum(
        jnp.dot(gate_up_grad, gelu_flat.T, preferred_element_type=jnp.float32).astype(
            jnp.bfloat16
        ),
        "tensor",
    )
    mlpgain_grad = jnp.sum(mlp_in_grad * normed_mlp, axis=0)
    resid_grad = out_cotangent.astype(jnp.float32) + norm_back(
        mlp_in_grad, normed_mlp, spread_mlp, mlp_scale
    )
    resid_bf = resid_grad.astype(jnp.bfloat16)
    out_grad = jnp.dot(resid_bf, proj_t, preferred_element_type=jnp.float32).astype(
        jnp.bfloat16
    )
    proj_grad_t = jnp.dot(resid_bf.T, mixed_flat, preferred_element_type=jnp.float32)

    def reduce_pack(packed, members):
        packed = context_gather(
            context_scatter_sum(packed, "context").astype(jnp.bfloat16), "context"
        ).astype(jnp.float32)
        pieces = []
        start = 0
        for member in members:
            pieces.append(packed[:, start : start + member.shape[1]])
            start += member.shape[1]
        return pieces

    mlp_members = [
        gelu_grad.reshape(feature_count, 2 * hidden),
        proj_grad_t,
        down_grad_t,
        mlpgain_grad[:, None],
    ]
    mlp_packed, out_grad = lax.optimization_barrier(
        (jnp.concatenate(mlp_members, axis=1).astype(jnp.bfloat16), out_grad)
    )
    mlp_shard = lax.psum_scatter(mlp_packed, "fsdp", scatter_dimension=0, tiled=True)
    out_heads = out_grad.reshape(row_count, head_count, HD)
    delta = jnp.transpose(
        jnp.sum(out_heads.astype(jnp.float32) * mixed.astype(jnp.float32), axis=2)
    )

    prob_grad = jnp.einsum(
        "qhd,khd->hqk", out_heads, values_heads, preferred_element_type=jnp.float32
    )
    score_grad = (fwd_probs * (prob_grad - delta[:, :, None])).astype(jnp.bfloat16)
    query_grad = (
        jnp.einsum("hqk,khd->qhd", score_grad, keys_heads, preferred_element_type=jnp.float32)
        * 0.125
    )
    key_all = (
        jnp.einsum("hqk,qhd->khd", score_grad, query_bf, preferred_element_type=jnp.float32)
        * 0.125
    ).reshape(group_rows, local_width)
    value_all = jnp.einsum(
        "hqk,qhd->khd", fwd_weights, out_heads, preferred_element_type=jnp.float32
    ).reshape(group_rows, local_width)
    value_partial, mlp_shard = lax.optimization_barrier(
        (value_all.astype(jnp.bfloat16), mlp_shard)
    )
    value_grad = context_scatter_sum(value_partial, "context")
    key_grad = context_scatter_sum(key_all.astype(jnp.bfloat16), "context")
    mlp_pieces = reduce_pack(mlp_shard, mlp_members)
    key_grad = key_grad.reshape(row_count, head_count, HD)
    value_grad = value_grad.reshape(row_count, head_count, HD)
    qkv_rows = (
        jnp.stack(
            [
                rotate_back(query_grad, cosine, sine_tab),
                rotate_back(key_grad, cosine, sine_tab),
                value_grad,
            ],
            axis=1,
        )
        .astype(jnp.bfloat16)
        .reshape(row_count, 3 * local_width)
    )
    qkv_grad = jnp.dot(hidden_attn.T, qkv_rows, preferred_element_type=jnp.float32).reshape(
        feature_count, 3, local_width
    )
    attn_in_grad = pair_sum(
        jnp.dot(qkv_rows, qkv_flat.T, preferred_element_type=jnp.float32).astype(jnp.bfloat16),
        "tensor",
    )
    attngain_grad = jnp.sum(attn_in_grad * normed_attn, axis=0)
    input_grad = resid_grad + norm_back(attn_in_grad, normed_attn, spread_attn, attn_scale)
    attn_members = [qkv_grad.reshape(feature_count, 3 * local_width), attngain_grad[:, None]]
    attn_pieces = reduce_pack(
        lax.psum_scatter(
            jnp.concatenate(attn_members, axis=1).astype(jnp.bfloat16),
            "fsdp",
            scatter_dimension=0,
            tiled=True,
        ),
        attn_members,
    )
    shares = (
        attn_pieces[1][:, 0],
        attn_pieces[0].reshape(shard_rows, 3, local_width),
        mlp_pieces[1].T,
        mlp_pieces[3][:, 0],
        mlp_pieces[0].reshape(shard_rows, 2, hidden),
        mlp_pieces[2].T,
    )
    return (
        block_output,
        input_grad,
        shares[0],
        shares[1],
        shares[2],
        shares[3],
        shares[4],
        shares[5],
    )


def solution(mesh):
    in_specs = (
        P(("fsdp", "context"), None),
        P("fsdp", None),
        P("fsdp"),
        P("fsdp", None, "tensor"),
        P("tensor", "fsdp"),
        P("fsdp"),
        P("fsdp", None, "tensor"),
        P("tensor", "fsdp"),
        P(("fsdp", "context"), None),
    )
    out_specs = (
        P(("fsdp", "context"), None),
        P(("fsdp", "context"), None),
        P("fsdp"),
        P("fsdp", None, "tensor"),
        P("tensor", "fsdp"),
        P("fsdp"),
        P("fsdp", None, "tensor"),
        P("tensor", "fsdp"),
    )
    return jax.shard_map(
        on_device, mesh=mesh, in_specs=in_specs, out_specs=out_specs, check_vma=False
    )
```

```python
import jax
import jax.numpy as jnp
from jax import lax
from jax.sharding import PartitionSpec as P

HD = 64


EPSILON = 1e-05
THETA = 160000.0
MASKED_LOW = -1e30


def layer_norm(values):
    centre = values - jnp.mean(values, axis=-1, keepdims=True)
    spread = lax.rsqrt(jnp.mean(centre * centre, axis=-1, keepdims=True) + EPSILON)
    return (centre * spread, spread)


def norm_back(grad_out, normed, spread, gain):
    scaled = grad_out * gain
    inner = jnp.mean(scaled, axis=-1, keepdims=True) + normed * jnp.mean(
        scaled * normed, axis=-1, keepdims=True
    )
    return spread * (scaled - inner)


def segments_of(row_ids, lengths):
    ends = jnp.cumsum(lengths)
    segment = jnp.sum((row_ids[:, None] >= ends[None, :]).astype(jnp.int32), axis=1)
    starts = ends - lengths
    picked = segment[:, None] == jnp.arange(lengths.shape[0], dtype=jnp.int32)[None, :]
    begin = jnp.sum(jnp.where(picked, starts[None, :], 0), axis=1)
    return (segment, row_ids - begin)


def rope_tables(positions, head_dim):
    half_dim = head_dim // 2
    exponent = jnp.arange(half_dim, dtype=jnp.float32) * (-2.0 / head_dim)
    frequency = jnp.power(jnp.float32(THETA), exponent)
    angles = positions.astype(jnp.float32)[:, None] * frequency[None, :]
    return (jnp.cos(angles)[:, None, :], jnp.sin(angles)[:, None, :])


def rotate(values, cosine, sine_tab):
    half_dim = values.shape[-1] // 2
    lower_half, upper_half = (values[..., :half_dim], values[..., half_dim:])
    return jnp.concatenate(
        [lower_half * cosine - upper_half * sine_tab, upper_half * cosine + lower_half * sine_tab],
        axis=-1,
    )


def rotate_back(grads, cosine, sine_tab):
    half_dim = grads.shape[-1] // 2
    lower_half, upper_half = (grads[..., :half_dim], grads[..., half_dim:])
    return jnp.concatenate(
        [lower_half * cosine + upper_half * sine_tab, upper_half * cosine - lower_half * sine_tab],
        axis=-1,
    )


def gelu_parts(gate_pre):
    normal_cdf = 0.5 * (1.0 + jax.scipy.special.erf(gate_pre * 0.7071067811865476))
    density = jnp.exp(-0.5 * gate_pre * gate_pre) * 0.3989422804014327
    return (gate_pre * normal_cdf, normal_cdf + gate_pre * density)


def pair_sum(values, axis_name):
    if lax.axis_size(axis_name) != 2:
        return lax.psum(values, axis_name)
    other = lax.ppermute(values, axis_name, perm=[(0, 1), (1, 0)])
    return values.astype(jnp.float32) + other.astype(jnp.float32)


def context_gather(values, axis_name):
    count = lax.axis_size(axis_name)
    spread = jnp.broadcast_to(values[None], (count,) + values.shape)
    gathered = lax.all_to_all(spread, axis_name, 0, 0, tiled=True)
    return gathered.reshape((count * values.shape[0],) + values.shape[1:])


def context_scatter_sum(values, axis_name):
    count = lax.axis_size(axis_name)
    rows = values.shape[0] // count
    parts = lax.all_to_all(
        values.reshape((count, rows) + values.shape[1:]), axis_name, 0, 0, tiled=True
    )
    return jnp.sum(parts.astype(jnp.float32), axis=0)


def on_device(
    block_input,
    seq_lengths,
    attn_gain,
    qkv_weight,
    proj_weight,
    mlp_gain,
    gelu_weight,
    down_weight,
    out_cotangent,
):
    row_count = block_input.shape[0]
    feature_count = block_input.shape[1]
    lengths = seq_lengths[0]
    group_rows = row_count * lax.axis_size("context")
    own_first = lax.axis_index("context") * row_count
    own_rows = own_first + jnp.arange(row_count, dtype=jnp.int32)
    own_segment, positions = segments_of(own_rows, lengths)
    inputs_group = context_gather(block_input, "context")
    cosine, sine_tab = rope_tables(positions, HD)
    shard_rows = qkv_weight.shape[0]
    local_width = qkv_weight.shape[2]
    head_count = local_width // HD
    hidden = gelu_weight.shape[2]
    first_pack = lax.all_gather(
        jnp.concatenate(
            [
                qkv_weight.reshape(shard_rows, 3 * local_width),
                attn_gain[:, None],
                mlp_gain[:, None],
            ],
            axis=1,
        ),
        "fsdp",
        axis=0,
        tiled=True,
    )
    second_pack = lax.all_gather(
        jnp.concatenate(
            [proj_weight.T, gelu_weight.reshape(shard_rows, 2 * hidden), down_weight.T], axis=1
        ),
        "fsdp",
        axis=0,
        tiled=True,
    )
    qkv_flat = first_pack[:, : 3 * local_width]
    attn_full = first_pack[:, 3 * local_width]
    mlp_full = first_pack[:, 3 * local_width + 1]
    proj_t = second_pack[:, :local_width]
    gelu_flat = second_pack[:, local_width : local_width + 2 * hidden]
    down_t = second_pack[:, local_width + 2 * hidden :]
    attn_scale = attn_full.astype(jnp.float32)
    mlp_scale = mlp_full.astype(jnp.float32)
    inputs = block_input.astype(jnp.float32)
    normed_attn, spread_attn = layer_norm(inputs)
    hidden_attn = (normed_attn * attn_scale).astype(jnp.bfloat16)
    query_bf = rotate(
        jnp.dot(
            hidden_attn, qkv_flat[:, :local_width], preferred_element_type=jnp.float32
        ).reshape(row_count, head_count, HD),
        cosine,
        sine_tab,
    ).astype(jnp.bfloat16)
    group_normed, unused_spread = layer_norm(inputs_group.astype(jnp.float32))
    hidden_group = (group_normed * attn_scale).astype(jnp.bfloat16)
    group_segment, group_pos = segments_of(jnp.arange(group_rows, dtype=jnp.int32), lengths)
    group_cos, group_sin = rope_tables(group_pos, HD)
    kv_projected = jnp.dot(
        hidden_group, qkv_flat[:, local_width:], preferred_element_type=jnp.float32
    ).reshape(group_rows, 2, head_count, HD)
    keys_heads = rotate(kv_projected[:, 0], group_cos, group_sin).astype(jnp.bfloat16)
    values_heads = kv_projected[:, 1].astype(jnp.bfloat16)
    same_group = (own_segment[:, None] == group_segment[None, :])[None]
    fwd_scores = (
        jnp.einsum("qhd,khd->hqk", query_bf, keys_heads, preferred_element_type=jnp.float32) * 0.125
    )
    row_max = jnp.max(jnp.where(same_group, fwd_scores, MASKED_LOW), axis=2)
    denom_sum = jnp.sum(
        jnp.where(same_group, jnp.exp(fwd_scores - row_max[:, :, None]), 0.0), axis=2
    )
    log_total = row_max + jnp.log(denom_sum)
    fwd_probs = jnp.where(same_group, jnp.exp(fwd_scores - log_total[:, :, None]), 0.0)
    fwd_weights = fwd_probs.astype(jnp.bfloat16)
    mixed = jnp.einsum(
        "hqk,khd->qhd", fwd_weights, values_heads, preferred_element_type=jnp.float32
    ).astype(jnp.bfloat16)
    mixed_flat = mixed.reshape(row_count, local_width)
    attn_part = jnp.dot(mixed_flat, proj_t.T, preferred_element_type=jnp.float32)
    residual = inputs + pair_sum(attn_part.astype(jnp.bfloat16), "tensor")
    normed_mlp, spread_mlp = layer_norm(residual)
    hidden_mlp = (normed_mlp * mlp_scale).astype(jnp.bfloat16)
    gate_up = jnp.dot(hidden_mlp, gelu_flat, preferred_element_type=jnp.float32).reshape(
        row_count, 2, hidden
    )
    gate_pre, up_pre = (gate_up[:, 0], gate_up[:, 1])
    gelu_val, gelu_slope = gelu_parts(gate_pre)
    activ = (gelu_val * up_pre).astype(jnp.bfloat16)
    mlp_part = jnp.dot(activ, down_t.T, preferred_element_type=jnp.float32)
    block_output = (
        residual + pair_sum(mlp_part.astype(jnp.bfloat16), "tensor")
    ).astype(jnp.bfloat16)
    act_grad = jnp.dot(out_cotangent, down_t, preferred_element_type=jnp.float32)
    down_grad_t = jnp.dot(out_cotangent.T, activ, preferred_element_type=jnp.bfloat16)
    gate_up_grad = (
        jnp.stack([act_grad * up_pre * gelu_slope, act_grad * gelu_val], axis=1)
        .astype(jnp.bfloat16)
        .reshape(row_count, 2 * hidden)
    )
    gelu_grad = jnp.dot(hidden_mlp.T, gate_up_grad, preferred_element_type=jnp.bfloat16).reshape(
        feature_count, 2, hidden
    )
    mlp_in_grad = pair_sum(
        jnp.dot(gate_up_grad, gelu_flat.T, preferred_element_type=jnp.float32).astype(
            jnp.bfloat16
        ),
        "tensor",
    )
    mlpgain_grad = jnp.sum(mlp_in_grad * normed_mlp, axis=0)
    resid_grad = out_cotangent.astype(jnp.float32) + norm_back(
        mlp_in_grad, normed_mlp, spread_mlp, mlp_scale
    )
    resid_bf = resid_grad.astype(jnp.bfloat16)
    out_grad = jnp.dot(resid_bf, proj_t, preferred_element_type=jnp.float32).astype(
        jnp.bfloat16
    )
    proj_grad_t = jnp.dot(resid_bf.T, mixed_flat, preferred_element_type=jnp.bfloat16)

    def reduce_pack(packed, members):
        packed = context_gather(
            context_scatter_sum(packed, "context").astype(jnp.bfloat16), "context"
        ).astype(jnp.float32)
        pieces = []
        start = 0
        for member in members:
            pieces.append(packed[:, start : start + member.shape[1]])
            start += member.shape[1]
        return pieces

    mlp_members = [
        gelu_grad.reshape(feature_count, 2 * hidden),
        proj_grad_t,
        down_grad_t,
        mlpgain_grad[:, None],
    ]
    mlp_packed, out_grad = lax.optimization_barrier(
        (jnp.concatenate(mlp_members, axis=1).astype(jnp.bfloat16), out_grad)
    )
    mlp_shard = lax.psum_scatter(mlp_packed, "fsdp", scatter_dimension=0, tiled=True)
    out_heads = out_grad.reshape(row_count, head_count, HD)
    delta = jnp.transpose(
        jnp.sum(out_heads.astype(jnp.float32) * mixed.astype(jnp.float32), axis=2)
    )

    prob_grad = jnp.einsum(
        "qhd,khd->hqk", out_heads, values_heads, preferred_element_type=jnp.float32
    )
    score_grad = (fwd_probs * (prob_grad - delta[:, :, None])).astype(jnp.bfloat16)
    query_grad = (
        jnp.einsum("hqk,khd->qhd", score_grad, keys_heads, preferred_element_type=jnp.float32)
        * 0.125
    )
    key_all = (
        jnp.einsum("hqk,qhd->khd", score_grad, query_bf, preferred_element_type=jnp.float32)
        * 0.125
    ).reshape(group_rows, local_width)
    value_all = jnp.einsum(
        "hqk,qhd->khd", fwd_weights, out_heads, preferred_element_type=jnp.float32
    ).reshape(group_rows, local_width)
    value_partial, mlp_shard = lax.optimization_barrier(
        (value_all.astype(jnp.bfloat16), mlp_shard)
    )
    value_grad = context_scatter_sum(value_partial, "context")
    key_grad = context_scatter_sum(key_all.astype(jnp.bfloat16), "context")
    mlp_pieces = reduce_pack(mlp_shard, mlp_members)
    key_grad = key_grad.reshape(row_count, head_count, HD)
    value_grad = value_grad.reshape(row_count, head_count, HD)
    qkv_rows = (
        jnp.stack(
            [
                rotate_back(query_grad, cosine, sine_tab),
                rotate_back(key_grad, cosine, sine_tab),
                value_grad,
            ],
            axis=1,
        )
        .astype(jnp.bfloat16)
        .reshape(row_count, 3 * local_width)
    )
    qkv_grad = jnp.dot(hidden_attn.T, qkv_rows, preferred_element_type=jnp.bfloat16).reshape(
        feature_count, 3, local_width
    )
    attn_in_grad = pair_sum(
        jnp.dot(qkv_rows, qkv_flat.T, preferred_element_type=jnp.float32).astype(jnp.bfloat16),
        "tensor",
    )
    attngain_grad = jnp.sum(attn_in_grad * normed_attn, axis=0)
    input_grad = resid_grad + norm_back(attn_in_grad, normed_attn, spread_attn, attn_scale)
    attn_members = [qkv_grad.reshape(feature_count, 3 * local_width), attngain_grad[:, None]]
    attn_pieces = reduce_pack(
        lax.psum_scatter(
            jnp.concatenate(attn_members, axis=1).astype(jnp.bfloat16),
            "fsdp",
            scatter_dimension=0,
            tiled=True,
        ),
        attn_members,
    )
    shares = (
        attn_pieces[1][:, 0],
        attn_pieces[0].reshape(shard_rows, 3, local_width),
        mlp_pieces[1].T,
        mlp_pieces[3][:, 0],
        mlp_pieces[0].reshape(shard_rows, 2, hidden),
        mlp_pieces[2].T,
    )
    return (
        block_output,
        input_grad,
        shares[0],
        shares[1],
        shares[2],
        shares[3],
        shares[4],
        shares[5],
    )


def solution(mesh):
    in_specs = (
        P(("fsdp", "context"), None),
        P("fsdp", None),
        P("fsdp"),
        P("fsdp", None, "tensor"),
        P("tensor", "fsdp"),
        P("fsdp"),
        P("fsdp", None, "tensor"),
        P("tensor", "fsdp"),
        P(("fsdp", "context"), None),
    )
    out_specs = (
        P(("fsdp", "context"), None),
        P(("fsdp", "context"), None),
        P("fsdp"),
        P("fsdp", None, "tensor"),
        P("tensor", "fsdp"),
        P("fsdp"),
        P("fsdp", None, "tensor"),
        P("tensor", "fsdp"),
    )
    return jax.shard_map(
        on_device, mesh=mesh, in_specs=in_specs, out_specs=out_specs, check_vma=False
    )
```
